512 devices in a mesh: energy: 32 (over z, x), slab: 16 (over y, core).
Axes of the slice: x: 4, y: 8, z: 8, core: 2. Of those that a mesh axis runs over, the one named last changes fastest.
Arguments:
- onsite: float32 [64, 128, 128], P('slab'), as said below
- coupling: float32 [64, 128, 128], P('slab')
- potential: float32 [64, 128], P('slab'), may hold values from -0.3 to 0.3
- sigma_left: float32 [32, 2, 128, 128], P('energy'), as said below
- sigma_right: float32 [32, 2, 128, 128], P('energy'), as said below
- energy_index: int32 [32], P('energy'), may hold values from 0 to 511
- density_in: float32 [64, 128], P('slab'), may hold values from -6 to 6
- hist_density: float32 [5, 64, 128], P(None, 'slab'), may hold values from -6 to 6
- hist_residual: float32 [5, 64, 128], P(None, 'slab'), may hold values from -3 to 3
Outputs:
- density_out: float32 [64, 128], P('slab')
- density_next: float32 [64, 128], P('slab')
The draws below stay inside these ranges and needn't reach their ends.
Inputs may be any that keep to these rules, and one draw needn't show every extreme that they name: Each block of onsite is symmetric. `sigma_left`: both parts of each self-energy are symmetric; the imaginary part is negative definite. `sigma_right`: both parts of each self-energy are symmetric; the imaginary part is negative definite.
All inputs are finite; a program needn't handle non-finite values.
Results may differ from the reference program's by a relative error of at most 0.0003.
Values sent between devices are 32-bit elements; how exact they have to be, the bound alone decides.
No kernel may reach another device: no remote copies, remote signals or barrier semaphores. Data moves between devices by JAX's collectives and lax.ppermute only.
A program may use at most 128 MiB of HBM per device.

```python
import math
import jax
import jax.numpy as jnp
from jax import lax

B = 128
HIST = 5
GRID = 512
SLABS = 64
ENERGIES = 32


def rough_values(key, shape):
    return jax.random.normal(key, shape, jnp.float32)


def symmetric_noise(key, shape, scale):
    values = rough_values(key, shape)
    return (values + jnp.swapaxes(values, -1, -2)) * (scale * 0.70710678)


def draw_onsite(key, part):
    identity = jnp.eye(B, dtype=jnp.float32)
    noise = symmetric_noise(jax.random.fold_in(key, 11), (SLABS, B, B), 0.5 / math.sqrt(B))
    levels = jax.random.uniform(jax.random.fold_in(key, 12), (SLABS, B, 1), jnp.float32, -0.3, 0.3)
    return noise * (1.0 - identity) + levels * identity


def draw_coupling(key, part):
    identity = jnp.eye(B, dtype=jnp.float32)
    values = rough_values(jax.random.fold_in(key, 21), (SLABS, B, B))
    return 1.2 * identity + values * (0.3 / math.sqrt(B))


def self_energy(key):
    identity = jnp.eye(B, dtype=jnp.float32)
    real_part = symmetric_noise(jax.random.fold_in(key, 41), (ENERGIES, B, B), 0.3 / math.sqrt(B))
    spread = jax.random.uniform(jax.random.fold_in(key, 42), (ENERGIES, B, B), jnp.float32, -0.2 / B, 0.2 / B)
    off_diag = (spread + jnp.swapaxes(spread, 1, 2)) * 0.5 * (1.0 - identity)
    depth = jax.random.uniform(jax.random.fold_in(key, 43), (ENERGIES, B, 1), jnp.float32, 0.3, 1.0)
    imag_part = off_diag - depth * identity
    return jnp.stack([real_part, imag_part], 1)


def draw_sigma_left(key, part):
    return self_energy(jax.random.fold_in(key, 101))


def draw_sigma_right(key, part):
    return self_energy(jax.random.fold_in(key, 202))


def plant(values, own_key, low, high):
    longest = values.shape.index(max(values.shape))
    spots = []
    for shift in (0, 1):
        where = [jax.random.randint(jax.random.fold_in(own_key, axis), (), 0, length) for axis, length in enumerate(values.shape)]
        where[longest] = (where[longest] + shift) % values.shape[longest]
        spots.append(tuple(where))
    return values.at[spots[0]].set(low).at[spots[1]].set(high)


def shard_levels(rng, extent, shards, low, largest):
    factor_of, own = 1.0, jax.random.fold_in(rng, 6)
    for axis_at, shards_of in shards:
        heights = jnp.exp(jax.random.uniform(jax.random.fold_in(own, axis_at), (shards_of,), jnp.float32, low / len(shards), largest / len(shards)))
        factor_of = factor_of * jnp.repeat(heights, extent[axis_at] // shards_of).reshape([-1 if axis == axis_at else 1 for axis in range(len(extent))])
    return factor_of


def normal_values(key, dims, scale, limit, shards=(), kind=jnp.bfloat16):
    result = jax.random.normal(key, dims, jnp.float32) * scale
    if len(shards) > 0:
        result = shard_levels(key, dims, shards, -0.22, 0.18) * result
    return jnp.clip(result, min=-limit, max=limit).astype(kind)


def setup_inputs(seed: int = 0) -> dict:
    arg_keys = jax.random.split(jax.random.key(seed), 10)
    return {
        "onsite": draw_onsite(jax.random.fold_in(arg_keys[9], 71), 0),
        "coupling": draw_coupling(jax.random.fold_in(arg_keys[9], 71), 0),
        "potential": jnp.clip(jax.random.uniform(arg_keys[2], (SLABS, B), jnp.float32, -0.3, 0.3) * shard_levels(arg_keys[2], (SLABS, B), ((0, 16),), -0.4, 0.0), -0.3, 0.3),
        "sigma_left": draw_sigma_left(jax.random.fold_in(arg_keys[9], 71), 0),
        "sigma_right": draw_sigma_right(jax.random.fold_in(arg_keys[9], 71), 0),
        "energy_index": plant(jax.random.randint(arg_keys[5], (ENERGIES,), 0, GRID), jax.random.fold_in(arg_keys[5], 1), 0, GRID - 1).astype(jnp.int32),
        "density_in": normal_values(arg_keys[6], (SLABS, B), 1.0, 6.0, ((0, 16),), jnp.float32),
        "hist_density": normal_values(arg_keys[7], (HIST, SLABS, B), 1.0, 6.0, ((1, 16),), jnp.float32),
        "hist_residual": normal_values(arg_keys[8], (HIST, SLABS, B), 0.5, 3.0, ((1, 16),), jnp.float32),
    }


HIGH = lax.Precision.HIGHEST
MIX_BETA = 0.3
RIDGE = 0.01

def matmul_high(left_mat, right_mat):
    return jnp.matmul(left_mat, right_mat, precision=HIGH)

def complex_inverse(real_part, imag_part):
    width = real_part.shape[-1]
    upper_rows = jnp.concatenate([real_part, -imag_part], 1)
    lower_rows = jnp.concatenate([imag_part, real_part], 1)
    inverse = jnp.linalg.inv(jnp.concatenate([upper_rows, lower_rows], 0))
    return (inverse[:width, :width], inverse[width:, :width])

def energy_density(onsite, lower_real, upper_real, potential, energy_value, sigma_one, sigma_two):
    width = onsite.shape[-1]
    count = onsite.shape[0]
    identity = jnp.eye(width, dtype=jnp.float32)
    diag_real = energy_value * identity - onsite - potential[:, :, None] * identity
    diag_imag = jnp.broadcast_to(2.0 / SLABS * identity, diag_real.shape)
    diag_real = diag_real.at[0].add(-sigma_one[0]).at[count - 1].add(-sigma_two[0])
    diag_imag = diag_imag.at[0].add(-sigma_one[1]).at[count - 1].add(-sigma_two[1])

    def backward(carry, inputs):
        cur_real, cur_imag = carry
        block_real, block_imag, upper_block, lower_block = inputs
        inv_real, inv_imag = complex_inverse(cur_real, cur_imag)
        prop_real = matmul_high(inv_real, lower_block)
        prop_imag = matmul_high(inv_imag, lower_block)
        new_real = block_real - matmul_high(upper_block, prop_real)
        new_imag = block_imag - matmul_high(upper_block, prop_imag)
        return ((new_real, new_imag), (prop_real, prop_imag))
    carry, props = lax.scan(backward, (diag_real[-1], diag_imag[-1]), (diag_real[:-1], diag_imag[:-1], upper_real[:-1], lower_real[1:]), reverse=True)
    first_real, first_imag = complex_inverse(carry[0], carry[1])

    def forward(carry, prop):
        cur_real, cur_imag = carry
        prop_real, prop_imag = prop
        new_real = -(matmul_high(prop_real, cur_real) - matmul_high(prop_imag, cur_imag))
        new_imag = -(matmul_high(prop_real, cur_imag) + matmul_high(prop_imag, cur_real))
        return ((new_real, new_imag), (new_real, new_imag))
    final, rest = lax.scan(forward, (first_real, first_imag), props)
    sol_real = jnp.concatenate([first_real[None], rest[0]], 0)
    sol_imag = jnp.concatenate([first_imag[None], rest[1]], 0)
    gamma = -(sigma_one[1] + sigma_one[1].T)
    return jnp.sum(matmul_high(sol_real, gamma) * sol_real + matmul_high(sol_imag, gamma) * sol_imag, -1)

def reference(onsite, coupling, potential, sigma_left, sigma_right, energy_index, density_in, hist_density, hist_residual):
    width = onsite.shape[-1]
    energy = -0.4 + 0.8 * (energy_index.astype(jnp.float32) + 0.5) / GRID
    weight = 4.0 / ENERGIES / (1.0 + jnp.exp(energy / 0.1))
    zero_block = jnp.zeros((1, width, width), jnp.float32)
    lower_real = jnp.concatenate([zero_block, -jnp.swapaxes(coupling[:-1], 1, 2)], 0)
    upper_real = jnp.concatenate([-coupling[:-1], zero_block], 0)

    def one_energy(inputs):
        energy_value, weight_value, sigma_one, sigma_two = inputs
        return weight_value * energy_density(onsite, lower_real, upper_real, potential, energy_value, sigma_one, sigma_two)
    per_energy = lax.map(one_energy, (energy, weight, sigma_left, sigma_right))
    density_out = jnp.sum(per_energy, 0)
    residual = density_out - density_in
    delta_n = density_in[None] - hist_density
    delta_f = residual[None] - hist_residual
    gram = jnp.einsum('kab,lab->kl', delta_f, delta_f, precision=HIGH)
    target = jnp.einsum('kab,ab->k', delta_f, residual, precision=HIGH)
    ridge = RIDGE * jnp.trace(gram) / HIST
    mix_coeffs = jnp.linalg.solve(gram + ridge * jnp.eye(HIST, dtype=jnp.float32), target)
    density_next = density_in + MIX_BETA * residual - jnp.einsum('k,kab->ab', mix_coeffs, delta_n + MIX_BETA * delta_f, precision=HIGH)
    return (density_out, density_next)
```

```python
import jax, jax.numpy as jnp
from jax import lax
from jax.experimental import pallas as pl
from jax.experimental.pallas import tpu as pltpu
from jax.sharding import PartitionSpec as P

INTERPRET = False
W = 128
PB = 16
F32 = jnp.float32
BF16 = jnp.bfloat16


def dot(a, b):
    return jnp.dot(a, b, preferred_element_type=F32)


def dot_tn(a, b):
    return lax.dot_general(a, b, (((0,), (0,)), ((), ())), preferred_element_type=F32)


def split2(x):
    hi = x.astype(BF16)
    return hi, (x - hi.astype(F32)).astype(BF16)


def split3(x):
    hi = x.astype(BF16)
    rest = x - hi.astype(F32)
    mid = rest.astype(BF16)
    return hi, mid, (rest - mid.astype(F32)).astype(BF16)


def swap_parts(x):
    return jnp.concatenate([-x[:, W:], x[:, :W]], 1)


def as_right(x):
    return jnp.concatenate([x, swap_parts(x)], 0)


def mul3(left, right):
    lh, ll = split2(left)
    rh, rl = split2(right)
    return dot(lh, rh) + (dot(ll, rh) + dot(lh, rl))


def cmul(left, right):
    return mul3(left, as_right(right))


def ctrans(x):
    return jnp.concatenate([x[:, :W].T, x[:, W:].T], 1)


def sweep_panels(mats):
    lane = lax.broadcasted_iota(jnp.int32, (8, W), 1)
    row = lax.broadcasted_iota(jnp.int32, (8, W), 0)
    keep = lax.broadcasted_iota(jnp.int32, (W - PB, W), 1) < W - PB
    halves = PB // 8

    def panel(_, carry):
        state = []
        for ref in mats:
            pr = [ref[8 * g : 8 * g + 8, :W] for g in range(halves)]
            pi = [ref[8 * g : 8 * g + 8, W:] for g in range(halves)]
            cols_r = [[jnp.broadcast_to(pr[g][:, j : j + 1], (8, W)) for g in range(halves)] for j in range(PB)]
            cols_i = [[jnp.broadcast_to(pi[g][:, j : j + 1], (8, W)) for g in range(halves)] for j in range(PB)]
            own_r = []
            own_i = []
            for g in range(halves):
                unit = jnp.where(lane == row + 8 * g, -1.0, 0.0)
                own_r.append(pltpu.roll(jnp.where(lane < PB, unit, pr[g]), W - PB, 1))
                own_i.append(pltpu.roll(jnp.where(lane < PB, 0.0, pi[g]), W - PB, 1))
            state.append((cols_r + [own_r], cols_i + [own_i], own_r, own_i))
        for k in range(PB):
            gk, rk = divmod(k, 8)
            for cols_r, cols_i, _, _ in state:
                mult_r, mult_i = cols_r[k], cols_i[k]
                piv_r = mult_r[gk][rk : rk + 1]
                piv_i = mult_i[gk][rk : rk + 1]
                den = 1.0 / (piv_r * piv_r + piv_i * piv_i)
                inv_r = piv_r * den
                inv_i = -piv_i * den
                for j in range(k + 1, PB + 1):
                    xr, xi = cols_r[j], cols_i[j]
                    row_r = xr[gk][rk : rk + 1]
                    row_i = xi[gk][rk : rk + 1]
                    sr = jnp.broadcast_to(row_r * inv_r - row_i * inv_i, (8, W))
                    si = jnp.broadcast_to(row_r * inv_i + row_i * inv_r, (8, W))
                    new_r, new_i = [], []
                    for g in range(halves):
                        nr = xr[g] - (mult_r[g] * sr - mult_i[g] * si)
                        ni = xi[g] - (mult_r[g] * si + mult_i[g] * sr)
                        if g == gk:
                            nr = jnp.where(row == rk, sr, nr)
                            ni = jnp.where(row == rk, si, ni)
                        new_r.append(nr)
                        new_i.append(ni)
                    cols_r[j], cols_i[j] = new_r, new_i
        for ref, (cols_r, cols_i, own_r, own_i) in zip(mats, state):
            pieces_p = split3(jnp.concatenate(own_r + own_i, 0))
            wr = jnp.concatenate(cols_r[PB], 0)
            wi = jnp.concatenate(cols_i[PB], 0)
            right = jnp.concatenate(
                [jnp.concatenate([wr, wi], 1), jnp.concatenate([-wi, wr], 1)], 0
            )
            pieces_w = split3(right)
            order = ((0, 0), (0, 1), (1, 0), (0, 2), (2, 0), (1, 1))
            lhs = jnp.concatenate([pieces_p[a] for a, _ in order], 0)
            rhs = jnp.concatenate([pieces_w[b] for _, b in order], 0)
            update = dot_tn(lhs, rhs)
            old_r = jnp.where(keep, pltpu.roll(ref[PB:, :W], W - PB, 1), 0.0)
            old_i = jnp.where(keep, pltpu.roll(ref[PB:, W:], W - PB, 1), 0.0)
            ref[: W - PB, :W] = old_r - update[: W - PB, :W]
            ref[: W - PB, W:] = old_i - update[: W - PB, W:]
            ref[W - PB :, :] = -update[W - PB :, :]
        return carry

    lax.fori_loop(0, W // PB, panel, 0)


def invert(refs):
    sweep_panels(refs)
    return [-ref[...] for ref in refs]


def local_kernel(flag_ref, energy_ref, onsite_ref, coupling_ref, potential_ref, left_ref, right_ref, segment_ref, prop_ref, mat_a, mat_b):
    is_first = flag_ref[0] == 1
    is_last = flag_ref[1] == 1
    energy = energy_ref[0]
    eye = (
        lax.broadcasted_iota(jnp.int32, (W, W), 0) == lax.broadcasted_iota(jnp.int32, (W, W), 1)
    )
    broaden = jnp.where(eye, energy_ref[1], 0.0)

    def diagonal(s):
        real = jnp.where(eye, energy - potential_ref[s : s + 1, :], 0.0) - onsite_ref[s]
        return jnp.concatenate([real, broaden], 1)

    mat_a[...] = diagonal(1)
    last = jnp.concatenate([right_ref[0], right_ref[1]], 1)
    mat_b[...] = diagonal(3) - jnp.where(is_last, last, 0.0)
    inv_1, inv_3 = invert([mat_a, mat_b])
    c0, c1, c2 = coupling_ref[0], coupling_ref[1], coupling_ref[2]
    c3 = jnp.where(is_last, 0.0, coupling_ref[3])
    c0t, c2t = c0.T, c2.T

    def real_right(inv, real):
        stacked = jnp.concatenate([inv[:, :W], inv[:, W:]], 0)
        out = mul3(stacked, real)
        return jnp.concatenate([out[:W], out[W:]], 1)

    prop_1l = real_right(inv_1, c0t)
    prop_1r = real_right(inv_1, c1)
    prop_3l = real_right(inv_3, c2t)
    prop_3r = real_right(inv_3, c3)
    mat_a[...] = diagonal(2) - mul3(c1.T, prop_1r) - mul3(c2, prop_3l)
    (inv_2,) = invert([mat_a])
    first = jnp.concatenate([left_ref[0], left_ref[1]], 1)
    top = diagonal(0) - jnp.where(is_first, first, 0.0) - mul3(c0, prop_1l)
    k02 = mul3(c0, prop_1r)
    k2n = mul3(c2, prop_3r)
    prop_2l = cmul(inv_2, ctrans(k02))
    prop_2r = cmul(inv_2, k2n)
    segment_ref[0] = top - cmul(k02, prop_2l)
    segment_ref[1] = mul3(c3.T, prop_3r) + cmul(ctrans(k2n), prop_2r)
    segment_ref[2] = cmul(k02, prop_2r)
    prop_ref[0] = prop_1l
    prop_ref[1] = prop_1r
    prop_ref[2] = prop_2l
    prop_ref[3] = prop_2r
    prop_ref[4] = prop_3l
    prop_ref[5] = prop_3r


def merge_kernel(flag_ref, mine_ref, other_ref, segment_ref, prop_ref, mat):
    on_left = flag_ref[0] == 1

    def pick(part):
        mine, other = mine_ref[part], other_ref[part]
        return jnp.where(on_left, mine, other), jnp.where(on_left, other, mine)

    diag_l, diag_r = pick(0)
    next_l, next_r = pick(1)
    k_l, k_r = pick(2)
    mat[...] = diag_r - next_l
    (inv,) = invert([mat])
    prop_l = cmul(inv, ctrans(k_l))
    prop_r = cmul(inv, k_r)
    segment_ref[0] = diag_l - cmul(k_l, prop_l)
    segment_ref[1] = next_r + cmul(ctrans(k_r), prop_r)
    segment_ref[2] = cmul(k_l, prop_r)
    prop_ref[0] = prop_l
    prop_ref[1] = prop_r


def final_kernel(flag_ref, weight_ref, mine_ref, other_ref, local_ref, prop_a_ref, prop_b_ref, prop_c_ref, left_ref, density_ref, mat):
    on_left = flag_ref[3] == 1

    def pick(part):
        mine, other = mine_ref[part], other_ref[part]
        return jnp.where(on_left, mine, other), jnp.where(on_left, other, mine)

    diag_l, diag_r = pick(0)
    next_l, _ = pick(1)
    k_l, _ = pick(2)
    mat[...] = diag_r - next_l
    (inv,) = invert([mat])
    prop = cmul(inv, ctrans(k_l))
    mat[...] = diag_l - cmul(k_l, prop)
    (root,) = invert([mat])
    middle = cmul(prop, root)
    x_left = jnp.where(on_left, root, middle)
    x_right = jnp.where(on_left, middle, 0.0)
    for level, ref in ((2, prop_c_ref), (1, prop_b_ref), (0, prop_a_ref)):
        inside = cmul(ref[0], x_left) + cmul(ref[1], x_right)
        goes = flag_ref[level] == 1
        x_left, x_right = jnp.where(goes, x_left, inside), jnp.where(goes, inside, x_right)
    x_2 = cmul(local_ref[2], x_left) + cmul(local_ref[3], x_right)
    x_1 = cmul(local_ref[0], x_left) + cmul(local_ref[1], x_2)
    x_3 = cmul(local_ref[4], x_2) + cmul(local_ref[5], x_right)
    imag = left_ref[1]
    gamma = -(imag + imag.T)
    weight = weight_ref[0]
    for s, x in enumerate((x_left, x_1, x_2, x_3)):
        stacked = jnp.concatenate([x[:, :W], x[:, W:]], 0)
        terms = mul3(stacked, gamma) * stacked
        both = terms[:W] + terms[W:]
        density_ref[s : s + 1, :] = weight * jnp.sum(both.T, axis=0, keepdims=True)


def call(kernel, shapes, in_smem, n_in, scratch):
    smem = pl.BlockSpec(memory_space=pltpu.SMEM)
    vmem = pl.BlockSpec(memory_space=pltpu.VMEM)
    return pl.pallas_call(
        kernel,
        out_shape=[jax.ShapeDtypeStruct(s, F32) for s in shapes],
        in_specs=[smem] * in_smem + [vmem] * n_in,
        out_specs=[vmem] * len(shapes),
        scratch_shapes=[pltpu.VMEM((W, 2 * W), F32)] * scratch,
        compiler_params=pltpu.CompilerParams(vmem_limit_bytes=32 << 20),
        interpret=INTERPRET,
    )


GRID = 512
MIX_BETA = 0.3
RIDGE = 0.01
HIGH = lax.Precision.HIGHEST


def swap(block, distance):
    count = lax.axis_size("slab")
    return lax.ppermute(block, "slab", [(i, i ^ distance) for i in range(count)])


def energy_sum(value):
    count = lax.axis_size("energy")
    inner = 4
    rows = [[z * inner + x for x in range(inner)] for z in range(count // inner)]
    cols = [[z * inner + x for z in range(count // inner)] for x in range(inner)]
    value = lax.psum(value, "energy", axis_index_groups=rows)
    return lax.psum(value, "energy", axis_index_groups=cols)


def solve_small(matrix, right_side):
    count = matrix.shape[0]
    work = jnp.concatenate([matrix, right_side[:, None]], 1)
    for k in range(count):
        scaled = work[k] / work[k, k]
        work = work - work[:, k : k + 1] * scaled[None]
        work = work.at[k].set(scaled)
    return work[:, count]


def anderson(total, current, past_density, past_residual):
    residual = total - current
    delta_n = current[None] - past_density
    delta_f = residual[None] - past_residual
    rows = jnp.concatenate([delta_f, residual[None]], 0)
    sums = jnp.sum(delta_f[:, None] * rows[None], (2, 3))
    sums = jnp.pad(sums, ((0, 8 - sums.shape[0]), (0, 128 - sums.shape[1])))
    sums = jnp.sum(lax.all_gather(sums, "slab"), 0)
    count = past_density.shape[0]
    gram, target = sums[:count, :count], sums[:count, count]
    ridge = RIDGE * jnp.trace(gram) / count
    mix = solve_small(gram + ridge * jnp.eye(count, dtype=F32), target)
    step = delta_n + MIX_BETA * delta_f
    return current + MIX_BETA * residual - jnp.sum(mix[:, None, None] * step, 0)


def on_device(onsite, coupling, potential, sigma_left, sigma_right, energy_index, density_in, hist_density, hist_residual):
    slab_count = lax.axis_size("slab")
    position = lax.axis_index("slab")
    per_dev = onsite.shape[0]
    energies_all = energy_index.shape[0] * lax.axis_size("energy")
    energy = -0.4 + 0.8 * (energy_index.astype(F32) + 0.5) / GRID
    weight = 4.0 / energies_all / (1.0 + jnp.exp(energy / 0.1))
    broaden = jnp.full((1,), 2.0 / (per_dev * slab_count), F32)
    ends = jnp.stack([position == 0, position == slab_count - 1]).astype(jnp.int32)
    sides = jnp.stack([(position // (1 << level)) % 2 == 0 for level in range(4)]).astype(jnp.int32)
    left, right = sigma_left[0], sigma_right[0]
    segment, local = call(local_kernel, [(3, W, 2 * W), (6, W, 2 * W)], 2, 5, 2)(
        ends, jnp.concatenate([energy, broaden]), onsite, coupling, potential, left, right
    )
    props = []
    for level in range(3):
        other = swap(segment, 1 << level)
        segment, prop = call(merge_kernel, [(3, W, 2 * W), (2, W, 2 * W)], 1, 2, 1)(
            sides[level : level + 1], segment, other
        )
        props.append(prop)
    other = swap(segment, 8)
    (density,) = call(final_kernel, [(per_dev, W)], 2, 7, 1)(
        sides, weight, segment, other, local, props[0], props[1], props[2], left
    )
    total = energy_sum(density)
    return (total, anderson(total, density_in, hist_density, hist_residual))


def solution(mesh):
    in_specs = (
        P("slab", None, None),
        P("slab", None, None),
        P("slab", None),
        P("energy", None, None, None),
        P("energy", None, None, None),
        P("energy"),
        P("slab", None),
        P(None, "slab", None),
        P(None, "slab", None),
    )
    out_specs = (P("slab", None), P("slab", None))
    return jax.shard_map(
        on_device, mesh=mesh, in_specs=in_specs, out_specs=out_specs, check_vma=False
    )
```

```python
import functools

import jax
import jax.numpy as jnp
from jax import lax
from jax.experimental import pallas as pl
from jax.experimental.pallas import tpu as pltpu
from jax.sharding import PartitionSpec as P

INTERPRET = False
W = 128
PB = 16
F32 = jnp.float32
BF16 = jnp.bfloat16


def dot(a, b):
    return jnp.dot(a, b, preferred_element_type=F32)


def dot_tn(a, b):
    return lax.dot_general(a, b, (((0,), (0,)), ((), ())), preferred_element_type=F32)


def split2(x):
    hi = x.astype(BF16)
    return hi, (x - hi.astype(F32)).astype(BF16)


def split3(x):
    hi = x.astype(BF16)
    rest = x - hi.astype(F32)
    mid = rest.astype(BF16)
    return hi, mid, (rest - mid.astype(F32)).astype(BF16)


def swap_parts(x):
    return jnp.concatenate([-x[:, W:], x[:, :W]], 1)


def as_right(x):
    return jnp.concatenate([x, swap_parts(x)], 0)


def mul3(left, right):
    lh, ll = split2(left)
    rh, rl = split2(right)
    return dot(lh, rh) + (dot(ll, rh) + dot(lh, rl))


def cmul(left, right):
    return mul3(left, as_right(right))


def ctrans(x):
    return jnp.concatenate([x[:, :W].T, x[:, W:].T], 1)


def sweep_panels(mats):
    lane = lax.broadcasted_iota(jnp.int32, (8, W), 1)
    row = lax.broadcasted_iota(jnp.int32, (8, W), 0)
    keep = lax.broadcasted_iota(jnp.int32, (W - PB, W), 1) < W - PB
    halves = PB // 8

    def panel(_, carry):
        state = []
        for ref in mats:
            pr = [ref[8 * g : 8 * g + 8, :W] for g in range(halves)]
            pi = [ref[8 * g : 8 * g + 8, W:] for g in range(halves)]
            cols_r = [[jnp.broadcast_to(pr[g][:, j : j + 1], (8, W)) for g in range(halves)] for j in range(PB)]
            cols_i = [[jnp.broadcast_to(pi[g][:, j : j + 1], (8, W)) for g in range(halves)] for j in range(PB)]
            own_r = []
            own_i = []
            for g in range(halves):
                unit = jnp.where(lane == row + 8 * g, -1.0, 0.0)
                own_r.append(pltpu.roll(jnp.where(lane < PB, unit, pr[g]), W - PB, 1))
                own_i.append(pltpu.roll(jnp.where(lane < PB, 0.0, pi[g]), W - PB, 1))
            state.append((cols_r + [own_r], cols_i + [own_i], own_r, own_i))
        for k in range(PB):
            gk, rk = divmod(k, 8)
            for cols_r, cols_i, _, _ in state:
                mult_r, mult_i = cols_r[k], cols_i[k]
                piv_r = mult_r[gk][rk : rk + 1]
                piv_i = mult_i[gk][rk : rk + 1]
                den = 1.0 / (piv_r * piv_r + piv_i * piv_i)
                inv_r = piv_r * den
                inv_i = -piv_i * den
                for j in range(k + 1, PB + 1):
                    xr, xi = cols_r[j], cols_i[j]
                    row_r = xr[gk][rk : rk + 1]
                    row_i = xi[gk][rk : rk + 1]
                    sr = jnp.broadcast_to(row_r * inv_r - row_i * inv_i, (8, W))
                    si = jnp.broadcast_to(row_r * inv_i + row_i * inv_r, (8, W))
                    new_r, new_i = [], []
                    for g in range(halves):
                        nr = xr[g] - (mult_r[g] * sr - mult_i[g] * si)
                        ni = xi[g] - (mult_r[g] * si + mult_i[g] * sr)
                        if g == gk:
                            nr = jnp.where(row == rk, sr, nr)
                            ni = jnp.where(row == rk, si, ni)
                        new_r.append(nr)
                        new_i.append(ni)
                    cols_r[j], cols_i[j] = new_r, new_i
        for ref, (cols_r, cols_i, own_r, own_i) in zip(mats, state):
            pieces_p = split3(jnp.concatenate(own_r + own_i, 0))
            wr = jnp.concatenate(cols_r[PB], 0)
            wi = jnp.concatenate(cols_i[PB], 0)
            right = jnp.concatenate(
                [jnp.concatenate([wr, wi], 1), jnp.concatenate([-wi, wr], 1)], 0
            )
            pieces_w = split3(right)
            order = ((0, 0), (0, 1), (1, 0), (0, 2), (2, 0), (1, 1))
            lhs = jnp.concatenate([pieces_p[a] for a, _ in order], 0)
            rhs = jnp.concatenate([pieces_w[b] for _, b in order], 0)
            update = dot_tn(lhs, rhs)
            old_r = jnp.where(keep, pltpu.roll(ref[PB:, :W], W - PB, 1), 0.0)
            old_i = jnp.where(keep, pltpu.roll(ref[PB:, W:], W - PB, 1), 0.0)
            ref[: W - PB, :W] = old_r - update[: W - PB, :W]
            ref[: W - PB, W:] = old_i - update[: W - PB, W:]
            ref[W - PB :, :] = -update[W - PB :, :]
        return carry

    lax.fori_loop(0, W // PB, panel, 0)


def invert(refs):
    sweep_panels(refs)
    return [-ref[...] for ref in refs]


def real_right(inv, real):
    out = mul3(jnp.concatenate([inv[:, :W], inv[:, W:]], 0), real)
    return jnp.concatenate([out[:W], out[W:]], 1)


def local_kernel(
    flag_ref, energy_ref, onsite_hbm, coupling_hbm, potential_ref, left_hbm, right_hbm,
    part_ref, prop_ref,
    onsite_ref, coupling_ref, left_ref, right_ref, mat_a, mat_b, sems,
):
    is_first = flag_ref[0] == 1
    is_last = flag_ref[1] == 1
    energy = energy_ref[0]
    copies = []

    def fetch(src, dst):
        copy = pltpu.make_async_copy(src, dst, sems.at[len(copies)])
        copy.start()
        copies.append(copy)
        return copy

    onsite_copy = {s: fetch(onsite_hbm.at[s], onsite_ref.at[s]) for s in (1, 3)}
    right_copy = fetch(right_hbm, right_ref)
    coupling_copy = [fetch(coupling_hbm.at[s], coupling_ref.at[s]) for s in range(4)]
    onsite_copy.update({s: fetch(onsite_hbm.at[s], onsite_ref.at[s]) for s in (2, 0)})
    left_copy = fetch(left_hbm, left_ref)
    eye = lax.broadcasted_iota(jnp.int32, (W, W), 0) == lax.broadcasted_iota(jnp.int32, (W, W), 1)
    broaden = jnp.where(eye, energy_ref[1], 0.0)

    def diagonal(s):
        onsite_copy[s].wait()
        real = jnp.where(eye, energy - potential_ref[s : s + 1, :], 0.0) - onsite_ref[s]
        return jnp.concatenate([real, broaden], 1)

    mat_a[...] = diagonal(1)
    diag_3 = diagonal(3)
    right_copy.wait()
    last = jnp.concatenate([right_ref[0], right_ref[1]], 1)
    mat_b[...] = diag_3 - jnp.where(is_last, last, 0.0)
    inv_1, inv_3 = invert([mat_a, mat_b])
    for copy in coupling_copy:
        copy.wait()
    c0, c1, c2 = coupling_ref[0], coupling_ref[1], coupling_ref[2]
    c3 = jnp.where(is_last, 0.0, coupling_ref[3])
    prop_1r = real_right(inv_1, c1)
    prop_3l = real_right(inv_3, c2.T)
    mat_a[...] = diagonal(2) - mul3(c1.T, prop_1r) - mul3(c2, prop_3l)
    (inv_2,) = invert([mat_a])
    prop_1l = real_right(inv_1, c0.T)
    prop_3r = real_right(inv_3, c3)
    diag_0 = diagonal(0)
    left_copy.wait()
    first = jnp.concatenate([left_ref[0], left_ref[1]], 1)
    top = diag_0 - jnp.where(is_first, first, 0.0) - mul3(c0, prop_1l)
    k02 = mul3(c0, prop_1r)
    k2n = mul3(c2, prop_3r)
    prop_2l = cmul(inv_2, ctrans(k02))
    prop_2r = cmul(inv_2, k2n)
    part_ref[0] = top - cmul(k02, prop_2l)
    part_ref[1] = mul3(c3.T, prop_3r) + cmul(ctrans(k2n), prop_2r)
    part_ref[2] = cmul(k02, prop_2r)
    for n, prop in enumerate((prop_1l, prop_1r, prop_2l, prop_2r, prop_3l, prop_3r)):
        prop_ref[n] = prop


def urgent(inv, link_l, link_r, diag_l, next_r, goes_left):
    side = jnp.where(goes_left, link_r, ctrans(link_l))
    prop = cmul(inv, side)
    change = cmul(ctrans(side), prop)
    return prop, jnp.where(goes_left, next_r + change, diag_l - change)


def others(inv, prop, link_l, link_r, diag_l, next_r, goes_left, rest_ref, prop_ref):
    side = jnp.where(goes_left, ctrans(link_l), link_r)
    second = cmul(inv, side)
    change = cmul(ctrans(side), second)
    prop_r = jnp.where(goes_left, prop, second)
    rest_ref[0] = jnp.where(goes_left, diag_l - change, next_r + change)
    rest_ref[1] = cmul(link_l, prop_r)
    prop_ref[0] = jnp.where(goes_left, second, prop)
    prop_ref[1] = prop_r


def chip_kernel(side_ref, mine_ref, other_ref, inv_ref, first_ref, crit_ref, mat):
    mat[...] = other_ref[0] - mine_ref[1]
    (inv,) = invert([mat])
    inv_ref[...] = inv
    first_ref[...], crit_ref[...] = urgent(
        inv, mine_ref[2], other_ref[2], mine_ref[0], other_ref[1], side_ref[1] == 1
    )


def chip_rest_kernel(side_ref, inv_ref, first_ref, mine_ref, other_ref, rest_ref, prop_ref):
    others(
        inv_ref[...], first_ref[...], mine_ref[2], other_ref[2], mine_ref[0], other_ref[1],
        side_ref[1] == 1, rest_ref, prop_ref,
    )


def inverse_kernel(level, side_ref, mine_ref, other_ref, inv_ref, mat):
    mine, other = mine_ref[...], other_ref[...]
    mat[...] = jnp.where(side_ref[level] == 1, other - mine, mine - other)
    (inv_ref[...],) = invert([mat])


def both_sides(level, side_ref, mine_ref, other_ref):
    on_left = side_ref[level] == 1

    def pick(part):
        mine, other = mine_ref[part], other_ref[part]
        return jnp.where(on_left, mine, other), jnp.where(on_left, other, mine)

    diag_l, next_r = pick(0)
    link_l, link_r = pick(1)
    return link_l, link_r, diag_l, next_r, side_ref[level + 1] == 1


def crit_kernel(level, side_ref, inv_ref, mine_ref, other_ref, first_ref, crit_ref):
    first_ref[...], crit_ref[...] = urgent(
        inv_ref[...], *both_sides(level, side_ref, mine_ref, other_ref)
    )


def rest_kernel(level, side_ref, inv_ref, first_ref, mine_ref, other_ref, rest_ref, prop_ref):
    others(
        inv_ref[...], first_ref[...], *both_sides(level, side_ref, mine_ref, other_ref), rest_ref, prop_ref
    )


def root_kernel(
    side_ref, inv_ref, mine_ref, other_ref, prop_a_ref, prop_b_ref, prop_c_ref, mine_out, partner_out, mat
):
    on_left = side_ref[3] == 1
    diag_l = jnp.where(on_left, mine_ref[0], other_ref[0])
    link_l = jnp.where(on_left, mine_ref[1], other_ref[1])
    prop = cmul(inv_ref[...], ctrans(link_l))
    mat[...] = diag_l - cmul(link_l, prop)
    (root,) = invert([mat])
    middle = cmul(prop, root)
    x_left = jnp.where(on_left, root, middle)
    x_right = jnp.where(on_left, middle, 0.0)
    for level, ref in ((2, prop_c_ref), (1, prop_b_ref)):
        inside = cmul(ref[0], x_left) + cmul(ref[1], x_right)
        goes = side_ref[level] == 1
        x_left, x_right = jnp.where(goes, x_left, inside), jnp.where(goes, inside, x_right)
    inside = cmul(prop_a_ref[0], x_left) + cmul(prop_a_ref[1], x_right)
    mine_out[0] = x_left
    mine_out[1] = inside
    partner_out[0] = inside
    partner_out[1] = x_right


def density_kernel(side_ref, weight_ref, mine_ref, got_ref, prop_ref, left_ref, density_ref):
    own = side_ref[0] == 1
    x_left = jnp.where(own, mine_ref[0], got_ref[0])
    x_right = jnp.where(own, mine_ref[1], got_ref[1])
    x_2 = cmul(prop_ref[2], x_left) + cmul(prop_ref[3], x_right)
    x_1 = cmul(prop_ref[0], x_left) + cmul(prop_ref[1], x_2)
    x_3 = cmul(prop_ref[4], x_2) + cmul(prop_ref[5], x_right)
    imag = left_ref[1]
    gamma = -(imag + imag.T)
    weight = weight_ref[0]
    for s, x in enumerate((x_left, x_1, x_2, x_3)):
        stacked = jnp.concatenate([x[:, :W], x[:, W:]], 0)
        terms = mul3(stacked, gamma) * stacked
        both = terms[:W] + terms[W:]
        density_ref[s : s + 1, :] = weight * jnp.sum(both.T, axis=0, keepdims=True)


def moments_kernel(total_ref, current_ref, past_ref, sums_ref):
    residual = total_ref[...] - current_ref[...]
    count = past_ref.shape[0]
    diffs = [residual - past_ref[k] for k in range(count)]
    rows = []
    for k in range(count):
        for other in diffs[k:] + [residual]:
            rows.append(jnp.sum(diffs[k] * other, axis=0, keepdims=True))
    rows.append(jnp.zeros((W - len(rows), W), F32))
    sums = jnp.sum(jnp.concatenate(rows, 0).T, axis=0, keepdims=True)
    sums_ref[...] = jnp.broadcast_to(sums, sums_ref.shape)


def mix_kernel(sums_ref, total_ref, current_ref, density_ref, past_ref, next_ref):
    count = past_ref.shape[0]
    sums = jnp.sum(sums_ref[...], axis=0)[0:1]
    gram = {}
    place = 0
    for k in range(count):
        for other in range(k, count + 1):
            entry = jnp.broadcast_to(sums[:, place : place + 1], (1, W))
            gram[k, other] = entry
            if other < count:
                gram[other, k] = entry
            place += 1
    trace = gram[0, 0]
    for k in range(1, count):
        trace = trace + gram[k, k]
    ridge = RIDGE * trace / count
    for k in range(count):
        gram[k, k] = gram[k, k] + ridge
    for k in range(count):
        pivot = 1.0 / gram[k, k]
        for col in range(k + 1, count + 1):
            gram[k, col] = gram[k, col] * pivot
        for row in range(k + 1, count):
            for col in range(k + 1, count + 1):
                gram[row, col] = gram[row, col] - gram[row, k] * gram[k, col]
    mix = [None] * count
    for k in reversed(range(count)):
        value = gram[k, count]
        for col in range(k + 1, count):
            value = value - gram[k, col] * mix[col]
        mix[k] = value
    current = current_ref[...]
    residual = total_ref[...] - current
    out = current + MIX_BETA * residual
    for k in range(count):
        step = (current - density_ref[k]) + MIX_BETA * (residual - past_ref[k])
        out = out - mix[k] * step
    next_ref[...] = out


SMEM = pl.BlockSpec(memory_space=pltpu.SMEM)
VMEM = pl.BlockSpec(memory_space=pltpu.VMEM)
ANY = pl.BlockSpec(memory_space=pltpu.MemorySpace.HBM)
BLOCK = (W, 2 * W)
MAT = pltpu.VMEM(BLOCK, F32)


def call(kernel, name, shapes, in_specs, scratch=(), micros=2):
    return pl.pallas_call(
        kernel,
        out_shape=[jax.ShapeDtypeStruct(s, F32) for s in shapes],
        in_specs=in_specs,
        out_specs=[VMEM] * len(shapes),
        scratch_shapes=list(scratch),
        compiler_params=pltpu.CompilerParams(vmem_limit_bytes=32 << 20),
        name=name,
        cost_estimate=pl.CostEstimate(
            flops=micros * 1000000000, transcendentals=0, bytes_accessed=micros * 3000000
        ),
        interpret=INTERPRET,
    )


GRID = 512
MIX_BETA = 0.3
RIDGE = 0.01


def energy_sum(value):
    count = lax.axis_size("energy")
    inner = 4
    rows = [[z * inner + x for x in range(inner)] for z in range(count // inner)]
    cols = [[z * inner + x for z in range(count // inner)] for x in range(inner)]
    value = lax.psum(value, "energy", axis_index_groups=rows)
    return lax.psum(value, "energy", axis_index_groups=cols)


def in_hbm(array):
    return pltpu.with_memory_space_constraint(array, pltpu.MemorySpace.HBM)


def send(block, route):
    return lax.ppermute(block, "slab", route)


def on_device(onsite, coupling, potential, sigma_left, sigma_right, energy_index, density_in, hist_density, hist_residual):
    slab_count = lax.axis_size("slab")
    position = lax.axis_index("slab")
    per_dev = onsite.shape[0]
    energies_all = energy_index.shape[0] * lax.axis_size("energy")
    energy = -0.4 + 0.8 * (energy_index.astype(F32) + 0.5) / GRID
    weight = 4.0 / energies_all / (1.0 + jnp.exp(energy / 0.1))
    broaden = jnp.full((1,), 2.0 / (per_dev * slab_count), F32)
    ends = jnp.stack([position == 0, position == slab_count - 1]).astype(jnp.int32)
    sides = jnp.stack([(position // (1 << level)) % 2 == 0 for level in range(4)]).astype(jnp.int32)
    left, right = sigma_left[0], sigma_right[0]
    pair = (2,) + BLOCK
    part, local = call(
        local_kernel, "local", [(3,) + BLOCK, (6,) + BLOCK],
        [SMEM, SMEM, ANY, ANY, VMEM, ANY, ANY],
        [
            pltpu.VMEM((per_dev, W, W), F32), pltpu.VMEM((per_dev, W, W), F32),
            pltpu.VMEM((2, W, W), F32), pltpu.VMEM((2, W, W), F32), MAT, MAT,
            pltpu.SemaphoreType.DMA((10,)),
        ],
    )(ends, jnp.concatenate([energy, broaden]), in_hbm(onsite), in_hbm(coupling), potential, in_hbm(left), in_hbm(right))
    evens = range(0, slab_count, 2)
    other = send(part, [(i + 1, i) for i in evens])
    inv, first, crit = call(chip_kernel, "chip", [BLOCK] * 3, [SMEM] + [VMEM] * 2, [MAT])(
        sides, part, other
    )
    route = [(i, i ^ 2) for i in evens]
    crit_other = send(crit, route)
    rest, prop = call(chip_rest_kernel, "chip_rest", [pair, pair], [SMEM] + [VMEM] * 4)(
        sides, inv, first, part, other
    )
    last = slab_count - 2
    props = [prop]
    for level in (1, 2):
        rest_other = send(rest, route)
        (inv,) = call(
            functools.partial(inverse_kernel, level), f"inverse{level}", [BLOCK], [SMEM, VMEM, VMEM], [MAT], 7
        )(sides, crit, crit_other)
        first, crit = call(
            functools.partial(crit_kernel, level), f"crit{level}", [BLOCK, BLOCK], [SMEM] + [VMEM] * 3
        )(sides, inv, rest, rest_other)
        route = [(i, i ^ 4) for i in evens] if level == 1 else [(i, last - i) for i in evens]
        crit_other = send(crit, route)
        rest, prop = call(
            functools.partial(rest_kernel, level), f"rest{level}", [pair, pair], [SMEM] + [VMEM] * 4
        )(sides, inv, first, rest, rest_other)
        props.append(prop)
    rest_other = send(rest, [(i, last - i) for i in evens if i < last - i])
    (inv,) = call(
        functools.partial(inverse_kernel, 3), "inverse3", [BLOCK], [SMEM, VMEM, VMEM], [MAT], 7
    )(sides, crit, crit_other)
    mine, partner = call(root_kernel, "root", [pair, pair], [SMEM] + [VMEM] * 6, [MAT])(
        sides, inv, rest, rest_other, *props
    )
    got = send(partner, [(i, i + 1) for i in evens])
    (density,) = call(density_kernel, "density", [(per_dev, W)], [SMEM, SMEM] + [VMEM] * 4)(
        sides, weight, mine, got, local, left
    )
    total = energy_sum(density)
    (sums,) = call(moments_kernel, "moments", [(8, W)], [VMEM] * 3)(total, density_in, hist_residual)
    sums = lax.all_gather(sums, "slab")
    (following,) = call(mix_kernel, "mix", [(per_dev, W)], [VMEM] * 5)(
        sums, total, density_in, hist_density, hist_residual
    )
    return (total, following)


def solution(mesh):
    in_specs = (
        P("slab", None, None),
        P("slab", None, None),
        P("slab", None),
        P("energy", None, None, None),
        P("energy", None, None, None),
        P("energy"),
        P("slab", None),
        P(None, "slab", None),
        P(None, "slab", None),
    )
    out_specs = (P("slab", None), P("slab", None))
    return jax.shard_map(
        on_device, mesh=mesh, in_specs=in_specs, out_specs=out_specs, check_vma=False
    )
```

```python
import functools

import jax
import jax.numpy as jnp
from jax import lax
from jax.experimental import pallas as pl
from jax.experimental.pallas import tpu as pltpu
from jax.sharding import PartitionSpec as P

INTERPRET = False
W = 128
PB = 16
SUB = 8
ORDER = ((0, 0), (0, 1), (1, 0), (0, 2), (2, 0), (1, 1))
F32 = jnp.float32
BF16 = jnp.bfloat16


def dot(a, b):
    return jnp.dot(a, b, preferred_element_type=F32)


def dot_tn(a, b):
    return lax.dot_general(a, b, (((0,), (0,)), ((), ())), preferred_element_type=F32)


def split2(x):
    hi = x.astype(BF16)
    return hi, (x - hi.astype(F32)).astype(BF16)


def split3(x):
    hi = x.astype(BF16)
    rest = x - hi.astype(F32)
    mid = rest.astype(BF16)
    return hi, mid, (rest - mid.astype(F32)).astype(BF16)


def swap_parts(x):
    return jnp.concatenate([-x[:, W:], x[:, :W]], 1)


def as_right(x):
    return jnp.concatenate([x, swap_parts(x)], 0)


def mul3(left, right):
    lh, ll = split2(left)
    rh, rl = split2(right)
    return dot(lh, rh) + (dot(ll, rh) + dot(lh, rl))


def cmul(left, right):
    return mul3(left, as_right(right))


def ctrans(x):
    return jnp.concatenate([x[:, :W].T, x[:, W:].T], 1)


def sweep_panels(mats):
    lane = lax.broadcasted_iota(jnp.int32, (8, W), 1)
    row = lax.broadcasted_iota(jnp.int32, (8, W), 0)
    keep = lax.broadcasted_iota(jnp.int32, (W - PB, W), 1) < W - PB
    halves = PB // 8

    def spread(parts, j):
        return [
            jnp.broadcast_to(jnp.sum(jnp.where(lane == j, p, 0.0), axis=1, keepdims=True), (8, W))
            for p in parts
        ]

    def eliminate(cols_r, cols_i, k, active):
        gk, rk = divmod(k, 8)
        here = row == rk
        mult_r, mult_i = cols_r[k], cols_i[k]
        piv_r = jnp.broadcast_to(mult_r[gk][rk : rk + 1], (8, W))
        piv_i = jnp.broadcast_to(mult_i[gk][rk : rk + 1], (8, W))
        den = 1.0 / (piv_r * piv_r + piv_i * piv_i)
        inv_r = piv_r * den
        inv_i = -piv_i * den
        fr, fi = [], []
        for g in range(halves):
            a = mult_r[g] * inv_r - mult_i[g] * inv_i
            b = mult_r[g] * inv_i + mult_i[g] * inv_r
            if g == gk:
                a = jnp.where(here, -inv_r, a)
                b = jnp.where(here, -inv_i, b)
            fr.append(a)
            fi.append(b)
        for j in active:
            xr, xi = cols_r[j], cols_i[j]
            row_r = jnp.broadcast_to(xr[gk][rk : rk + 1], (8, W))
            row_i = jnp.broadcast_to(xi[gk][rk : rk + 1], (8, W))
            new_r, new_i = [], []
            for g in range(halves):
                br, bi = xr[g], xi[g]
                if g == gk:
                    br = jnp.where(here, 0.0, br)
                    bi = jnp.where(here, 0.0, bi)
                new_r.append(br - (fr[g] * row_r - fi[g] * row_i))
                new_i.append(bi - (fr[g] * row_i + fi[g] * row_r))
            cols_r[j], cols_i[j] = new_r, new_i

    def panel(_, carry):
        state = []
        for ref in mats:
            pr = [ref[8 * g : 8 * g + 8, :W] for g in range(halves)]
            pi = [ref[8 * g : 8 * g + 8, W:] for g in range(halves)]
            cols_r = {j: spread(pr, j) for j in range(SUB)}
            cols_i = {j: spread(pi, j) for j in range(SUB)}
            own_r = []
            own_i = []
            for g in range(halves):
                unit = jnp.where(lane == row + 8 * g, -1.0, 0.0)
                own_r.append(pltpu.roll(jnp.where(lane < PB, unit, pr[g]), W - PB, 1))
                own_i.append(pltpu.roll(jnp.where(lane < PB, 0.0, pi[g]), W - PB, 1))
            cols_r["w"], cols_i["w"] = own_r, own_i
            cols_r["p"], cols_i["p"] = pr, pi
            state.append((cols_r, cols_i, own_r, own_i))
        for base in range(0, PB, SUB):
            if base:
                for cols_r, cols_i, _, _ in state:
                    for j in range(base, base + SUB):
                        cols_r[j] = spread(cols_r["p"], j)
                        cols_i[j] = spread(cols_i["p"], j)
            for k in range(base, base + SUB):
                active = list(range(k + 1, base + SUB)) + (["p"] if base + SUB < PB else []) + ["w"]
                for cols_r, cols_i, _, _ in state:
                    eliminate(cols_r, cols_i, k, active)
        for ref, (cols_r, cols_i, own_r, own_i) in zip(mats, state):
            pieces_p = split3(jnp.concatenate(own_r + own_i, 0))
            wr = jnp.concatenate(cols_r["w"], 0)
            wi = jnp.concatenate(cols_i["w"], 0)
            right = jnp.concatenate(
                [jnp.concatenate([wr, wi], 1), jnp.concatenate([-wi, wr], 1)], 0
            )
            pieces_w = split3(right)
            lhs = jnp.concatenate([pieces_p[a] for a, _ in ORDER], 0)
            rhs = jnp.concatenate([pieces_w[b] for _, b in ORDER], 0)
            update = dot_tn(lhs, rhs)
            old_r = jnp.where(keep, pltpu.roll(ref[PB:, :W], W - PB, 1), 0.0)
            old_i = jnp.where(keep, pltpu.roll(ref[PB:, W:], W - PB, 1), 0.0)
            ref[: W - PB, :W] = old_r - update[: W - PB, :W]
            ref[: W - PB, W:] = old_i - update[: W - PB, W:]
            ref[W - PB :, :] = -update[W - PB :, :]
        return carry

    lax.fori_loop(0, W // PB, panel, 0)


def invert(refs):
    sweep_panels(refs)
    return [-ref[...] for ref in refs]


def real_right(inv, real):
    out = mul3(jnp.concatenate([inv[:, :W], inv[:, W:]], 0), real)
    return jnp.concatenate([out[:W], out[W:]], 1)


def local_kernel(
    flag_ref, energy_ref, onsite_hbm, coupling_hbm, potential_ref, left_hbm, right_hbm,
    part_ref, prop_ref,
    onsite_ref, coupling_ref, left_ref, right_ref, mat_a, mat_b, sems,
):
    is_first = flag_ref[0] == 1
    is_last = flag_ref[1] == 1
    energy = energy_ref[0]
    copies = []

    def fetch(src, dst):
        copy = pltpu.make_async_copy(src, dst, sems.at[len(copies)])
        copy.start()
        copies.append(copy)
        return copy

    onsite_copy = {s: fetch(onsite_hbm.at[s], onsite_ref.at[s]) for s in (1, 3)}
    right_copy = fetch(right_hbm, right_ref)
    coupling_copy = [fetch(coupling_hbm.at[s], coupling_ref.at[s]) for s in range(4)]
    onsite_copy.update({s: fetch(onsite_hbm.at[s], onsite_ref.at[s]) for s in (2, 0)})
    left_copy = fetch(left_hbm, left_ref)
    eye = lax.broadcasted_iota(jnp.int32, (W, W), 0) == lax.broadcasted_iota(jnp.int32, (W, W), 1)
    broaden = jnp.where(eye, energy_ref[1], 0.0)

    def diagonal(s):
        onsite_copy[s].wait()
        real = jnp.where(eye, energy - potential_ref[s : s + 1, :], 0.0) - onsite_ref[s]
        return jnp.concatenate([real, broaden], 1)

    mat_a[...] = diagonal(1)
    diag_3 = diagonal(3)
    right_copy.wait()
    last = jnp.concatenate([right_ref[0], right_ref[1]], 1)
    mat_b[...] = diag_3 - jnp.where(is_last, last, 0.0)
    inv_1, inv_3 = invert([mat_a, mat_b])
    for copy in coupling_copy:
        copy.wait()
    c0, c1, c2 = coupling_ref[0], coupling_ref[1], coupling_ref[2]
    c3 = jnp.where(is_last, 0.0, coupling_ref[3])
    prop_1r = real_right(inv_1, c1)
    prop_3l = real_right(inv_3, c2.T)
    mat_a[...] = diagonal(2) - mul3(c1.T, prop_1r) - mul3(c2, prop_3l)
    (inv_2,) = invert([mat_a])
    prop_1l = real_right(inv_1, c0.T)
    prop_3r = real_right(inv_3, c3)
    diag_0 = diagonal(0)
    left_copy.wait()
    first = jnp.concatenate([left_ref[0], left_ref[1]], 1)
    top = diag_0 - jnp.where(is_first, first, 0.0) - mul3(c0, prop_1l)
    k02 = mul3(c0, prop_1r)
    k2n = mul3(c2, prop_3r)
    prop_2l = cmul(inv_2, ctrans(k02))
    prop_2r = cmul(inv_2, k2n)
    part_ref[0] = top - cmul(k02, prop_2l)
    part_ref[1] = mul3(c3.T, prop_3r) + cmul(ctrans(k2n), prop_2r)
    part_ref[2] = cmul(k02, prop_2r)
    for n, prop in enumerate((prop_1l, prop_1r, prop_2l, prop_2r, prop_3l, prop_3r)):
        prop_ref[n] = prop


def urgent(inv, link_l, link_r, diag_l, next_r, goes_left):
    side = jnp.where(goes_left, link_r, ctrans(link_l))
    prop = cmul(inv, side)
    change = cmul(ctrans(side), prop)
    return prop, jnp.where(goes_left, next_r + change, diag_l - change)


def others(inv, prop, link_l, link_r, diag_l, next_r, goes_left, rest_ref, prop_ref):
    side = jnp.where(goes_left, ctrans(link_l), link_r)
    second = cmul(inv, side)
    change = cmul(ctrans(side), second)
    prop_r = jnp.where(goes_left, prop, second)
    rest_ref[0] = jnp.where(goes_left, diag_l - change, next_r + change)
    rest_ref[1] = cmul(link_l, prop_r)
    prop_ref[0] = jnp.where(goes_left, second, prop)
    prop_ref[1] = prop_r


def chip_kernel(side_ref, mine_ref, other_ref, inv_ref, first_ref, crit_ref, mat):
    mat[...] = other_ref[0] - mine_ref[1]
    (inv,) = invert([mat])
    inv_ref[...] = inv
    first_ref[...], crit_ref[...] = urgent(
        inv, mine_ref[2], other_ref[2], mine_ref[0], other_ref[1], side_ref[1] == 1
    )


def chip_rest_kernel(side_ref, inv_ref, first_ref, mine_ref, other_ref, rest_ref, prop_ref):
    others(
        inv_ref[...], first_ref[...], mine_ref[2], other_ref[2], mine_ref[0], other_ref[1],
        side_ref[1] == 1, rest_ref, prop_ref,
    )


def inverse_kernel(level, side_ref, mine_ref, other_ref, inv_ref, mat):
    mine, other = mine_ref[...], other_ref[...]
    mat[...] = jnp.where(side_ref[level] == 1, other - mine, mine - other)
    (inv_ref[...],) = invert([mat])


def both_sides(level, side_ref, mine_ref, other_ref):
    on_left = side_ref[level] == 1

    def pick(part):
        mine, other = mine_ref[part], other_ref[part]
        return jnp.where(on_left, mine, other), jnp.where(on_left, other, mine)

    diag_l, next_r = pick(0)
    link_l, link_r = pick(1)
    return link_l, link_r, diag_l, next_r, side_ref[level + 1] == 1


def crit_kernel(level, side_ref, inv_ref, mine_ref, other_ref, first_ref, crit_ref):
    first_ref[...], crit_ref[...] = urgent(
        inv_ref[...], *both_sides(level, side_ref, mine_ref, other_ref)
    )


def rest_kernel(level, side_ref, inv_ref, first_ref, mine_ref, other_ref, rest_ref, prop_ref):
    others(
        inv_ref[...], first_ref[...], *both_sides(level, side_ref, mine_ref, other_ref), rest_ref, prop_ref
    )


def root_kernel(
    side_ref, inv_ref, mine_ref, other_ref, prop_a_ref, prop_b_ref, prop_c_ref, mine_out, partner_out, mat
):
    on_left = side_ref[3] == 1
    diag_l = jnp.where(on_left, mine_ref[0], other_ref[0])
    link_l = jnp.where(on_left, mine_ref[1], other_ref[1])
    prop = cmul(inv_ref[...], ctrans(link_l))
    mat[...] = diag_l - cmul(link_l, prop)
    (root,) = invert([mat])
    middle = cmul(prop, root)
    x_left = jnp.where(on_left, root, middle)
    x_right = jnp.where(on_left, middle, 0.0)
    for level, ref in ((2, prop_c_ref), (1, prop_b_ref)):
        inside = cmul(ref[0], x_left) + cmul(ref[1], x_right)
        goes = side_ref[level] == 1
        x_left, x_right = jnp.where(goes, x_left, inside), jnp.where(goes, inside, x_right)
    inside = cmul(prop_a_ref[0], x_left) + cmul(prop_a_ref[1], x_right)
    mine_out[0] = x_left
    mine_out[1] = inside
    partner_out[0] = inside
    partner_out[1] = x_right


def density_kernel(side_ref, weight_ref, mine_ref, got_ref, prop_ref, left_ref, density_ref):
    own = side_ref[0] == 1
    x_left = jnp.where(own, mine_ref[0], got_ref[0])
    x_right = jnp.where(own, mine_ref[1], got_ref[1])
    x_2 = cmul(prop_ref[2], x_left) + cmul(prop_ref[3], x_right)
    x_1 = cmul(prop_ref[0], x_left) + cmul(prop_ref[1], x_2)
    x_3 = cmul(prop_ref[4], x_2) + cmul(prop_ref[5], x_right)
    imag = left_ref[1]
    gamma = -(imag + imag.T)
    weight = weight_ref[0]
    for s, x in enumerate((x_left, x_1, x_2, x_3)):
        stacked = jnp.concatenate([x[:, :W], x[:, W:]], 0)
        terms = mul3(stacked, gamma) * stacked
        both = terms[:W] + terms[W:]
        row = weight * jnp.sum(both.T, axis=0, keepdims=True)
        density_ref[:, s, :] = jnp.broadcast_to(row, (density_ref.shape[0], W))


def moments_kernel(parts_ref, current_ref, past_ref, total_ref, sums_ref):
    total = jnp.sum(parts_ref[...], axis=0)
    total_ref[...] = total
    residual = total - current_ref[...]
    count = past_ref.shape[0]
    diffs = [residual - past_ref[k] for k in range(count)]
    rows = []
    for k in range(count):
        for other in diffs[k:] + [residual]:
            rows.append(jnp.sum(diffs[k] * other, axis=0, keepdims=True))
    rows.append(jnp.zeros((W - len(rows), W), F32))
    sums = jnp.sum(jnp.concatenate(rows, 0).T, axis=0, keepdims=True)
    sums_ref[...] = jnp.broadcast_to(sums, sums_ref.shape)


def mix_kernel(sums_ref, total_ref, current_ref, density_ref, past_ref, next_ref):
    count = past_ref.shape[0]
    sums = jnp.sum(sums_ref[...], axis=0)[0:1]
    gram = {}
    place = 0
    for k in range(count):
        for other in range(k, count + 1):
            entry = jnp.broadcast_to(sums[:, place : place + 1], (1, W))
            gram[k, other] = entry
            if other < count:
                gram[other, k] = entry
            place += 1
    trace = gram[0, 0]
    for k in range(1, count):
        trace = trace + gram[k, k]
    ridge = RIDGE * trace / count
    for k in range(count):
        gram[k, k] = gram[k, k] + ridge
    for k in range(count):
        pivot = 1.0 / gram[k, k]
        for col in range(k + 1, count + 1):
            gram[k, col] = gram[k, col] * pivot
        for row in range(k + 1, count):
            for col in range(k + 1, count + 1):
                gram[row, col] = gram[row, col] - gram[row, k] * gram[k, col]
    mix = [None] * count
    for k in reversed(range(count)):
        value = gram[k, count]
        for col in range(k + 1, count):
            value = value - gram[k, col] * mix[col]
        mix[k] = value
    current = current_ref[...]
    residual = total_ref[...] - current
    out = current + MIX_BETA * residual
    for k in range(count):
        step = (current - density_ref[k]) + MIX_BETA * (residual - past_ref[k])
        out = out - mix[k] * step
    next_ref[...] = out


SMEM = pl.BlockSpec(memory_space=pltpu.SMEM)
VMEM = pl.BlockSpec(memory_space=pltpu.VMEM)
ANY = pl.BlockSpec(memory_space=pltpu.MemorySpace.HBM)
BLOCK = (W, 2 * W)
MAT = pltpu.VMEM(BLOCK, F32)


def call(kernel, name, shapes, in_specs, scratch=(), micros=2):
    return pl.pallas_call(
        kernel,
        out_shape=[jax.ShapeDtypeStruct(s, F32) for s in shapes],
        in_specs=in_specs,
        out_specs=[VMEM] * len(shapes),
        scratch_shapes=list(scratch),
        compiler_params=pltpu.CompilerParams(vmem_limit_bytes=32 << 20),
        name=name,
        cost_estimate=pl.CostEstimate(
            flops=micros * 1000000000, transcendentals=0, bytes_accessed=micros * 3000000
        ),
        interpret=INTERPRET,
    )


GRID = 512
MIX_BETA = 0.3
RIDGE = 0.01


def in_hbm(array):
    return pltpu.with_memory_space_constraint(array, pltpu.MemorySpace.HBM)


def send(block, route):
    return lax.ppermute(block, "slab", route)


def on_device(onsite, coupling, potential, sigma_left, sigma_right, energy_index, density_in, hist_density, hist_residual):
    slab_count = lax.axis_size("slab")
    position = lax.axis_index("slab")
    per_dev = onsite.shape[0]
    energies_all = energy_index.shape[0] * lax.axis_size("energy")
    energy = -0.4 + 0.8 * (energy_index.astype(F32) + 0.5) / GRID
    weight = 4.0 / energies_all / (1.0 + jnp.exp(energy / 0.1))
    broaden = jnp.full((1,), 2.0 / (per_dev * slab_count), F32)
    ends = jnp.stack([position == 0, position == slab_count - 1]).astype(jnp.int32)
    sides = jnp.stack([(position // (1 << level)) % 2 == 0 for level in range(4)]).astype(jnp.int32)
    left, right = sigma_left[0], sigma_right[0]
    pair = (2,) + BLOCK
    part, local = call(
        local_kernel, "local", [(3,) + BLOCK, (6,) + BLOCK],
        [SMEM, SMEM, ANY, ANY, VMEM, ANY, ANY],
        [
            pltpu.VMEM((per_dev, W, W), F32), pltpu.VMEM((per_dev, W, W), F32),
            pltpu.VMEM((2, W, W), F32), pltpu.VMEM((2, W, W), F32), MAT, MAT,
            pltpu.SemaphoreType.DMA((10,)),
        ],
    )(ends, jnp.concatenate([energy, broaden]), in_hbm(onsite), in_hbm(coupling), potential, in_hbm(left), in_hbm(right))
    evens = range(0, slab_count, 2)
    other = send(part, [(i + 1, i) for i in evens])
    inv, first, crit = call(chip_kernel, "chip", [BLOCK] * 3, [SMEM] + [VMEM] * 2, [MAT])(
        sides, part, other
    )
    route = [(i, i ^ 2) for i in evens]
    crit_other = send(crit, route)
    rest, prop = call(chip_rest_kernel, "chip_rest", [pair, pair], [SMEM] + [VMEM] * 4)(
        sides, inv, first, part, other
    )
    last = slab_count - 2
    props = [prop]
    for level in (1, 2):
        rest_other = send(rest, route)
        (inv,) = call(
            functools.partial(inverse_kernel, level), f"inverse{level}", [BLOCK], [SMEM, VMEM, VMEM], [MAT], 7
        )(sides, crit, crit_other)
        first, crit = call(
            functools.partial(crit_kernel, level), f"crit{level}", [BLOCK, BLOCK], [SMEM] + [VMEM] * 3
        )(sides, inv, rest, rest_other)
        route = [(i, i ^ 4) for i in evens] if level == 1 else [(i, last - i) for i in evens]
        crit_other = send(crit, route)
        rest, prop = call(
            functools.partial(rest_kernel, level), f"rest{level}", [pair, pair], [SMEM] + [VMEM] * 4
        )(sides, inv, first, rest, rest_other)
        props.append(prop)
    rest_other = send(rest, [(i, last - i) for i in evens if i < last - i])
    (inv,) = call(
        functools.partial(inverse_kernel, 3), "inverse3", [BLOCK], [SMEM, VMEM, VMEM], [MAT], 7
    )(sides, crit, crit_other)
    mine, partner = call(root_kernel, "root", [pair, pair], [SMEM] + [VMEM] * 6, [MAT])(
        sides, inv, rest, rest_other, *props
    )
    got = send(partner, [(i, i + 1) for i in evens])
    (density,) = call(density_kernel, "density", [(lax.axis_size("energy"), per_dev, W)], [SMEM, SMEM] + [VMEM] * 4)(
        sides, weight, mine, got, local, left
    )
    density = lax.all_to_all(density, "energy", 0, 0)
    total, sums = call(
        moments_kernel, "moments", [(per_dev, W), (slab_count, 8, W)], [VMEM] * 3
    )(density, density_in, hist_residual)
    sums = lax.all_to_all(sums, "slab", 0, 0)
    (following,) = call(mix_kernel, "mix", [(per_dev, W)], [VMEM] * 5)(
        sums, total, density_in, hist_density, hist_residual
    )
    return (total, following)


def solution(mesh):
    in_specs = (
        P("slab", None, None),
        P("slab", None, None),
        P("slab", None),
        P("energy", None, None, None),
        P("energy", None, None, None),
        P("energy"),
        P("slab", None),
        P(None, "slab", None),
        P(None, "slab", None),
    )
    out_specs = (P("slab", None), P("slab", None))
    return jax.shard_map(
        on_device, mesh=mesh, in_specs=in_specs, out_specs=out_specs, check_vma=False
    )
```

```python
import functools

import jax
import jax.numpy as jnp
from jax import lax
from jax.experimental import pallas as pl
from jax.experimental.pallas import tpu as pltpu
from jax.sharding import PartitionSpec as P

INTERPRET = False
W = 128
PB = 16
SUB = 8
ORDER = ((0, 0), (0, 1), (1, 0), (0, 2), (2, 0), (1, 1))
F32 = jnp.float32
BF16 = jnp.bfloat16


def dot(a, b):
    return jnp.dot(a, b, preferred_element_type=F32)


def dot_tn(a, b):
    return lax.dot_general(a, b, (((0,), (0,)), ((), ())), preferred_element_type=F32)


def split2(x):
    hi = x.astype(BF16)
    return hi, (x - hi.astype(F32)).astype(BF16)


def split3(x):
    hi = x.astype(BF16)
    rest = x - hi.astype(F32)
    mid = rest.astype(BF16)
    return hi, mid, (rest - mid.astype(F32)).astype(BF16)


def mul3(left, right):
    return split_product(split2(left), split2(right))


def split_product(left, right):
    lh, ll = left
    rh, rl = right
    rows = lh.shape[0]
    both = dot(jnp.concatenate([lh, ll], 0), rh)
    return both[:rows] + (both[rows:] + dot(lh, rl))


def as_right(x):
    return jnp.concatenate([x, jnp.concatenate([-x[:, W:], x[:, :W]], 1)], 0)


def cmul(left, right):
    rh, rl = split2(right)
    return split_product(split2(left), (as_right(rh), as_right(rl)))


def ctrans(x):
    return jnp.concatenate([x[:, :W].T, x[:, W:].T], 1)


def sweep_panels(mats):
    lane = lax.broadcasted_iota(jnp.int32, (8, W), 1)
    row = lax.broadcasted_iota(jnp.int32, (8, W), 0)
    keep = lax.broadcasted_iota(jnp.int32, (W - PB, W), 1) < W - PB
    halves = PB // 8

    def spread(parts, j):
        return [
            jnp.broadcast_to(jnp.sum(jnp.where(lane == j, p, 0.0), axis=1, keepdims=True), (8, W))
            for p in parts
        ]

    def eliminate(cols_r, cols_i, k, active):
        gk, rk = divmod(k, 8)
        here = row == rk
        mult_r, mult_i = cols_r[k], cols_i[k]
        piv_r = jnp.broadcast_to(mult_r[gk][rk : rk + 1], (8, W))
        piv_i = jnp.broadcast_to(mult_i[gk][rk : rk + 1], (8, W))
        den = 1.0 / (piv_r * piv_r + piv_i * piv_i)
        inv_r = piv_r * den
        inv_i = -piv_i * den
        fr, fi = [], []
        for g in range(halves):
            a = mult_r[g] * inv_r - mult_i[g] * inv_i
            b = mult_r[g] * inv_i + mult_i[g] * inv_r
            if g == gk:
                a = jnp.where(here, -inv_r, a)
                b = jnp.where(here, -inv_i, b)
            fr.append(a)
            fi.append(b)
        at = lane == W - PB + k
        for j in active:
            xr, xi = cols_r[j], cols_i[j]
            row_r = jnp.broadcast_to(xr[gk][rk : rk + 1], (8, W))
            row_i = jnp.broadcast_to(xi[gk][rk : rk + 1], (8, W))
            new_r, new_i = [], []
            for g in range(halves):
                br, bi = xr[g], xi[g]
                if g == gk:
                    br = jnp.where(here, 0.0, br)
                    bi = jnp.where(here, 0.0, bi)
                nr = br - (fr[g] * row_r - fi[g] * row_i)
                ni = bi - (fr[g] * row_i + fi[g] * row_r)
                if j == "w":
                    nr, ni = jnp.where(at, fr[g], nr), jnp.where(at, fi[g], ni)
                new_r.append(nr)
                new_i.append(ni)
            cols_r[j], cols_i[j] = new_r, new_i

    def panel(_, carry):
        state = []
        for ref in mats:
            pr = [ref[8 * g : 8 * g + 8, :W] for g in range(halves)]
            pi = [ref[8 * g : 8 * g + 8, W:] for g in range(halves)]
            cols_r = {j: spread(pr, j) for j in range(SUB)}
            cols_i = {j: spread(pi, j) for j in range(SUB)}
            cols_r["w"] = [pltpu.roll(p, W - PB, 1) for p in pr]
            cols_i["w"] = [pltpu.roll(p, W - PB, 1) for p in pi]
            own_r = []
            own_i = []
            for g in range(halves):
                unit = jnp.where(lane == W - PB + row + 8 * g, -1.0, 0.0)
                own_r.append(jnp.where(lane < W - PB, cols_r["w"][g], unit))
                own_i.append(jnp.where(lane < W - PB, cols_i["w"][g], 0.0))
            state.append((cols_r, cols_i, own_r, own_i))
        for base in range(0, PB, SUB):
            if base:
                for cols_r, cols_i, _, _ in state:
                    for j in range(base, base + SUB):
                        cols_r[j] = spread(cols_r["w"], W - PB + j)
                        cols_i[j] = spread(cols_i["w"], W - PB + j)
            for k in range(base, base + SUB):
                active = list(range(k + 1, base + SUB)) + ["w"]
                for cols_r, cols_i, _, _ in state:
                    eliminate(cols_r, cols_i, k, active)
        for ref, (cols_r, cols_i, own_r, own_i) in zip(mats, state):
            pieces_p = split3(jnp.concatenate(own_r + own_i, 0))
            wr = jnp.concatenate(cols_r["w"], 0)
            wi = jnp.concatenate(cols_i["w"], 0)
            pieces_w = [
                jnp.concatenate([jnp.concatenate([r, i], 1), jnp.concatenate([-i, r], 1)], 0)
                for r, i in zip(split3(wr), split3(wi))
            ]
            lhs = jnp.concatenate([pieces_p[a] for a, _ in ORDER], 0)
            rhs = jnp.concatenate([pieces_w[b] for _, b in ORDER], 0)
            update = dot_tn(lhs, rhs)
            old_r = jnp.where(keep, pltpu.roll(ref[PB:, :W], W - PB, 1), 0.0)
            old_i = jnp.where(keep, pltpu.roll(ref[PB:, W:], W - PB, 1), 0.0)
            ref[: W - PB, :W] = old_r - update[: W - PB, :W]
            ref[: W - PB, W:] = old_i - update[: W - PB, W:]
            ref[W - PB :, :] = -update[W - PB :, :]
        return carry

    lax.fori_loop(0, W // PB, panel, 0)


def invert(refs):
    sweep_panels(refs)
    return [-ref[...] for ref in refs]


def triangles():
    row = lax.broadcasted_iota(jnp.int32, (W, W), 0)
    col = lax.broadcasted_iota(jnp.int32, (W, W), 1)
    return row, col


def pack(x):
    row, col = triangles()
    real, imag = x[:, :W], x[:, W:]
    tip = jnp.sum(jnp.where(row == col, imag, 0.0), axis=0, keepdims=True)
    return jnp.concatenate([jnp.where(row <= col, real, imag), jnp.broadcast_to(tip, (8, W))], 0)


def unpack(packed):
    row, col = triangles()
    body = packed[:W]
    turned = body.T
    imag = jnp.where(row == col, packed[W : W + 1], turned)
    return jnp.concatenate(
        [jnp.where(row <= col, body, turned), jnp.where(row > col, body, imag)], 1
    )


def tall(x):
    return jnp.concatenate([x[:, :W], x[:, W:]], 0)


def wide(x):
    return jnp.concatenate([x[:W], x[W:]], 1)


def real_right(inv, real):
    out = mul3(jnp.concatenate([inv[:, :W], inv[:, W:]], 0), real)
    return jnp.concatenate([out[:W], out[W:]], 1)


def local_kernel(
    flag_ref, energy_ref, onsite_hbm, coupling_hbm, potential_hbm, left_hbm, right_hbm,
    part_ref, prop_ref,
    onsite_ref, coupling_ref, potential_ref, left_ref, right_ref, mat_a, mat_b, sems,
):
    is_first = flag_ref[0] == 1
    is_last = flag_ref[1] == 1
    energy = energy_ref[0]
    copies = []

    def fetch(src, dst):
        copy = pltpu.make_async_copy(src, dst, sems.at[len(copies)])
        copy.start()
        copies.append(copy)
        return copy

    potential_copy = fetch(potential_hbm, potential_ref)
    onsite_copy = {s: fetch(onsite_hbm.at[s], onsite_ref.at[s]) for s in (1, 3)}
    right_copy = fetch(right_hbm, right_ref)
    coupling_copy = [fetch(coupling_hbm.at[s], coupling_ref.at[s]) for s in range(4)]
    onsite_copy.update({s: fetch(onsite_hbm.at[s], onsite_ref.at[s]) for s in (2, 0)})
    left_copy = fetch(left_hbm, left_ref)
    eye = lax.broadcasted_iota(jnp.int32, (W, W), 0) == lax.broadcasted_iota(jnp.int32, (W, W), 1)
    broaden = jnp.where(eye, energy_ref[1], 0.0)

    def diagonal(s):
        onsite_copy[s].wait()
        real = jnp.where(eye, energy - potential_ref[s : s + 1, :], 0.0) - onsite_ref[s]
        return jnp.concatenate([real, broaden], 1)

    potential_copy.wait()
    mat_a[...] = diagonal(1)
    diag_3 = diagonal(3)
    right_copy.wait()
    last = jnp.concatenate([right_ref[0], right_ref[1]], 1)
    mat_b[...] = diag_3 - jnp.where(is_last, last, 0.0)
    inv_1, inv_3 = invert([mat_a, mat_b])
    for copy in coupling_copy:
        copy.wait()
    c0, c1, c2 = coupling_ref[0], coupling_ref[1], coupling_ref[2]
    c3 = jnp.where(is_last, 0.0, coupling_ref[3])
    prop_1r = real_right(inv_1, c1)
    prop_3l = real_right(inv_3, c2.T)
    mat_a[...] = diagonal(2) - mul3(c1.T, prop_1r) - mul3(c2, prop_3l)
    (inv_2,) = invert([mat_a])
    prop_1l = real_right(inv_1, c0.T)
    prop_3r = real_right(inv_3, c3)
    diag_0 = diagonal(0)
    left_copy.wait()
    first = jnp.concatenate([left_ref[0], left_ref[1]], 1)
    top = diag_0 - jnp.where(is_first, first, 0.0) - mul3(c0, prop_1l)
    k02 = mul3(c0, prop_1r)
    k2n = mul3(c2, prop_3r)
    prop_2l = cmul(inv_2, ctrans(k02))
    prop_2r = cmul(inv_2, k2n)
    part_ref[:PACKED] = pack(top - cmul(k02, prop_2l))
    part_ref[PACKED : 2 * PACKED] = pack(mul3(c3.T, prop_3r) + cmul(ctrans(k2n), prop_2r))
    part_ref[2 * PACKED :] = tall(cmul(k02, prop_2r))
    for n, prop in enumerate((prop_1l, prop_1r, prop_2l, prop_2r, prop_3l, prop_3r)):
        prop_ref[n] = prop


def urgent(inv, link_l, link_r, base, goes_left):
    side = jnp.where(goes_left, link_r, ctrans(link_l))
    prop = cmul(inv, side)
    change = cmul(ctrans(side), prop)
    return prop, pack(unpack(base) + jnp.where(goes_left, change, -change))


def others(inv, prop, link_l, link_r, base, goes_left, rest_ref, prop_ref):
    side = jnp.where(goes_left, ctrans(link_l), link_r)
    second = cmul(inv, side)
    change = cmul(ctrans(side), second)
    prop_r = jnp.where(goes_left, prop, second)
    rest_ref[:PACKED] = pack(unpack(base) + jnp.where(goes_left, -change, change))
    rest_ref[PACKED:] = tall(cmul(link_l, prop_r))
    prop_ref[0] = jnp.where(goes_left, second, prop)
    prop_ref[1] = prop_r


def chip_sides(side_ref, mine_ref, other_ref):
    goes_left = side_ref[1] == 1
    diag_l = mine_ref[:PACKED]
    next_r = other_ref[PACKED : 2 * PACKED]
    links = wide(mine_ref[2 * PACKED :]), wide(other_ref[2 * PACKED :])
    return links, (diag_l, next_r), goes_left


def chip_kernel(side_ref, mine_ref, other_ref, inv_ref, first_ref, crit_ref, mat):
    mat[...] = unpack(other_ref[:PACKED] - mine_ref[PACKED : 2 * PACKED])
    (inv,) = invert([mat])
    inv_ref[...] = inv
    links, (diag_l, next_r), goes_left = chip_sides(side_ref, mine_ref, other_ref)
    first_ref[...], crit_ref[...] = urgent(inv, *links, jnp.where(goes_left, next_r, diag_l), goes_left)


def chip_rest_kernel(side_ref, inv_ref, first_ref, mine_ref, other_ref, rest_ref, prop_ref):
    links, (diag_l, next_r), goes_left = chip_sides(side_ref, mine_ref, other_ref)
    others(
        inv_ref[...], first_ref[...], *links, jnp.where(goes_left, diag_l, next_r), goes_left,
        rest_ref, prop_ref,
    )


def inverse_kernel(level, side_ref, mine_ref, other_ref, inv_ref, mat):
    mine, other = mine_ref[...], other_ref[...]
    mat[...] = unpack(jnp.where(side_ref[level] == 1, other - mine, mine - other))
    (inv_ref[...],) = invert([mat])


def both_sides(level, side_ref, mine_ref, other_ref):
    on_left = side_ref[level] == 1
    mine, other = mine_ref[...], other_ref[...]
    left, right = jnp.where(on_left, mine, other), jnp.where(on_left, other, mine)
    links = wide(left[PACKED:]), wide(right[PACKED:])
    return links, (left[:PACKED], right[:PACKED]), side_ref[level + 1] == 1


def crit_kernel(level, side_ref, inv_ref, mine_ref, other_ref, first_ref, crit_ref):
    links, (diag_l, next_r), goes_left = both_sides(level, side_ref, mine_ref, other_ref)
    first_ref[...], crit_ref[...] = urgent(
        inv_ref[...], *links, jnp.where(goes_left, next_r, diag_l), goes_left
    )


def rest_kernel(level, side_ref, inv_ref, first_ref, mine_ref, other_ref, rest_ref, prop_ref):
    links, (diag_l, next_r), goes_left = both_sides(level, side_ref, mine_ref, other_ref)
    others(
        inv_ref[...], first_ref[...], *links, jnp.where(goes_left, diag_l, next_r), goes_left,
        rest_ref, prop_ref,
    )


def root_kernel(
    side_ref, inv_ref, mine_ref, other_ref, prop_a_ref, prop_b_ref, prop_c_ref, mine_out, partner_out, mat
):
    on_left = side_ref[3] == 1
    lower = jnp.where(on_left, mine_ref[...], other_ref[...])
    diag_l = unpack(lower[:PACKED])
    link_l = wide(lower[PACKED:])
    prop = cmul(inv_ref[...], ctrans(link_l))
    mat[...] = diag_l - cmul(link_l, prop)
    (root,) = invert([mat])
    middle = cmul(prop, root)
    x_left = jnp.where(on_left, root, middle)
    x_right = jnp.where(on_left, middle, 0.0)
    for level, ref in ((2, prop_c_ref), (1, prop_b_ref)):
        inside = cmul(ref[0], x_left) + cmul(ref[1], x_right)
        goes = side_ref[level] == 1
        x_left, x_right = jnp.where(goes, x_left, inside), jnp.where(goes, inside, x_right)
    inside = cmul(prop_a_ref[0], x_left) + cmul(prop_a_ref[1], x_right)
    mine_out[0] = x_left
    mine_out[1] = inside
    partner_out[0] = inside
    partner_out[1] = x_right


def density_kernel(side_ref, weight_ref, mine_ref, got_ref, prop_ref, left_ref, density_ref):
    own = side_ref[0] == 1
    x_left = jnp.where(own, mine_ref[0], got_ref[0])
    x_right = jnp.where(own, mine_ref[1], got_ref[1])
    x_2 = cmul(prop_ref[2], x_left) + cmul(prop_ref[3], x_right)
    x_1 = cmul(prop_ref[0], x_left) + cmul(prop_ref[1], x_2)
    x_3 = cmul(prop_ref[4], x_2) + cmul(prop_ref[5], x_right)
    imag = left_ref[1]
    gamma = -(imag + imag.T)
    weight = weight_ref[0]
    stacked = jnp.concatenate([tall(x) for x in (x_left, x_1, x_2, x_3)], 0)
    terms = mul3(stacked, gamma) * stacked
    for s in range(density_ref.shape[1]):
        both = terms[2 * s * W : (2 * s + 1) * W] + terms[(2 * s + 1) * W : (2 * s + 2) * W]
        row = weight * jnp.sum(both.T, axis=0, keepdims=True)
        density_ref[:, s, :] = jnp.broadcast_to(row, (density_ref.shape[0], W))


def moments_kernel(parts_ref, current_ref, past_ref, total_ref, sums_ref):
    total = jnp.sum(parts_ref[...], axis=0)
    total_ref[...] = total
    residual = total - current_ref[...]
    count = past_ref.shape[0]
    diffs = [residual - past_ref[k] for k in range(count)]
    rows = []
    for k in range(count):
        for other in diffs[k:] + [residual]:
            rows.append(jnp.sum(diffs[k] * other, axis=0, keepdims=True))
    rows.append(jnp.zeros((W - len(rows), W), F32))
    sums = jnp.sum(jnp.concatenate(rows, 0).T, axis=0, keepdims=True)
    sums_ref[...] = jnp.broadcast_to(sums, sums_ref.shape)


def mix_kernel(sums_ref, total_ref, current_ref, density_ref, past_ref, next_ref):
    count = past_ref.shape[0]
    sums = jnp.sum(sums_ref[...], axis=0)[0:1]
    gram = {}
    place = 0
    for k in range(count):
        for other in range(k, count + 1):
            entry = jnp.broadcast_to(sums[:, place : place + 1], (1, W))
            gram[k, other] = entry
            if other < count:
                gram[other, k] = entry
            place += 1
    trace = gram[0, 0]
    for k in range(1, count):
        trace = trace + gram[k, k]
    ridge = RIDGE * trace / count
    for k in range(count):
        gram[k, k] = gram[k, k] + ridge
    for k in range(count):
        pivot = 1.0 / gram[k, k]
        for col in range(k + 1, count + 1):
            gram[k, col] = gram[k, col] * pivot
        for row in range(k + 1, count):
            for col in range(k + 1, count + 1):
                gram[row, col] = gram[row, col] - gram[row, k] * gram[k, col]
    mix = [None] * count
    for k in reversed(range(count)):
        value = gram[k, count]
        for col in range(k + 1, count):
            value = value - gram[k, col] * mix[col]
        mix[k] = value
    current = current_ref[...]
    residual = total_ref[...] - current
    out = current + MIX_BETA * residual
    for k in range(count):
        step = (current - density_ref[k]) + MIX_BETA * (residual - past_ref[k])
        out = out - mix[k] * step
    next_ref[...] = out


SMEM = pl.BlockSpec(memory_space=pltpu.SMEM)
VMEM = pl.BlockSpec(memory_space=pltpu.VMEM)
ANY = pl.BlockSpec(memory_space=pltpu.MemorySpace.HBM)
BLOCK = (W, 2 * W)
MAT = pltpu.VMEM(BLOCK, F32)
PACKED = W + 8
CRIT = (PACKED, W)
REST = (PACKED + 2 * W, W)
PART = (2 * PACKED + 2 * W, W)


def call(kernel, name, shapes, in_specs, scratch=(), micros=2):
    return pl.pallas_call(
        kernel,
        out_shape=[jax.ShapeDtypeStruct(s, F32) for s in shapes],
        in_specs=in_specs,
        out_specs=[VMEM] * len(shapes),
        scratch_shapes=list(scratch),
        compiler_params=pltpu.CompilerParams(vmem_limit_bytes=32 << 20),
        name=name,
        cost_estimate=pl.CostEstimate(
            flops=micros * 1000000000, transcendentals=0, bytes_accessed=micros * 3000000
        ),
        interpret=INTERPRET,
    )


GRID = 512
MIX_BETA = 0.3
RIDGE = 0.01


def in_hbm(array):
    return pltpu.with_memory_space_constraint(array, pltpu.MemorySpace.HBM)


def send(block, route):
    return lax.ppermute(block, "slab", route)


def on_device(onsite, coupling, potential, sigma_left, sigma_right, energy_index, density_in, hist_density, hist_residual):
    slab_count = lax.axis_size("slab")
    position = lax.axis_index("slab")
    per_dev = onsite.shape[0]
    energies_all = energy_index.shape[0] * lax.axis_size("energy")
    energy = -0.4 + 0.8 * (energy_index.astype(F32) + 0.5) / GRID
    weight = 4.0 / energies_all / (1.0 + jnp.exp(energy / 0.1))
    broaden = jnp.full((1,), 2.0 / (per_dev * slab_count), F32)
    ends = jnp.stack([position == 0, position == slab_count - 1]).astype(jnp.int32)
    sides = jnp.stack([(position // (1 << level)) % 2 == 0 for level in range(4)]).astype(jnp.int32)
    left, right = sigma_left[0], sigma_right[0]
    pair = (2,) + BLOCK
    part, local = call(
        local_kernel, "local", [PART, (6,) + BLOCK],
        [SMEM, SMEM, ANY, ANY, ANY, ANY, ANY],
        [
            pltpu.VMEM((per_dev, W, W), F32), pltpu.VMEM((per_dev, W, W), F32), pltpu.VMEM((per_dev, W), F32),
            pltpu.VMEM((2, W, W), F32), pltpu.VMEM((2, W, W), F32), MAT, MAT,
            pltpu.SemaphoreType.DMA((11,)),
        ],
    )(ends, jnp.concatenate([energy, broaden]), in_hbm(onsite), in_hbm(coupling), in_hbm(potential), in_hbm(left), in_hbm(right))
    evens = range(0, slab_count, 2)
    other = send(part, [(i + 1, i) for i in evens])
    inv, first, crit = call(chip_kernel, "chip", [BLOCK, BLOCK, CRIT], [SMEM] + [VMEM] * 2, [MAT])(
        sides, part, other
    )
    route = [(i, i ^ 2) for i in evens]
    crit_other = send(crit, route)
    rest, prop = call(chip_rest_kernel, "chip_rest", [REST, pair], [SMEM] + [VMEM] * 4)(
        sides, inv, first, part, other
    )
    last = slab_count - 2
    props = [prop]
    for level in (1, 2):
        rest_other = send(rest, route)
        (inv,) = call(
            functools.partial(inverse_kernel, level), f"inverse{level}", [BLOCK], [SMEM, VMEM, VMEM], [MAT], 7
        )(sides, crit, crit_other)
        first, crit = call(
            functools.partial(crit_kernel, level), f"crit{level}", [BLOCK, CRIT], [SMEM] + [VMEM] * 3
        )(sides, inv, rest, rest_other)
        route = [(i, i ^ 4) for i in evens] if level == 1 else [(i, last - i) for i in evens]
        crit_other = send(crit, route)
        rest, prop = call(
            functools.partial(rest_kernel, level), f"rest{level}", [REST, pair], [SMEM] + [VMEM] * 4
        )(sides, inv, first, rest, rest_other)
        props.append(prop)
    rest_other = send(rest, [(i, last - i) for i in evens if i < last - i])
    (inv,) = call(
        functools.partial(inverse_kernel, 3), "inverse3", [BLOCK], [SMEM, VMEM, VMEM], [MAT], 7
    )(sides, crit, crit_other)
    mine, partner = call(root_kernel, "root", [pair, pair], [SMEM] + [VMEM] * 6, [MAT])(
        sides, inv, rest, rest_other, *props
    )
    got = send(partner, [(i, i + 1) for i in evens])
    (density,) = call(density_kernel, "density", [(lax.axis_size("energy"), per_dev, W)], [SMEM, SMEM] + [VMEM] * 4)(
        sides, weight, mine, got, local, left
    )
    density = lax.all_to_all(density, "energy", 0, 0)
    total, sums = call(
        moments_kernel, "moments", [(per_dev, W), (slab_count, 8, W)], [VMEM] * 3
    )(density, density_in, hist_residual)
    sums = lax.all_to_all(sums, "slab", 0, 0)
    (following,) = call(mix_kernel, "mix", [(per_dev, W)], [VMEM] * 5)(
        sums, total, density_in, hist_density, hist_residual
    )
    return (total, following)


def solution(mesh):
    in_specs = (
        P("slab", None, None),
        P("slab", None, None),
        P("slab", None),
        P("energy", None, None, None),
        P("energy", None, None, None),
        P("energy"),
        P("slab", None),
        P(None, "slab", None),
        P(None, "slab", None),
    )
    out_specs = (P("slab", None), P("slab", None))
    return jax.shard_map(
        on_device, mesh=mesh, in_specs=in_specs, out_specs=out_specs, check_vma=False
    )
```

```python
import functools

import jax
import jax.numpy as jnp
from jax import lax
from jax.experimental import pallas as pl
from jax.experimental.pallas import tpu as pltpu
from jax.sharding import PartitionSpec as P

INTERPRET = False
W = 128
PB = 16
ORDER = ((0, 0), (0, 1), (1, 0), (0, 2), (2, 0), (1, 1))
F32 = jnp.float32
BF16 = jnp.bfloat16


def dot(a, b):
    return jnp.dot(a, b, preferred_element_type=F32)


def dot_tn(a, b):
    return lax.dot_general(a, b, (((0,), (0,)), ((), ())), preferred_element_type=F32)


def split2(x):
    hi = x.astype(BF16)
    return hi, (x - hi.astype(F32)).astype(BF16)


def split3(x):
    hi = x.astype(BF16)
    rest = x - hi.astype(F32)
    mid = rest.astype(BF16)
    return hi, mid, (rest - mid.astype(F32)).astype(BF16)


def mul3(left, right):
    return split_product(split2(left), split2(right))


def split_product(left, right):
    lh, ll = left
    rh, rl = right
    rows = lh.shape[0]
    both = dot(jnp.concatenate([lh, ll], 0), rh)
    return both[:rows] + (both[rows:] + dot(lh, rl))


def as_right(x):
    return jnp.concatenate([x, jnp.concatenate([-x[:, W:], x[:, :W]], 1)], 0)


def cmul(left, right):
    rh, rl = split2(right)
    return split_product(split2(left), (as_right(rh), as_right(rl)))


def ctrans(x):
    return jnp.concatenate([x[:, :W].T, x[:, W:].T], 1)


def sweep_panels(mats):
    lane = lax.broadcasted_iota(jnp.int32, (8, W), 1)
    row = lax.broadcasted_iota(jnp.int32, (8, W), 0)
    keep = lax.broadcasted_iota(jnp.int32, (W - PB, W), 1) < W - PB

    groups = PB // 8

    def spread(parts, j):
        return {
            g: jnp.broadcast_to(jnp.sum(jnp.where(lane == j, p, 0.0), axis=1, keepdims=True), (8, W))
            for g, p in parts.items()
        }

    def eliminate(cols_r, cols_i, k, active, live):
        gk, rk = divmod(k, 8)
        here = row == rk
        mult_r, mult_i = cols_r[k], cols_i[k]
        piv_r = jnp.broadcast_to(mult_r[gk][rk : rk + 1], (8, W))
        piv_i = jnp.broadcast_to(mult_i[gk][rk : rk + 1], (8, W))
        den = 1.0 / (piv_r * piv_r + piv_i * piv_i)
        inv_r = piv_r * den
        inv_i = -piv_i * den
        fr, fi = {}, {}
        for g in live:
            a = mult_r[g] * inv_r - mult_i[g] * inv_i
            b = mult_r[g] * inv_i + mult_i[g] * inv_r
            if g == gk:
                a = jnp.where(here, -inv_r, a)
                b = jnp.where(here, -inv_i, b)
            fr[g], fi[g] = a, b
        at = lane == W - PB + k
        for j in active:
            xr, xi = cols_r[j], cols_i[j]
            row_r = jnp.broadcast_to(xr[gk][rk : rk + 1], (8, W))
            row_i = jnp.broadcast_to(xi[gk][rk : rk + 1], (8, W))
            new_r, new_i = dict(xr), dict(xi)
            for g in live:
                br, bi = xr[g], xi[g]
                if g == gk:
                    br = jnp.where(here, 0.0, br)
                    bi = jnp.where(here, 0.0, bi)
                nr = br - (fr[g] * row_r - fi[g] * row_i)
                ni = bi - (fr[g] * row_i + fi[g] * row_r)
                if j == "w":
                    nr, ni = jnp.where(at, fr[g], nr), jnp.where(at, fi[g], ni)
                new_r[g], new_i[g] = nr, ni
            cols_r[j], cols_i[j] = new_r, new_i

    def panel(_, carry):
        state = []
        for ref in mats:
            pr = {g: ref[8 * g : 8 * g + 8, :W] for g in range(groups)}
            pi = {g: ref[8 * g : 8 * g + 8, W:] for g in range(groups)}
            cols_r = {j: spread(pr, j) for j in range(8)}
            cols_i = {j: spread(pi, j) for j in range(8)}
            cols_r["w"] = {g: pltpu.roll(p, W - PB, 1) for g, p in pr.items()}
            cols_i["w"] = {g: pltpu.roll(p, W - PB, 1) for g, p in pi.items()}
            state.append((cols_r, cols_i, [], []))
        for s in range(groups):
            edge = W - PB + 8 * s
            unit = jnp.where(lane == edge + row, -1.0, 0.0)
            for cols_r, cols_i, left_r, left_i in state:
                left_r.append(jnp.where(lane < edge, cols_r["w"][s], unit))
                left_i.append(jnp.where(lane < edge, cols_i["w"][s], 0.0))
                for cols in (cols_r, cols_i):
                    if s:
                        below = {g: cols["w"][g] for g in range(s, groups)}
                        for j in range(8 * s, 8 * s + 8):
                            cols[j] = spread(below, W - PB + j)
            for k in range(8 * s, 8 * s + 8):
                active = list(range(k + 1, 8 * s + 8)) + ["w"]
                for cols_r, cols_i, _, _ in state:
                    eliminate(cols_r, cols_i, k, active, range(s, groups))
            for cols_r, cols_i, _, _ in state:
                for cols in (cols_r, cols_i):
                    cols["w"][s] = jnp.where(lane < edge + 8, cols["w"][s], 0.0)
        for ref, (cols_r, cols_i, left_r, left_i) in zip(mats, state):
            pieces_p = split3(jnp.concatenate(left_r + left_i, 0))
            wr = jnp.concatenate([cols_r["w"][g] for g in range(groups)], 0)
            wi = jnp.concatenate([cols_i["w"][g] for g in range(groups)], 0)
            pieces_w = [
                jnp.concatenate([jnp.concatenate([r, i], 1), jnp.concatenate([-i, r], 1)], 0)
                for r, i in zip(split3(wr), split3(wi))
            ]
            lhs = jnp.concatenate([pieces_p[a] for a, _ in ORDER], 0)
            rhs = jnp.concatenate([pieces_w[b] for _, b in ORDER], 0)
            update = dot_tn(lhs, rhs)
            old_r = jnp.where(keep, pltpu.roll(ref[PB:, :W], W - PB, 1), 0.0)
            old_i = jnp.where(keep, pltpu.roll(ref[PB:, W:], W - PB, 1), 0.0)
            ref[: W - PB, :W] = old_r - update[: W - PB, :W]
            ref[: W - PB, W:] = old_i - update[: W - PB, W:]
            ref[W - PB :, :] = -update[W - PB :, :]
        return carry

    lax.fori_loop(0, W // PB, panel, 0)


def invert(refs):
    sweep_panels(refs)
    return [-ref[...] for ref in refs]


def triangles():
    row = lax.broadcasted_iota(jnp.int32, (W, W), 0)
    col = lax.broadcasted_iota(jnp.int32, (W, W), 1)
    return row, col


def pack(x):
    row, col = triangles()
    real, imag = x[:, :W], x[:, W:]
    tip = jnp.sum(jnp.where(row == col, imag, 0.0), axis=0, keepdims=True)
    return jnp.concatenate([jnp.where(row <= col, real, imag), jnp.broadcast_to(tip, (8, W))], 0)


def unpack(packed):
    row, col = triangles()
    body = packed[:W]
    turned = body.T
    imag = jnp.where(row == col, packed[W : W + 1], turned)
    return jnp.concatenate(
        [jnp.where(row <= col, body, turned), jnp.where(row > col, body, imag)], 1
    )


def tall(x):
    return jnp.concatenate([x[:, :W], x[:, W:]], 0)


def wide(x):
    return jnp.concatenate([x[:W], x[W:]], 1)


def real_right(inv, real):
    out = mul3(jnp.concatenate([inv[:, :W], inv[:, W:]], 0), real)
    return jnp.concatenate([out[:W], out[W:]], 1)


def local_kernel(
    flag_ref, energy_ref, onsite_hbm, coupling_hbm, potential_hbm, left_hbm, right_hbm,
    part_ref, prop_ref,
    onsite_ref, coupling_ref, potential_ref, left_ref, right_ref, mat_a, mat_b, sems,
):
    is_first = flag_ref[0] == 1
    is_last = flag_ref[1] == 1
    energy = energy_ref[0]
    copies = []

    def fetch(src, dst):
        copy = pltpu.make_async_copy(src, dst, sems.at[len(copies)])
        copy.start()
        copies.append(copy)
        return copy

    potential_copy = fetch(potential_hbm, potential_ref)
    onsite_copy = {s: fetch(onsite_hbm.at[s], onsite_ref.at[s]) for s in (1, 3)}
    right_copy = fetch(right_hbm, right_ref)
    coupling_copy = [fetch(coupling_hbm.at[s], coupling_ref.at[s]) for s in range(4)]
    onsite_copy.update({s: fetch(onsite_hbm.at[s], onsite_ref.at[s]) for s in (2, 0)})
    left_copy = fetch(left_hbm, left_ref)
    eye = lax.broadcasted_iota(jnp.int32, (W, W), 0) == lax.broadcasted_iota(jnp.int32, (W, W), 1)
    broaden = jnp.where(eye, energy_ref[1], 0.0)

    def diagonal(s):
        onsite_copy[s].wait()
        real = jnp.where(eye, energy - potential_ref[s : s + 1, :], 0.0) - onsite_ref[s]
        return jnp.concatenate([real, broaden], 1)

    potential_copy.wait()
    mat_a[...] = diagonal(1)
    diag_3 = diagonal(3)
    right_copy.wait()
    last = jnp.concatenate([right_ref[0], right_ref[1]], 1)
    mat_b[...] = diag_3 - jnp.where(is_last, last, 0.0)
    inv_1, inv_3 = invert([mat_a, mat_b])
    for copy in coupling_copy:
        copy.wait()
    c0, c1, c2 = coupling_ref[0], coupling_ref[1], coupling_ref[2]
    c3 = jnp.where(is_last, 0.0, coupling_ref[3])
    prop_1r = real_right(inv_1, c1)
    prop_3l = real_right(inv_3, c2.T)
    mat_a[...] = diagonal(2) - mul3(c1.T, prop_1r) - mul3(c2, prop_3l)
    (inv_2,) = invert([mat_a])
    prop_1l = real_right(inv_1, c0.T)
    prop_3r = real_right(inv_3, c3)
    diag_0 = diagonal(0)
    left_copy.wait()
    first = jnp.concatenate([left_ref[0], left_ref[1]], 1)
    top = diag_0 - jnp.where(is_first, first, 0.0) - mul3(c0, prop_1l)
    k02 = mul3(c0, prop_1r)
    k2n = mul3(c2, prop_3r)
    prop_2l = cmul(inv_2, ctrans(k02))
    prop_2r = cmul(inv_2, k2n)
    part_ref[:PACKED] = pack(top - cmul(k02, prop_2l))
    part_ref[PACKED : 2 * PACKED] = pack(mul3(c3.T, prop_3r) + cmul(ctrans(k2n), prop_2r))
    part_ref[2 * PACKED :] = tall(cmul(k02, prop_2r))
    for n, prop in enumerate((prop_1l, prop_1r, prop_2l, prop_2r, prop_3l, prop_3r)):
        prop_ref[n] = prop


def facing(link_l, link_r, to_right):
    plain = jnp.where(to_right, link_r, link_l)
    turned = ctrans(plain)
    return jnp.where(to_right, plain, turned), jnp.where(to_right, turned, plain)


def urgent(inv, link_l, link_r, base, goes_left):
    side, side_t = facing(link_l, link_r, goes_left)
    prop = cmul(inv, side)
    change = cmul(side_t, prop)
    return prop, pack(unpack(base) + jnp.where(goes_left, change, -change))


def others(inv, prop, link_l, link_r, base, goes_left, rest_ref, prop_ref):
    side, side_t = facing(link_l, link_r, jnp.logical_not(goes_left))
    second = cmul(inv, side)
    change = cmul(side_t, second)
    prop_r = jnp.where(goes_left, prop, second)
    rest_ref[:PACKED] = pack(unpack(base) + jnp.where(goes_left, -change, change))
    rest_ref[PACKED:] = tall(cmul(link_l, prop_r))
    prop_ref[0] = jnp.where(goes_left, second, prop)
    prop_ref[1] = prop_r


def chip_sides(side_ref, mine_ref, other_ref):
    goes_left = side_ref[1] == 1
    diag_l = mine_ref[:PACKED]
    next_r = other_ref[PACKED : 2 * PACKED]
    links = wide(mine_ref[2 * PACKED :]), wide(other_ref[2 * PACKED :])
    return links, (diag_l, next_r), goes_left


def chip_kernel(side_ref, mine_ref, other_ref, inv_ref, first_ref, crit_ref, mat):
    mat[...] = unpack(other_ref[:PACKED] - mine_ref[PACKED : 2 * PACKED])
    (inv,) = invert([mat])
    inv_ref[...] = inv
    links, (diag_l, next_r), goes_left = chip_sides(side_ref, mine_ref, other_ref)
    first_ref[...], crit_ref[...] = urgent(inv, *links, jnp.where(goes_left, next_r, diag_l), goes_left)


def chip_rest_kernel(side_ref, inv_ref, first_ref, mine_ref, other_ref, rest_ref, prop_ref):
    links, (diag_l, next_r), goes_left = chip_sides(side_ref, mine_ref, other_ref)
    others(
        inv_ref[...], first_ref[...], *links, jnp.where(goes_left, diag_l, next_r), goes_left,
        rest_ref, prop_ref,
    )


def inverse_kernel(level, side_ref, mine_ref, other_ref, inv_ref, mat):
    mine, other = mine_ref[...], other_ref[...]
    mat[...] = unpack(jnp.where(side_ref[level] == 1, other - mine, mine - other))
    (inv_ref[...],) = invert([mat])


def both_sides(level, side_ref, mine_ref, other_ref):
    on_left = side_ref[level] == 1
    mine, other = mine_ref[...], other_ref[...]
    left, right = jnp.where(on_left, mine, other), jnp.where(on_left, other, mine)
    links = wide(left[PACKED:]), wide(right[PACKED:])
    return links, (left[:PACKED], right[:PACKED]), side_ref[level + 1] == 1


def crit_kernel(level, side_ref, inv_ref, mine_ref, other_ref, first_ref, crit_ref):
    links, (diag_l, next_r), goes_left = both_sides(level, side_ref, mine_ref, other_ref)
    first_ref[...], crit_ref[...] = urgent(
        inv_ref[...], *links, jnp.where(goes_left, next_r, diag_l), goes_left
    )


def rest_kernel(level, side_ref, inv_ref, first_ref, mine_ref, other_ref, rest_ref, prop_ref):
    links, (diag_l, next_r), goes_left = both_sides(level, side_ref, mine_ref, other_ref)
    others(
        inv_ref[...], first_ref[...], *links, jnp.where(goes_left, diag_l, next_r), goes_left,
        rest_ref, prop_ref,
    )


def root_kernel(
    side_ref, inv_ref, mine_ref, other_ref, prop_a_ref, prop_b_ref, prop_c_ref, mine_out, partner_out, mat
):
    on_left = side_ref[3] == 1
    lower = jnp.where(on_left, mine_ref[...], other_ref[...])
    diag_l = unpack(lower[:PACKED])
    link_l = wide(lower[PACKED:])
    prop = cmul(inv_ref[...], ctrans(link_l))
    mat[...] = diag_l - cmul(link_l, prop)
    (root,) = invert([mat])
    middle = cmul(prop, root)
    x_left = jnp.where(on_left, root, middle)
    x_right = jnp.where(on_left, middle, 0.0)
    for level, ref in ((2, prop_c_ref), (1, prop_b_ref)):
        inside = cmul(ref[0], x_left) + cmul(ref[1], x_right)
        goes = side_ref[level] == 1
        x_left, x_right = jnp.where(goes, x_left, inside), jnp.where(goes, inside, x_right)
    inside = cmul(prop_a_ref[0], x_left) + cmul(prop_a_ref[1], x_right)
    mine_out[0] = x_left
    mine_out[1] = inside
    partner_out[0] = inside
    partner_out[1] = x_right


def fold_kernel(prop_ref, out_ref):
    to_l, to_r = prop_ref[2], prop_ref[3]
    out_ref[0] = prop_ref[0] + cmul(prop_ref[1], to_l)
    out_ref[1] = cmul(prop_ref[1], to_r)
    out_ref[2] = to_l
    out_ref[3] = to_r
    out_ref[4] = cmul(prop_ref[4], to_l)
    out_ref[5] = prop_ref[5] + cmul(prop_ref[4], to_r)


def density_kernel(side_ref, weight_ref, mine_ref, got_ref, prop_ref, left_ref, density_ref):
    own = side_ref[0] == 1
    x_left = jnp.where(own, mine_ref[0], got_ref[0])
    x_right = jnp.where(own, mine_ref[1], got_ref[1])
    x_2 = cmul(prop_ref[2], x_left) + cmul(prop_ref[3], x_right)
    x_1 = cmul(prop_ref[0], x_left) + cmul(prop_ref[1], x_right)
    x_3 = cmul(prop_ref[4], x_left) + cmul(prop_ref[5], x_right)
    imag = left_ref[1]
    gamma = -(imag + imag.T)
    weight = weight_ref[0]
    stacked = jnp.concatenate([tall(x) for x in (x_left, x_1, x_2, x_3)], 0)
    terms = mul3(stacked, gamma) * stacked
    for s in range(density_ref.shape[1]):
        both = terms[2 * s * W : (2 * s + 1) * W] + terms[(2 * s + 1) * W : (2 * s + 2) * W]
        row = weight * jnp.sum(both.T, axis=0, keepdims=True)
        density_ref[:, s, :] = jnp.broadcast_to(row, (density_ref.shape[0], W))


def moments_kernel(parts_ref, current_ref, past_ref, total_ref, sums_ref):
    total = jnp.sum(parts_ref[...], axis=0)
    total_ref[...] = total
    residual = total - current_ref[...]
    count = past_ref.shape[0]
    diffs = [residual - past_ref[k] for k in range(count)]
    rows = []
    for k in range(count):
        for other in diffs[k:] + [residual]:
            rows.append(jnp.sum(diffs[k] * other, axis=0, keepdims=True))
    rows.append(jnp.zeros((W - len(rows), W), F32))
    sums = jnp.sum(jnp.concatenate(rows, 0).T, axis=0, keepdims=True)
    sums_ref[...] = jnp.broadcast_to(sums, sums_ref.shape)


def mix_kernel(sums_ref, total_ref, current_ref, density_ref, past_ref, next_ref):
    count = past_ref.shape[0]
    sums = jnp.sum(sums_ref[...], axis=0)[0:1]
    gram = {}
    place = 0
    for k in range(count):
        for other in range(k, count + 1):
            entry = jnp.broadcast_to(sums[:, place : place + 1], (1, W))
            gram[k, other] = entry
            if other < count:
                gram[other, k] = entry
            place += 1
    trace = gram[0, 0]
    for k in range(1, count):
        trace = trace + gram[k, k]
    ridge = RIDGE * trace / count
    for k in range(count):
        gram[k, k] = gram[k, k] + ridge
    for k in range(count):
        pivot = 1.0 / gram[k, k]
        for col in range(k + 1, count + 1):
            gram[k, col] = gram[k, col] * pivot
        for row in range(k + 1, count):
            for col in range(k + 1, count + 1):
                gram[row, col] = gram[row, col] - gram[row, k] * gram[k, col]
    mix = [None] * count
    for k in reversed(range(count)):
        value = gram[k, count]
        for col in range(k + 1, count):
            value = value - gram[k, col] * mix[col]
        mix[k] = value
    current = current_ref[...]
    residual = total_ref[...] - current
    out = current + MIX_BETA * residual
    for k in range(count):
        step = (current - density_ref[k]) + MIX_BETA * (residual - past_ref[k])
        out = out - mix[k] * step
    next_ref[...] = out


SMEM = pl.BlockSpec(memory_space=pltpu.SMEM)
VMEM = pl.BlockSpec(memory_space=pltpu.VMEM)
ANY = pl.BlockSpec(memory_space=pltpu.MemorySpace.HBM)
BLOCK = (W, 2 * W)
MAT = pltpu.VMEM(BLOCK, F32)
PACKED = W + 8
CRIT = (PACKED, W)
REST = (PACKED + 2 * W, W)
PART = (2 * PACKED + 2 * W, W)


def call(kernel, name, shapes, in_specs, scratch=(), micros=2):
    return pl.pallas_call(
        kernel,
        out_shape=[jax.ShapeDtypeStruct(s, F32) for s in shapes],
        in_specs=in_specs,
        out_specs=[VMEM] * len(shapes),
        scratch_shapes=list(scratch),
        compiler_params=pltpu.CompilerParams(vmem_limit_bytes=32 << 20),
        name=name,
        cost_estimate=pl.CostEstimate(
            flops=micros * 1000000000, transcendentals=0, bytes_accessed=micros * 3000000
        ),
        interpret=INTERPRET,
    )


GRID = 512
MIX_BETA = 0.3
RIDGE = 0.01


def in_hbm(array):
    return pltpu.with_memory_space_constraint(array, pltpu.MemorySpace.HBM)


def send(block, route):
    return lax.ppermute(block, "slab", route)


def on_device(onsite, coupling, potential, sigma_left, sigma_right, energy_index, density_in, hist_density, hist_residual):
    slab_count = lax.axis_size("slab")
    position = lax.axis_index("slab")
    per_dev = onsite.shape[0]
    energies_all = energy_index.shape[0] * lax.axis_size("energy")
    energy = -0.4 + 0.8 * (energy_index.astype(F32) + 0.5) / GRID
    weight = 4.0 / energies_all / (1.0 + jnp.exp(energy / 0.1))
    broaden = jnp.full((1,), 2.0 / (per_dev * slab_count), F32)
    ends = jnp.stack([position == 0, position == slab_count - 1]).astype(jnp.int32)
    sides = jnp.stack([(position // (1 << level)) % 2 == 0 for level in range(4)]).astype(jnp.int32)
    left, right = sigma_left[0], sigma_right[0]
    pair = (2,) + BLOCK
    part, local = call(
        local_kernel, "local", [PART, (6,) + BLOCK],
        [SMEM, SMEM, ANY, ANY, ANY, ANY, ANY],
        [
            pltpu.VMEM((per_dev, W, W), F32), pltpu.VMEM((per_dev, W, W), F32), pltpu.VMEM((per_dev, W), F32),
            pltpu.VMEM((2, W, W), F32), pltpu.VMEM((2, W, W), F32), MAT, MAT,
            pltpu.SemaphoreType.DMA((11,)),
        ],
    )(ends, jnp.concatenate([energy, broaden]), in_hbm(onsite), in_hbm(coupling), in_hbm(potential), in_hbm(left), in_hbm(right))
    evens = range(0, slab_count, 2)
    other = send(part, [(i + 1, i) for i in evens])
    (local,) = call(fold_kernel, "fold", [(6,) + BLOCK], [VMEM], micros=1)(local)
    other, local = lax.optimization_barrier((other, local))
    inv, first, crit = call(chip_kernel, "chip", [BLOCK, BLOCK, CRIT], [SMEM] + [VMEM] * 2, [MAT])(
        sides, part, other
    )
    route = [(i, i ^ 2) for i in evens]
    crit_other = send(crit, route)
    rest, prop = call(chip_rest_kernel, "chip_rest", [REST, pair], [SMEM] + [VMEM] * 4)(
        sides, inv, first, part, other
    )
    last = slab_count - 2
    props = [prop]
    for level in (1, 2):
        rest_other = send(rest, route)
        (inv,) = call(
            functools.partial(inverse_kernel, level), f"inverse{level}", [BLOCK], [SMEM, VMEM, VMEM], [MAT], 7
        )(sides, crit, crit_other)
        first, crit = call(
            functools.partial(crit_kernel, level), f"crit{level}", [BLOCK, CRIT], [SMEM] + [VMEM] * 3
        )(sides, inv, rest, rest_other)
        route = [(i, i ^ 4) for i in evens] if level == 1 else [(i, last - i) for i in evens]
        crit_other = send(crit, route)
        rest, prop = call(
            functools.partial(rest_kernel, level), f"rest{level}", [REST, pair], [SMEM] + [VMEM] * 4
        )(sides, inv, first, rest, rest_other)
        props.append(prop)
    rest_other = send(rest, [(i, last - i) for i in evens if i < last - i])
    (inv,) = call(
        functools.partial(inverse_kernel, 3), "inverse3", [BLOCK], [SMEM, VMEM, VMEM], [MAT], 7
    )(sides, crit, crit_other)
    mine, partner = call(root_kernel, "root", [pair, pair], [SMEM] + [VMEM] * 6, [MAT])(
        sides, inv, rest, rest_other, *props
    )
    got = send(partner, [(i, i + 1) for i in evens])
    (density,) = call(density_kernel, "density", [(lax.axis_size("energy"), per_dev, W)], [SMEM, SMEM] + [VMEM] * 4)(
        sides, weight, mine, got, local, left
    )
    density = lax.all_to_all(density, "energy", 0, 0)
    total, sums = call(
        moments_kernel, "moments", [(per_dev, W), (slab_count, 8, W)], [VMEM] * 3
    )(density, density_in, hist_residual)
    sums = lax.all_to_all(sums, "slab", 0, 0)
    (following,) = call(mix_kernel, "mix", [(per_dev, W)], [VMEM] * 5)(
        sums, total, density_in, hist_density, hist_residual
    )
    return (total, following)


def solution(mesh):
    in_specs = (
        P("slab", None, None),
        P("slab", None, None),
        P("slab", None),
        P("energy", None, None, None),
        P("energy", None, None, None),
        P("energy"),
        P("slab", None),
        P(None, "slab", None),
        P(None, "slab", None),
    )
    out_specs = (P("slab", None), P("slab", None))
    return jax.shard_map(
        on_device, mesh=mesh, in_specs=in_specs, out_specs=out_specs, check_vma=False
    )
```

```python
import functools

import jax
import jax.numpy as jnp
from jax import lax
from jax.experimental import pallas as pl
from jax.experimental.pallas import tpu as pltpu
from jax.sharding import PartitionSpec as P

INTERPRET = False
W = 128
PB = 16
ORDER = ((0, 0), (0, 1), (1, 0), (0, 2), (2, 0), (1, 1))
F32 = jnp.float32
BF16 = jnp.bfloat16


def dot(a, b):
    return jnp.dot(a, b, preferred_element_type=F32)


def dot_tn(a, b):
    return lax.dot_general(a, b, (((0,), (0,)), ((), ())), preferred_element_type=F32)


def split2(x):
    hi = x.astype(BF16)
    return hi, (x - hi.astype(F32)).astype(BF16)


def split3(x):
    hi = x.astype(BF16)
    rest = x - hi.astype(F32)
    mid = rest.astype(BF16)
    return hi, mid, (rest - mid.astype(F32)).astype(BF16)


def mul3(left, right):
    return split_product(split2(left), split2(right))


def split_product(left, right):
    lh, ll = left
    rh, rl = right
    rows = lh.shape[0]
    both = dot(jnp.concatenate([lh, ll], 0), rh)
    return both[:rows] + (both[rows:] + dot(lh, rl))


def as_right(x):
    return jnp.concatenate([x, jnp.concatenate([-x[:, W:], x[:, :W]], 1)], 0)


def cmul(left, right):
    rh, rl = split2(right)
    return split_product(split2(left), (as_right(rh), as_right(rl)))


def ctrans(x):
    return jnp.concatenate([x[:, :W].T, x[:, W:].T], 1)


def sweep_panels(mats):
    lane = lax.broadcasted_iota(jnp.int32, (8, W), 1)
    row = lax.broadcasted_iota(jnp.int32, (8, W), 0)
    keep = lax.broadcasted_iota(jnp.int32, (W - PB, W), 1) < W - PB

    groups = PB // 8

    def spread(parts, j):
        return {
            g: jnp.broadcast_to(jnp.sum(jnp.where(lane == j, p, 0.0), axis=1, keepdims=True), (8, W))
            for g, p in parts.items()
        }

    def eliminate(cols_r, cols_i, k, active, live):
        gk, rk = divmod(k, 8)
        here = row == rk
        mult_r, mult_i = cols_r[k], cols_i[k]
        piv_r = jnp.broadcast_to(mult_r[gk][rk : rk + 1], (8, W))
        piv_i = jnp.broadcast_to(mult_i[gk][rk : rk + 1], (8, W))
        den = 1.0 / (piv_r * piv_r + piv_i * piv_i)
        inv_r = piv_r * den
        inv_i = -piv_i * den
        fr, fi = {}, {}
        for g in live:
            a = mult_r[g] * inv_r - mult_i[g] * inv_i
            b = mult_r[g] * inv_i + mult_i[g] * inv_r
            if g == gk:
                a = jnp.where(here, -inv_r, a)
                b = jnp.where(here, -inv_i, b)
            fr[g], fi[g] = a, b
        at = lane == W - PB + k
        for j in active:
            xr, xi = cols_r[j], cols_i[j]
            row_r = jnp.broadcast_to(xr[gk][rk : rk + 1], (8, W))
            row_i = jnp.broadcast_to(xi[gk][rk : rk + 1], (8, W))
            new_r, new_i = dict(xr), dict(xi)
            for g in live:
                br, bi = xr[g], xi[g]
                if g == gk:
                    br = jnp.where(here, 0.0, br)
                    bi = jnp.where(here, 0.0, bi)
                nr = br - (fr[g] * row_r - fi[g] * row_i)
                ni = bi - (fr[g] * row_i + fi[g] * row_r)
                if j == "w":
                    nr, ni = jnp.where(at, fr[g], nr), jnp.where(at, fi[g], ni)
                new_r[g], new_i[g] = nr, ni
            cols_r[j], cols_i[j] = new_r, new_i

    def panel(_, carry):
        state = []
        for ref in mats:
            pr = {g: ref[8 * g : 8 * g + 8, :W] for g in range(groups)}
            pi = {g: ref[8 * g : 8 * g + 8, W:] for g in range(groups)}
            cols_r = {j: spread(pr, j) for j in range(8)}
            cols_i = {j: spread(pi, j) for j in range(8)}
            cols_r["w"] = {g: pltpu.roll(p, W - PB, 1) for g, p in pr.items()}
            cols_i["w"] = {g: pltpu.roll(p, W - PB, 1) for g, p in pi.items()}
            state.append((cols_r, cols_i, [], []))
        for s in range(groups):
            edge = W - PB + 8 * s
            unit = jnp.where(lane == edge + row, -1.0, 0.0)
            for cols_r, cols_i, left_r, left_i in state:
                left_r.append(jnp.where(lane < edge, cols_r["w"][s], unit))
                left_i.append(jnp.where(lane < edge, cols_i["w"][s], 0.0))
                for cols in (cols_r, cols_i):
                    if s:
                        below = {g: cols["w"][g] for g in range(s, groups)}
                        for j in range(8 * s, 8 * s + 8):
                            cols[j] = spread(below, W - PB + j)
            for k in range(8 * s, 8 * s + 8):
                active = list(range(k + 1, 8 * s + 8)) + ["w"]
                for cols_r, cols_i, _, _ in state:
                    eliminate(cols_r, cols_i, k, active, range(s, groups))
            for cols_r, cols_i, _, _ in state:
                for cols in (cols_r, cols_i):
                    cols["w"][s] = jnp.where(lane < edge + 8, cols["w"][s], 0.0)
        for ref, (cols_r, cols_i, left_r, left_i) in zip(mats, state):
            pieces_p = split3(jnp.concatenate(left_r + left_i, 0))
            wr = jnp.concatenate([cols_r["w"][g] for g in range(groups)], 0)
            wi = jnp.concatenate([cols_i["w"][g] for g in range(groups)], 0)
            pieces_w = [
                jnp.concatenate([jnp.concatenate([r, i], 1), jnp.concatenate([-i, r], 1)], 0)
                for r, i in zip(split3(wr), split3(wi))
            ]
            lhs = jnp.concatenate([pieces_p[a] for a, _ in ORDER], 0)
            rhs = jnp.concatenate([pieces_w[b] for _, b in ORDER], 0)
            update = dot_tn(lhs, rhs)
            old_r = jnp.where(keep, pltpu.roll(ref[PB:, :W], W - PB, 1), 0.0)
            old_i = jnp.where(keep, pltpu.roll(ref[PB:, W:], W - PB, 1), 0.0)
            ref[: W - PB, :W] = old_r - update[: W - PB, :W]
            ref[: W - PB, W:] = old_i - update[: W - PB, W:]
            ref[W - PB :, :] = -update[W - PB :, :]
        return carry

    lax.fori_loop(0, W // PB, panel, 0)


def invert(refs):
    sweep_panels(refs)
    return [-ref[...] for ref in refs]


def triangles():
    row = lax.broadcasted_iota(jnp.int32, (W, W), 0)
    col = lax.broadcasted_iota(jnp.int32, (W, W), 1)
    return row, col


def pack(x):
    row, col = triangles()
    real, imag = x[:, :W], x[:, W:]
    tip = jnp.sum(jnp.where(row == col, imag, 0.0), axis=0, keepdims=True)
    return jnp.concatenate([jnp.where(row <= col, real, imag), jnp.broadcast_to(tip, (8, W))], 0)


def unpack(packed):
    row, col = triangles()
    body = packed[:W]
    turned = body.T
    imag = jnp.where(row == col, packed[W : W + 1], turned)
    return jnp.concatenate(
        [jnp.where(row <= col, body, turned), jnp.where(row > col, body, imag)], 1
    )


def tall(x):
    return jnp.concatenate([x[:, :W], x[:, W:]], 0)


def wide(x):
    return jnp.concatenate([x[:W], x[W:]], 1)


def real_right(inv, real):
    out = mul3(jnp.concatenate([inv[:, :W], inv[:, W:]], 0), real)
    return jnp.concatenate([out[:W], out[W:]], 1)


def local_kernel(
    flag_ref, energy_ref, onsite_hbm, coupling_hbm, potential_hbm, left_hbm, right_hbm,
    part_ref, prop_ref,
    onsite_ref, coupling_ref, potential_ref, left_ref, right_ref, mat_a, mat_b, sems,
):
    is_first = flag_ref[0] == 1
    is_last = flag_ref[1] == 1
    energy = energy_ref[0]
    copies = []

    def fetch(src, dst):
        copy = pltpu.make_async_copy(src, dst, sems.at[len(copies)])
        copy.start()
        copies.append(copy)
        return copy

    potential_copy = fetch(potential_hbm, potential_ref)
    onsite_copy = {s: fetch(onsite_hbm.at[s], onsite_ref.at[s]) for s in (1, 3)}
    right_copy = fetch(right_hbm, right_ref)
    coupling_copy = [fetch(coupling_hbm.at[s], coupling_ref.at[s]) for s in range(4)]
    onsite_copy.update({s: fetch(onsite_hbm.at[s], onsite_ref.at[s]) for s in (2, 0)})
    left_copy = fetch(left_hbm, left_ref)
    eye = lax.broadcasted_iota(jnp.int32, (W, W), 0) == lax.broadcasted_iota(jnp.int32, (W, W), 1)
    broaden = jnp.where(eye, energy_ref[1], 0.0)

    def diagonal(s):
        onsite_copy[s].wait()
        real = jnp.where(eye, energy - potential_ref[s : s + 1, :], 0.0) - onsite_ref[s]
        return jnp.concatenate([real, broaden], 1)

    potential_copy.wait()
    mat_a[...] = diagonal(1)
    diag_3 = diagonal(3)
    right_copy.wait()
    last = jnp.concatenate([right_ref[0], right_ref[1]], 1)
    mat_b[...] = diag_3 - jnp.where(is_last, last, 0.0)
    inv_1, inv_3 = invert([mat_a, mat_b])
    for copy in coupling_copy:
        copy.wait()
    c0, c1, c2 = coupling_ref[0], coupling_ref[1], coupling_ref[2]
    c3 = jnp.where(is_last, 0.0, coupling_ref[3])
    prop_1r = real_right(inv_1, c1)
    prop_3l = real_right(inv_3, c2.T)
    mat_a[...] = diagonal(2) - mul3(c1.T, prop_1r) - mul3(c2, prop_3l)
    (inv_2,) = invert([mat_a])
    prop_1l = real_right(inv_1, c0.T)
    prop_3r = real_right(inv_3, c3)
    diag_0 = diagonal(0)
    left_copy.wait()
    first = jnp.concatenate([left_ref[0], left_ref[1]], 1)
    top = diag_0 - jnp.where(is_first, first, 0.0) - mul3(c0, prop_1l)
    k02 = mul3(c0, prop_1r)
    k2n = mul3(c2, prop_3r)
    prop_2l = cmul(inv_2, ctrans(k02))
    prop_2r = cmul(inv_2, k2n)
    part_ref[:PACKED] = pack(top - cmul(k02, prop_2l))
    part_ref[PACKED : 2 * PACKED] = pack(mul3(c3.T, prop_3r) + cmul(ctrans(k2n), prop_2r))
    part_ref[2 * PACKED :] = tall(cmul(k02, prop_2r))
    for n, prop in enumerate((prop_1l, prop_1r, prop_2l, prop_2r, prop_3l, prop_3r)):
        prop_ref[n] = prop


def facing(link_l, link_r, to_right):
    plain = jnp.where(to_right, link_r, link_l)
    turned = ctrans(plain)
    return jnp.where(to_right, plain, turned), jnp.where(to_right, turned, plain)


def urgent(inv, link_l, link_r, base, goes_left):
    side, side_t = facing(link_l, link_r, goes_left)
    prop = cmul(inv, side)
    change = cmul(side_t, prop)
    return prop, pack(unpack(base) + jnp.where(goes_left, change, -change))


def joined(prop, link_l, link_r, goes_left):
    return cmul(
        jnp.where(goes_left, link_l, ctrans(prop)), jnp.where(goes_left, prop, link_r)
    )


def others(inv, prop, link_l, link_r, base, goes_left, base_ref, prop_ref):
    side, side_t = facing(link_l, link_r, jnp.logical_not(goes_left))
    second = cmul(inv, side)
    change = cmul(side_t, second)
    prop_r = jnp.where(goes_left, prop, second)
    base_ref[...] = pack(unpack(base) + jnp.where(goes_left, -change, change))
    prop_ref[0] = jnp.where(goes_left, second, prop)
    prop_ref[1] = prop_r


def chip_sides(side_ref, mine_ref, other_ref):
    goes_left = side_ref[1] == 1
    diag_l = mine_ref[:PACKED]
    next_r = other_ref[PACKED : 2 * PACKED]
    links = wide(mine_ref[2 * PACKED :]), wide(other_ref[2 * PACKED :])
    return links, (diag_l, next_r), goes_left


def chip_kernel(side_ref, mine_ref, other_ref, inv_ref, first_ref, crit_ref, mat):
    mat[...] = unpack(other_ref[:PACKED] - mine_ref[PACKED : 2 * PACKED])
    (inv,) = invert([mat])
    inv_ref[...] = inv
    links, (diag_l, next_r), goes_left = chip_sides(side_ref, mine_ref, other_ref)
    first_ref[...], crit_ref[...] = urgent(inv, *links, jnp.where(goes_left, next_r, diag_l), goes_left)


def chip_rest_kernel(side_ref, inv_ref, first_ref, mine_ref, other_ref, rest_ref, prop_ref):
    links, (diag_l, next_r), goes_left = chip_sides(side_ref, mine_ref, other_ref)
    first = first_ref[...]
    others(
        inv_ref[...], first, *links, jnp.where(goes_left, diag_l, next_r), goes_left,
        rest_ref.at[:PACKED], prop_ref,
    )
    rest_ref[PACKED:] = tall(joined(first, *links, goes_left))


def inverse_kernel(level, side_ref, mine_ref, other_ref, inv_ref, mat):
    mine, other = mine_ref[...], other_ref[...]
    mat[...] = unpack(jnp.where(side_ref[level] == 1, other - mine, mine - other))
    (inv_ref[...],) = invert([mat])


def both_sides(level, side_ref, base_refs, link_refs):
    on_left = side_ref[level] == 1

    def pick(refs):
        mine, other = (ref[...] for ref in refs)
        return jnp.where(on_left, mine, other), jnp.where(on_left, other, mine)

    links = [wide(link) for link in pick(link_refs)]
    return links, pick(base_refs), side_ref[level + 1] == 1


def halves(ref):
    return ref.at[:PACKED], ref.at[PACKED:]


def crit1_kernel(side_ref, inv_ref, mine_ref, other_ref, first_ref, crit_ref, link_ref):
    bases, ends = zip(halves(mine_ref), halves(other_ref))
    links, (diag_l, next_r), goes_left = both_sides(1, side_ref, bases, ends)
    first, crit_ref[...] = urgent(
        inv_ref[...], *links, jnp.where(goes_left, next_r, diag_l), goes_left
    )
    first_ref[...] = first
    link_ref[...] = tall(joined(first, *links, goes_left))


def rest1_kernel(side_ref, inv_ref, first_ref, mine_ref, other_ref, base_ref, prop_ref):
    bases, ends = zip(halves(mine_ref), halves(other_ref))
    links, (diag_l, next_r), goes_left = both_sides(1, side_ref, bases, ends)
    others(
        inv_ref[...], first_ref[...], *links, jnp.where(goes_left, diag_l, next_r), goes_left,
        base_ref, prop_ref,
    )


def crit2_kernel(side_ref, inv_ref, base_ref, base_other, link_ref, link_other, first_ref, crit_ref):
    links, (diag_l, next_r), goes_left = both_sides(
        2, side_ref, (base_ref, base_other), (link_ref, link_other)
    )
    first_ref[...], crit_ref[...] = urgent(
        inv_ref[...], *links, jnp.where(goes_left, next_r, diag_l), goes_left
    )


def rest2_kernel(side_ref, inv_ref, first_ref, base_ref, base_other, link_ref, link_other, rest_ref, prop_ref):
    links, (diag_l, next_r), goes_left = both_sides(
        2, side_ref, (base_ref, base_other), (link_ref, link_other)
    )
    first = first_ref[...]
    others(
        inv_ref[...], first, *links, jnp.where(goes_left, diag_l, next_r), goes_left,
        rest_ref.at[:PACKED], prop_ref,
    )
    rest_ref[PACKED:] = tall(joined(first, *links, goes_left))


def root_kernel(
    side_ref, inv_ref, mine_ref, other_ref, prop_a_ref, prop_b_ref, prop_c_ref, mine_out, partner_out, mat
):
    on_left = side_ref[3] == 1
    lower = jnp.where(on_left, mine_ref[...], other_ref[...])
    diag_l = unpack(lower[:PACKED])
    link_l = wide(lower[PACKED:])
    prop = cmul(inv_ref[...], ctrans(link_l))
    mat[...] = diag_l - cmul(link_l, prop)
    (root,) = invert([mat])
    middle = cmul(prop, root)
    x_left = jnp.where(on_left, root, middle)
    x_right = jnp.where(on_left, middle, 0.0)
    for level, ref in ((2, prop_c_ref), (1, prop_b_ref)):
        inside = cmul(ref[0], x_left) + cmul(ref[1], x_right)
        goes = side_ref[level] == 1
        x_left, x_right = jnp.where(goes, x_left, inside), jnp.where(goes, inside, x_right)
    inside = cmul(prop_a_ref[0], x_left) + cmul(prop_a_ref[1], x_right)
    mine_out[0] = x_left
    mine_out[1] = inside
    partner_out[0] = inside
    partner_out[1] = x_right


def fold_kernel(prop_ref, out_ref):
    to_l, to_r = prop_ref[2], prop_ref[3]
    out_ref[0] = prop_ref[0] + cmul(prop_ref[1], to_l)
    out_ref[1] = cmul(prop_ref[1], to_r)
    out_ref[2] = to_l
    out_ref[3] = to_r
    out_ref[4] = cmul(prop_ref[4], to_l)
    out_ref[5] = prop_ref[5] + cmul(prop_ref[4], to_r)


def density_kernel(side_ref, weight_ref, mine_ref, got_ref, prop_ref, left_ref, density_ref):
    own = side_ref[0] == 1
    x_left = jnp.where(own, mine_ref[0], got_ref[0])
    x_right = jnp.where(own, mine_ref[1], got_ref[1])
    x_2 = cmul(prop_ref[2], x_left) + cmul(prop_ref[3], x_right)
    x_1 = cmul(prop_ref[0], x_left) + cmul(prop_ref[1], x_right)
    x_3 = cmul(prop_ref[4], x_left) + cmul(prop_ref[5], x_right)
    imag = left_ref[1]
    gamma = -(imag + imag.T)
    weight = weight_ref[0]
    stacked = jnp.concatenate([tall(x) for x in (x_left, x_1, x_2, x_3)], 0)
    terms = mul3(stacked, gamma) * stacked
    for s in range(density_ref.shape[1]):
        both = terms[2 * s * W : (2 * s + 1) * W] + terms[(2 * s + 1) * W : (2 * s + 2) * W]
        row = weight * jnp.sum(both.T, axis=0, keepdims=True)
        density_ref[:, s, :] = jnp.broadcast_to(row, (density_ref.shape[0], W))


def moments_kernel(parts_ref, current_ref, past_ref, total_ref, sums_ref):
    total = jnp.sum(parts_ref[...], axis=0)
    total_ref[...] = total
    residual = total - current_ref[...]
    count = past_ref.shape[0]
    diffs = [residual - past_ref[k] for k in range(count)]
    rows = []
    for k in range(count):
        for other in diffs[k:] + [residual]:
            rows.append(jnp.sum(diffs[k] * other, axis=0, keepdims=True))
    rows.append(jnp.zeros((W - len(rows), W), F32))
    sums = jnp.sum(jnp.concatenate(rows, 0).T, axis=0, keepdims=True)
    sums_ref[...] = jnp.broadcast_to(sums, sums_ref.shape)


def mix_kernel(sums_ref, total_ref, current_ref, density_ref, past_ref, next_ref):
    count = past_ref.shape[0]
    sums = jnp.sum(sums_ref[...], axis=0)[0:1]
    gram = {}
    place = 0
    for k in range(count):
        for other in range(k, count + 1):
            entry = jnp.broadcast_to(sums[:, place : place + 1], (1, W))
            gram[k, other] = entry
            if other < count:
                gram[other, k] = entry
            place += 1
    trace = gram[0, 0]
    for k in range(1, count):
        trace = trace + gram[k, k]
    ridge = RIDGE * trace / count
    for k in range(count):
        gram[k, k] = gram[k, k] + ridge
    for k in range(count):
        pivot = 1.0 / gram[k, k]
        for col in range(k + 1, count + 1):
            gram[k, col] = gram[k, col] * pivot
        for row in range(k + 1, count):
            for col in range(k + 1, count + 1):
                gram[row, col] = gram[row, col] - gram[row, k] * gram[k, col]
    mix = [None] * count
    for k in reversed(range(count)):
        value = gram[k, count]
        for col in range(k + 1, count):
            value = value - gram[k, col] * mix[col]
        mix[k] = value
    current = current_ref[...]
    residual = total_ref[...] - current
    out = current + MIX_BETA * residual
    for k in range(count):
        step = (current - density_ref[k]) + MIX_BETA * (residual - past_ref[k])
        out = out - mix[k] * step
    next_ref[...] = out


SMEM = pl.BlockSpec(memory_space=pltpu.SMEM)
VMEM = pl.BlockSpec(memory_space=pltpu.VMEM)
ANY = pl.BlockSpec(memory_space=pltpu.MemorySpace.HBM)
BLOCK = (W, 2 * W)
MAT = pltpu.VMEM(BLOCK, F32)
PACKED = W + 8
CRIT = (PACKED, W)
LINK = (2 * W, W)
REST = (PACKED + 2 * W, W)
PART = (2 * PACKED + 2 * W, W)


def call(kernel, name, shapes, in_specs, scratch=(), micros=2):
    return pl.pallas_call(
        kernel,
        out_shape=[jax.ShapeDtypeStruct(s, F32) for s in shapes],
        in_specs=in_specs,
        out_specs=[VMEM] * len(shapes),
        scratch_shapes=list(scratch),
        compiler_params=pltpu.CompilerParams(vmem_limit_bytes=32 << 20),
        name=name,
        cost_estimate=pl.CostEstimate(
            flops=micros * 1000000000, transcendentals=0, bytes_accessed=micros * 3000000
        ),
        interpret=INTERPRET,
    )


GRID = 512
MIX_BETA = 0.3
RIDGE = 0.01


def in_hbm(array):
    return pltpu.with_memory_space_constraint(array, pltpu.MemorySpace.HBM)


def send(block, route):
    return lax.ppermute(block, "slab", route)


def on_device(onsite, coupling, potential, sigma_left, sigma_right, energy_index, density_in, hist_density, hist_residual):
    slab_count = lax.axis_size("slab")
    position = lax.axis_index("slab")
    per_dev = onsite.shape[0]
    energies_all = energy_index.shape[0] * lax.axis_size("energy")
    energy = -0.4 + 0.8 * (energy_index.astype(F32) + 0.5) / GRID
    weight = 4.0 / energies_all / (1.0 + jnp.exp(energy / 0.1))
    broaden = jnp.full((1,), 2.0 / (per_dev * slab_count), F32)
    ends = jnp.stack([position == 0, position == slab_count - 1]).astype(jnp.int32)
    sides = jnp.stack([(position // (1 << level)) % 2 == 0 for level in range(4)]).astype(jnp.int32)
    left, right = sigma_left[0], sigma_right[0]
    pair = (2,) + BLOCK
    part, local = call(
        local_kernel, "local", [PART, (6,) + BLOCK],
        [SMEM, SMEM, ANY, ANY, ANY, ANY, ANY],
        [
            pltpu.VMEM((per_dev, W, W), F32), pltpu.VMEM((per_dev, W, W), F32), pltpu.VMEM((per_dev, W), F32),
            pltpu.VMEM((2, W, W), F32), pltpu.VMEM((2, W, W), F32), MAT, MAT,
            pltpu.SemaphoreType.DMA((11,)),
        ],
    )(ends, jnp.concatenate([energy, broaden]), in_hbm(onsite), in_hbm(coupling), in_hbm(potential), in_hbm(left), in_hbm(right))
    evens = range(0, slab_count, 2)
    other = send(part, [(i + 1, i) for i in evens])
    (local,) = call(fold_kernel, "fold", [(6,) + BLOCK], [VMEM], micros=1)(local)
    other, local = lax.optimization_barrier((other, local))
    inv, first, crit = call(chip_kernel, "chip", [BLOCK, BLOCK, CRIT], [SMEM] + [VMEM] * 2, [MAT])(
        sides, part, other
    )
    route = [(i, i ^ 2) for i in evens]
    crit_other = send(crit, route)
    rest, prop = call(chip_rest_kernel, "chip_rest", [REST, pair], [SMEM] + [VMEM] * 4)(
        sides, inv, first, part, other
    )
    last = slab_count - 2
    props = [prop]

    def inverse(level, crit, crit_other):
        return call(
            functools.partial(inverse_kernel, level), f"inverse{level}", [BLOCK], [SMEM, VMEM, VMEM], [MAT], 1 if level == 2 else 7
        )(sides, crit, crit_other)[0]

    rest_other = send(rest, route)
    inv = inverse(1, crit, crit_other)
    first, crit, link = call(crit1_kernel, "crit1", [BLOCK, CRIT, LINK], [SMEM] + [VMEM] * 3)(
        sides, inv, rest, rest_other
    )
    route = [(i, i ^ 4) for i in evens]
    crit_other = send(crit, route)
    link_other = send(link, route)
    base, prop = call(rest1_kernel, "rest1", [CRIT, pair], [SMEM] + [VMEM] * 4, micros=4)(
        sides, inv, first, rest, rest_other
    )
    props.append(prop)
    base_other = send(base, route)
    inv = inverse(2, crit, crit_other)
    parts = (base, base_other, link, link_other)
    first, crit = call(crit2_kernel, "crit2", [BLOCK, CRIT], [SMEM] + [VMEM] * 5)(sides, inv, *parts)
    crit_other = send(crit, [(i, last - i) for i in evens])
    rest, prop = call(rest2_kernel, "rest2", [REST, pair], [SMEM] + [VMEM] * 6)(sides, inv, first, *parts)
    props.append(prop)
    rest_other = send(rest, [(i, last - i) for i in evens if i < last - i])
    inv = inverse(3, crit, crit_other)
    mine, partner = call(root_kernel, "root", [pair, pair], [SMEM] + [VMEM] * 6, [MAT])(
        sides, inv, rest, rest_other, *props
    )
    got = send(partner, [(i, i + 1) for i in evens])
    (density,) = call(density_kernel, "density", [(lax.axis_size("energy"), per_dev, W)], [SMEM, SMEM] + [VMEM] * 4)(
        sides, weight, mine, got, local, left
    )
    density = lax.all_to_all(density, "energy", 0, 0)
    total, sums = call(
        moments_kernel, "moments", [(per_dev, W), (slab_count, 8, W)], [VMEM] * 3
    )(density, density_in, hist_residual)
    sums = lax.all_to_all(sums, "slab", 0, 0)
    (following,) = call(mix_kernel, "mix", [(per_dev, W)], [VMEM] * 5)(
        sums, total, density_in, hist_density, hist_residual
    )
    return (total, following)


def solution(mesh):
    in_specs = (
        P("slab", None, None),
        P("slab", None, None),
        P("slab", None),
        P("energy", None, None, None),
        P("energy", None, None, None),
        P("energy"),
        P("slab", None),
        P(None, "slab", None),
        P(None, "slab", None),
    )
    out_specs = (P("slab", None), P("slab", None))
    return jax.shard_map(
        on_device, mesh=mesh, in_specs=in_specs, out_specs=out_specs, check_vma=False
    )
```

```python
import functools

import jax
import jax.numpy as jnp
from jax import lax
from jax.experimental import pallas as pl
from jax.experimental.pallas import tpu as pltpu
from jax.sharding import PartitionSpec as P

INTERPRET = False
W = 128
PB = 16
ORDER = ((0, 0), (0, 1), (1, 0), (0, 2), (2, 0), (1, 1))
F32 = jnp.float32
BF16 = jnp.bfloat16


def dot(a, b):
    return jnp.dot(a, b, preferred_element_type=F32)


def dot_tn(a, b):
    return lax.dot_general(a, b, (((0,), (0,)), ((), ())), preferred_element_type=F32)


def split2(x):
    hi = x.astype(BF16)
    return hi, (x - hi.astype(F32)).astype(BF16)


def split3(x):
    hi = x.astype(BF16)
    rest = x - hi.astype(F32)
    mid = rest.astype(BF16)
    return hi, mid, (rest - mid.astype(F32)).astype(BF16)


def mul3(left, right):
    return split_product(split2(left), split2(right))


def split_product(left, right):
    lh, ll = left
    rh, rl = right
    rows = lh.shape[0]
    both = dot(jnp.concatenate([lh, ll], 0), rh)
    return both[:rows] + (both[rows:] + dot(lh, rl))


def as_right(x):
    return jnp.concatenate([x, jnp.concatenate([-x[:, W:], x[:, :W]], 1)], 0)


def cmul(left, right):
    rh, rl = split2(right)
    return split_product(split2(left), (as_right(rh), as_right(rl)))


def ctrans(x):
    return jnp.concatenate([x[:, :W].T, x[:, W:].T], 1)


def sweep_panels(mats):
    lane = lax.broadcasted_iota(jnp.int32, (8, W), 1)
    row = lax.broadcasted_iota(jnp.int32, (8, W), 0)
    keep = lax.broadcasted_iota(jnp.int32, (W - PB, W), 1) < W - PB

    groups = PB // 8

    def spread(parts, j):
        return {
            g: jnp.broadcast_to(jnp.sum(jnp.where(lane == j, p, 0.0), axis=1, keepdims=True), (8, W))
            for g, p in parts.items()
        }

    def eliminate(cols_r, cols_i, k, active, live):
        gk, rk = divmod(k, 8)
        here = row == rk
        mult_r, mult_i = cols_r[k], cols_i[k]
        piv_r = jnp.broadcast_to(mult_r[gk][rk : rk + 1], (8, W))
        piv_i = jnp.broadcast_to(mult_i[gk][rk : rk + 1], (8, W))
        den = 1.0 / (piv_r * piv_r + piv_i * piv_i)
        inv_r = piv_r * den
        inv_i = -piv_i * den
        fr, fi = {}, {}
        for g in live:
            a = mult_r[g] * inv_r - mult_i[g] * inv_i
            b = mult_r[g] * inv_i + mult_i[g] * inv_r
            if g == gk:
                a = jnp.where(here, -inv_r, a)
                b = jnp.where(here, -inv_i, b)
            fr[g], fi[g] = a, b
        at = lane == W - PB + k
        for j in active:
            xr, xi = cols_r[j], cols_i[j]
            row_r = jnp.broadcast_to(xr[gk][rk : rk + 1], (8, W))
            row_i = jnp.broadcast_to(xi[gk][rk : rk + 1], (8, W))
            new_r, new_i = dict(xr), dict(xi)
            for g in live:
                br, bi = xr[g], xi[g]
                if g == gk:
                    br = jnp.where(here, 0.0, br)
                    bi = jnp.where(here, 0.0, bi)
                nr = br - (fr[g] * row_r - fi[g] * row_i)
                ni = bi - (fr[g] * row_i + fi[g] * row_r)
                if j == "w":
                    nr, ni = jnp.where(at, fr[g], nr), jnp.where(at, fi[g], ni)
                new_r[g], new_i[g] = nr, ni
            cols_r[j], cols_i[j] = new_r, new_i

    def panel(_, carry):
        state = []
        for ref in mats:
            pr = {g: ref[8 * g : 8 * g + 8, :W] for g in range(groups)}
            pi = {g: ref[8 * g : 8 * g + 8, W:] for g in range(groups)}
            cols_r = {j: spread(pr, j) for j in range(8)}
            cols_i = {j: spread(pi, j) for j in range(8)}
            cols_r["w"] = {g: pltpu.roll(p, W - PB, 1) for g, p in pr.items()}
            cols_i["w"] = {g: pltpu.roll(p, W - PB, 1) for g, p in pi.items()}
            state.append((cols_r, cols_i, [], []))
        for s in range(groups):
            edge = W - PB + 8 * s
            unit = jnp.where(lane == edge + row, -1.0, 0.0)
            for cols_r, cols_i, left_r, left_i in state:
                left_r.append(jnp.where(lane < edge, cols_r["w"][s], unit))
                left_i.append(jnp.where(lane < edge, cols_i["w"][s], 0.0))
                for cols in (cols_r, cols_i):
                    if s:
                        below = {g: cols["w"][g] for g in range(s, groups)}
                        for j in range(8 * s, 8 * s + 8):
                            cols[j] = spread(below, W - PB + j)
            for k in range(8 * s, 8 * s + 8):
                active = list(range(k + 1, 8 * s + 8)) + ["w"]
                for cols_r, cols_i, _, _ in state:
                    eliminate(cols_r, cols_i, k, active, range(s, groups))
            for cols_r, cols_i, _, _ in state:
                for cols in (cols_r, cols_i):
                    cols["w"][s] = jnp.where(lane < edge + 8, cols["w"][s], 0.0)
        for ref, (cols_r, cols_i, left_r, left_i) in zip(mats, state):
            pieces_p = split3(jnp.concatenate(left_r + left_i, 0))
            wr = jnp.concatenate([cols_r["w"][g] for g in range(groups)], 0)
            wi = jnp.concatenate([cols_i["w"][g] for g in range(groups)], 0)
            pieces_w = [
                jnp.concatenate([jnp.concatenate([r, i], 1), jnp.concatenate([-i, r], 1)], 0)
                for r, i in zip(split3(wr), split3(wi))
            ]
            lhs = jnp.concatenate([pieces_p[a] for a, _ in ORDER], 0)
            rhs = jnp.concatenate([pieces_w[b] for _, b in ORDER], 0)
            update = dot_tn(lhs, rhs)
            old_r = jnp.where(keep, pltpu.roll(ref[PB:, :W], W - PB, 1), 0.0)
            old_i = jnp.where(keep, pltpu.roll(ref[PB:, W:], W - PB, 1), 0.0)
            ref[: W - PB, :W] = old_r - update[: W - PB, :W]
            ref[: W - PB, W:] = old_i - update[: W - PB, W:]
            ref[W - PB :, :] = -update[W - PB :, :]
        return carry

    lax.fori_loop(0, W // PB, panel, 0)


def invert(refs):
    sweep_panels(refs)
    return [-ref[...] for ref in refs]


def triangles():
    row = lax.broadcasted_iota(jnp.int32, (W, W), 0)
    col = lax.broadcasted_iota(jnp.int32, (W, W), 1)
    return row, col


def pack(x):
    row, col = triangles()
    real, imag = x[:, :W], x[:, W:]
    tip = jnp.sum(jnp.where(row == col, imag, 0.0), axis=0, keepdims=True)
    return jnp.concatenate([jnp.where(row <= col, real, imag), jnp.broadcast_to(tip, (8, W))], 0)


def unpack(packed):
    row, col = triangles()
    body = packed[:W]
    turned = body.T
    imag = jnp.where(row == col, packed[W : W + 1], turned)
    return jnp.concatenate(
        [jnp.where(row <= col, body, turned), jnp.where(row > col, body, imag)], 1
    )


def tall(x):
    return jnp.concatenate([x[:, :W], x[:, W:]], 0)


def wide(x):
    return jnp.concatenate([x[:W], x[W:]], 1)


def real_right(inv, real):
    out = mul3(jnp.concatenate([inv[:, :W], inv[:, W:]], 0), real)
    return jnp.concatenate([out[:W], out[W:]], 1)


def local_kernel(
    flag_ref, energy_ref, onsite_hbm, coupling_hbm, potential_hbm, left_hbm, right_hbm,
    part_ref, prop_ref,
    onsite_ref, coupling_ref, potential_ref, left_ref, right_ref, mat_a, mat_b, sems,
):
    is_first = flag_ref[0] == 1
    is_last = flag_ref[1] == 1
    energy = energy_ref[0]
    copies = []

    def fetch(src, dst):
        copy = pltpu.make_async_copy(src, dst, sems.at[len(copies)])
        copy.start()
        copies.append(copy)
        return copy

    potential_copy = fetch(potential_hbm, potential_ref)
    onsite_copy = {s: fetch(onsite_hbm.at[s], onsite_ref.at[s]) for s in (1, 3)}
    right_copy = fetch(right_hbm, right_ref)
    coupling_copy = [fetch(coupling_hbm.at[s], coupling_ref.at[s]) for s in range(4)]
    onsite_copy.update({s: fetch(onsite_hbm.at[s], onsite_ref.at[s]) for s in (2, 0)})
    left_copy = fetch(left_hbm, left_ref)
    eye = lax.broadcasted_iota(jnp.int32, (W, W), 0) == lax.broadcasted_iota(jnp.int32, (W, W), 1)
    broaden = jnp.where(eye, energy_ref[1], 0.0)

    def diagonal(s):
        onsite_copy[s].wait()
        real = jnp.where(eye, energy - potential_ref[s : s + 1, :], 0.0) - onsite_ref[s]
        return jnp.concatenate([real, broaden], 1)

    potential_copy.wait()
    mat_a[...] = diagonal(1)
    diag_3 = diagonal(3)
    right_copy.wait()
    last = jnp.concatenate([right_ref[0], right_ref[1]], 1)
    mat_b[...] = diag_3 - jnp.where(is_last, last, 0.0)
    inv_1, inv_3 = invert([mat_a, mat_b])
    for copy in coupling_copy:
        copy.wait()
    c0, c1, c2 = coupling_ref[0], coupling_ref[1], coupling_ref[2]
    c3 = jnp.where(is_last, 0.0, coupling_ref[3])
    prop_1r = real_right(inv_1, c1)
    prop_3l = real_right(inv_3, c2.T)
    mat_a[...] = diagonal(2) - mul3(c1.T, prop_1r) - mul3(c2, prop_3l)
    (inv_2,) = invert([mat_a])
    prop_1l = real_right(inv_1, c0.T)
    prop_3r = real_right(inv_3, c3)
    diag_0 = diagonal(0)
    left_copy.wait()
    first = jnp.concatenate([left_ref[0], left_ref[1]], 1)
    top = diag_0 - jnp.where(is_first, first, 0.0) - mul3(c0, prop_1l)
    k02 = mul3(c0, prop_1r)
    k2n = mul3(c2, prop_3r)
    prop_2l = cmul(inv_2, ctrans(k02))
    prop_2r = cmul(inv_2, k2n)
    part_ref[:PACKED] = pack(top - cmul(k02, prop_2l))
    part_ref[PACKED : 2 * PACKED] = pack(mul3(c3.T, prop_3r) + cmul(ctrans(k2n), prop_2r))
    part_ref[2 * PACKED :] = tall(cmul(k02, prop_2r))
    for n, prop in enumerate((prop_1l, prop_1r, prop_2l, prop_2r, prop_3l, prop_3r)):
        prop_ref[n] = prop


def facing(link_l, link_r, to_right):
    plain = jnp.where(to_right, link_r, link_l)
    turned = ctrans(plain)
    return jnp.where(to_right, plain, turned), jnp.where(to_right, turned, plain)


def urgent(inv, link_l, link_r, base, goes_left):
    side, side_t = facing(link_l, link_r, goes_left)
    prop = cmul(inv, side)
    change = cmul(side_t, prop)
    return prop, pack(unpack(base) + jnp.where(goes_left, change, -change))


def others(inv, prop, link_l, link_r, base, goes_left, rest_ref, prop_ref):
    side, side_t = facing(link_l, link_r, jnp.logical_not(goes_left))
    second = cmul(inv, side)
    change = cmul(side_t, second)
    prop_r = jnp.where(goes_left, prop, second)
    rest_ref[:PACKED] = pack(unpack(base) + jnp.where(goes_left, -change, change))
    rest_ref[PACKED:] = tall(cmul(link_l, prop_r))
    prop_ref[0] = jnp.where(goes_left, second, prop)
    prop_ref[1] = prop_r


def chip_sides(side_ref, mine_ref, other_ref):
    goes_left = side_ref[1] == 1
    diag_l = mine_ref[:PACKED]
    next_r = other_ref[PACKED : 2 * PACKED]
    links = wide(mine_ref[2 * PACKED :]), wide(other_ref[2 * PACKED :])
    return links, (diag_l, next_r), goes_left


def chip_kernel(side_ref, mine_ref, other_ref, inv_ref, first_ref, crit_ref, mat):
    mat[...] = unpack(other_ref[:PACKED] - mine_ref[PACKED : 2 * PACKED])
    (inv,) = invert([mat])
    inv_ref[...] = inv
    links, (diag_l, next_r), goes_left = chip_sides(side_ref, mine_ref, other_ref)
    first_ref[...], crit_ref[...] = urgent(inv, *links, jnp.where(goes_left, next_r, diag_l), goes_left)


def chip_rest_kernel(side_ref, inv_ref, first_ref, mine_ref, other_ref, rest_ref, prop_ref):
    links, (diag_l, next_r), goes_left = chip_sides(side_ref, mine_ref, other_ref)
    others(
        inv_ref[...], first_ref[...], *links, jnp.where(goes_left, diag_l, next_r), goes_left,
        rest_ref, prop_ref,
    )


def inverse_kernel(level, side_ref, mine_ref, other_ref, inv_ref, mat):
    mine, other = mine_ref[...], other_ref[...]
    mat[...] = unpack(jnp.where(side_ref[level] == 1, other - mine, mine - other))
    (inv_ref[...],) = invert([mat])


def both_sides(level, side_ref, mine_ref, other_ref):
    on_left = side_ref[level] == 1
    mine, other = mine_ref[...], other_ref[...]
    left, right = jnp.where(on_left, mine, other), jnp.where(on_left, other, mine)
    links = wide(left[PACKED:]), wide(right[PACKED:])
    return links, (left[:PACKED], right[:PACKED]), side_ref[level + 1] == 1


def crit_kernel(level, side_ref, inv_ref, mine_ref, other_ref, first_ref, crit_ref):
    links, (diag_l, next_r), goes_left = both_sides(level, side_ref, mine_ref, other_ref)
    first_ref[...], crit_ref[...] = urgent(
        inv_ref[...], *links, jnp.where(goes_left, next_r, diag_l), goes_left
    )


def rest_kernel(level, side_ref, inv_ref, first_ref, mine_ref, other_ref, rest_ref, prop_ref):
    links, (diag_l, next_r), goes_left = both_sides(level, side_ref, mine_ref, other_ref)
    others(
        inv_ref[...], first_ref[...], *links, jnp.where(goes_left, diag_l, next_r), goes_left,
        rest_ref, prop_ref,
    )


def composed(goes_left, inner, outer):
    near, far = inner
    through = jnp.where(goes_left, far, near)
    return (
        cmul(through, outer[0]) + jnp.where(goes_left, near, 0.0),
        cmul(through, outer[1]) + jnp.where(goes_left, 0.0, far),
    )


def map1_kernel(side_ref, inner_ref, outer_ref, after_ref, out_ref):
    goes = side_ref[1] == 1
    out_ref[0], out_ref[1] = composed(goes, (inner_ref[0], inner_ref[1]), outer_ref)


def map2_kernel(side_ref, mid_ref, inner_ref, outer_ref, out_ref):
    goes = side_ref[2] == 1
    out_ref[0], out_ref[1] = composed(goes, (mid_ref[0], mid_ref[1]), outer_ref)
    out_ref[2], out_ref[3] = composed(goes, (inner_ref[0], inner_ref[1]), outer_ref)


def root_kernel(
    side_ref, inv_ref, mine_ref, other_ref, prop_ref, map_ref, mine_out, partner_out, mat
):
    on_left = side_ref[3] == 1
    lower = jnp.where(on_left, mine_ref[...], other_ref[...])
    diag_l = unpack(lower[:PACKED])
    link_l = wide(lower[PACKED:])
    prop = cmul(inv_ref[...], ctrans(link_l))
    mat[...] = diag_l - cmul(link_l, prop)
    (root,) = invert([mat])
    middle = cmul(prop, root)
    x_left = jnp.where(on_left, root, middle)
    x_right = jnp.where(on_left, middle, 0.0)
    inside_2 = cmul(prop_ref[0], x_left) + cmul(prop_ref[1], x_right)
    inside_1 = cmul(map_ref[0], x_left) + cmul(map_ref[1], x_right)
    inside = cmul(map_ref[2], x_left) + cmul(map_ref[3], x_right)
    for level, middle in ((2, inside_2), (1, inside_1)):
        goes = side_ref[level] == 1
        x_left, x_right = jnp.where(goes, x_left, middle), jnp.where(goes, middle, x_right)
    mine_out[0] = x_left
    mine_out[1] = inside
    partner_out[0] = inside
    partner_out[1] = x_right


def fold_kernel(prop_ref, out_ref):
    to_l, to_r = prop_ref[2], prop_ref[3]
    out_ref[0] = prop_ref[0] + cmul(prop_ref[1], to_l)
    out_ref[1] = cmul(prop_ref[1], to_r)
    out_ref[2] = to_l
    out_ref[3] = to_r
    out_ref[4] = cmul(prop_ref[4], to_l)
    out_ref[5] = prop_ref[5] + cmul(prop_ref[4], to_r)


def density_kernel(side_ref, weight_ref, mine_ref, got_ref, prop_ref, left_ref, density_ref):
    own = side_ref[0] == 1
    x_left = jnp.where(own, mine_ref[0], got_ref[0])
    x_right = jnp.where(own, mine_ref[1], got_ref[1])
    x_2 = cmul(prop_ref[2], x_left) + cmul(prop_ref[3], x_right)
    x_1 = cmul(prop_ref[0], x_left) + cmul(prop_ref[1], x_right)
    x_3 = cmul(prop_ref[4], x_left) + cmul(prop_ref[5], x_right)
    imag = left_ref[1]
    gamma = -(imag + imag.T)
    weight = weight_ref[0]
    stacked = jnp.concatenate([tall(x) for x in (x_left, x_1, x_2, x_3)], 0)
    terms = mul3(stacked, gamma) * stacked
    for s in range(density_ref.shape[1]):
        both = terms[2 * s * W : (2 * s + 1) * W] + terms[(2 * s + 1) * W : (2 * s + 2) * W]
        row = weight * jnp.sum(both.T, axis=0, keepdims=True)
        density_ref[:, s, :] = jnp.broadcast_to(row, (density_ref.shape[0], W))


def moments_kernel(parts_ref, current_ref, past_ref, total_ref, sums_ref):
    total = jnp.sum(parts_ref[...], axis=0)
    total_ref[...] = total
    residual = total - current_ref[...]
    count = past_ref.shape[0]
    diffs = [residual - past_ref[k] for k in range(count)]
    rows = []
    for k in range(count):
        for other in diffs[k:] + [residual]:
            rows.append(jnp.sum(diffs[k] * other, axis=0, keepdims=True))
    rows.append(jnp.zeros((W - len(rows), W), F32))
    sums = jnp.sum(jnp.concatenate(rows, 0).T, axis=0, keepdims=True)
    sums_ref[...] = jnp.broadcast_to(sums, sums_ref.shape)


def mix_kernel(sums_ref, total_ref, current_ref, density_ref, past_ref, next_ref):
    count = past_ref.shape[0]
    sums = jnp.sum(sums_ref[...], axis=0)[0:1]
    gram = {}
    place = 0
    for k in range(count):
        for other in range(k, count + 1):
            entry = jnp.broadcast_to(sums[:, place : place + 1], (1, W))
            gram[k, other] = entry
            if other < count:
                gram[other, k] = entry
            place += 1
    trace = gram[0, 0]
    for k in range(1, count):
        trace = trace + gram[k, k]
    ridge = RIDGE * trace / count
    for k in range(count):
        gram[k, k] = gram[k, k] + ridge
    for k in range(count):
        pivot = 1.0 / gram[k, k]
        for col in range(k + 1, count + 1):
            gram[k, col] = gram[k, col] * pivot
        for row in range(k + 1, count):
            for col in range(k + 1, count + 1):
                gram[row, col] = gram[row, col] - gram[row, k] * gram[k, col]
    mix = [None] * count
    for k in reversed(range(count)):
        value = gram[k, count]
        for col in range(k + 1, count):
            value = value - gram[k, col] * mix[col]
        mix[k] = value
    current = current_ref[...]
    residual = total_ref[...] - current
    out = current + MIX_BETA * residual
    for k in range(count):
        step = (current - density_ref[k]) + MIX_BETA * (residual - past_ref[k])
        out = out - mix[k] * step
    next_ref[...] = out


SMEM = pl.BlockSpec(memory_space=pltpu.SMEM)
VMEM = pl.BlockSpec(memory_space=pltpu.VMEM)
ANY = pl.BlockSpec(memory_space=pltpu.MemorySpace.HBM)
BLOCK = (W, 2 * W)
MAT = pltpu.VMEM(BLOCK, F32)
PACKED = W + 8
CRIT = (PACKED, W)
REST = (PACKED + 2 * W, W)
PART = (2 * PACKED + 2 * W, W)


def call(kernel, name, shapes, in_specs, scratch=(), micros=2):
    return pl.pallas_call(
        kernel,
        out_shape=[jax.ShapeDtypeStruct(s, F32) for s in shapes],
        in_specs=in_specs,
        out_specs=[VMEM] * len(shapes),
        scratch_shapes=list(scratch),
        compiler_params=pltpu.CompilerParams(vmem_limit_bytes=32 << 20),
        name=name,
        cost_estimate=pl.CostEstimate(
            flops=micros * 1000000000, transcendentals=0, bytes_accessed=micros * 3000000
        ),
        interpret=INTERPRET,
    )


GRID = 512
MIX_BETA = 0.3
RIDGE = 0.01


def in_hbm(array):
    return pltpu.with_memory_space_constraint(array, pltpu.MemorySpace.HBM)


def send(block, route):
    return lax.ppermute(block, "slab", route)


def on_device(onsite, coupling, potential, sigma_left, sigma_right, energy_index, density_in, hist_density, hist_residual):
    slab_count = lax.axis_size("slab")
    position = lax.axis_index("slab")
    per_dev = onsite.shape[0]
    energies_all = energy_index.shape[0] * lax.axis_size("energy")
    energy = -0.4 + 0.8 * (energy_index.astype(F32) + 0.5) / GRID
    weight = 4.0 / energies_all / (1.0 + jnp.exp(energy / 0.1))
    broaden = jnp.full((1,), 2.0 / (per_dev * slab_count), F32)
    ends = jnp.stack([position == 0, position == slab_count - 1]).astype(jnp.int32)
    sides = jnp.stack([(position // (1 << level)) % 2 == 0 for level in range(4)]).astype(jnp.int32)
    left, right = sigma_left[0], sigma_right[0]
    pair = (2,) + BLOCK
    part, local = call(
        local_kernel, "local", [PART, (6,) + BLOCK],
        [SMEM, SMEM, ANY, ANY, ANY, ANY, ANY],
        [
            pltpu.VMEM((per_dev, W, W), F32), pltpu.VMEM((per_dev, W, W), F32), pltpu.VMEM((per_dev, W), F32),
            pltpu.VMEM((2, W, W), F32), pltpu.VMEM((2, W, W), F32), MAT, MAT,
            pltpu.SemaphoreType.DMA((11,)),
        ],
    )(ends, jnp.concatenate([energy, broaden]), in_hbm(onsite), in_hbm(coupling), in_hbm(potential), in_hbm(left), in_hbm(right))
    evens = range(0, slab_count, 2)
    other = send(part, [(i + 1, i) for i in evens])
    (local,) = call(fold_kernel, "fold", [(6,) + BLOCK], [VMEM], micros=1)(local)
    other, local = lax.optimization_barrier((other, local))
    inv, first, crit = call(chip_kernel, "chip", [BLOCK, BLOCK, CRIT], [SMEM] + [VMEM] * 2, [MAT])(
        sides, part, other
    )
    route = [(i, i ^ 2) for i in evens]
    crit_other = send(crit, route)
    rest, prop = call(chip_rest_kernel, "chip_rest", [REST, pair], [SMEM] + [VMEM] * 4)(
        sides, inv, first, part, other
    )
    last = slab_count - 2
    props = [prop]
    for level in (1, 2):
        rest_other = send(rest, route)
        (inv,) = call(
            functools.partial(inverse_kernel, level), f"inverse{level}", [BLOCK], [SMEM, VMEM, VMEM], [MAT], 7
        )(sides, crit, crit_other)
        if level == 2:
            (inner,) = call(map1_kernel, "map1", [pair], [SMEM] + [VMEM] * 3, micros=1)(sides, *props, inv)
            rest_other, inner = lax.optimization_barrier((rest_other, inner))
        first, crit = call(
            functools.partial(crit_kernel, level), f"crit{level}", [BLOCK, CRIT], [SMEM] + [VMEM] * 3
        )(sides, inv, rest, rest_other)
        route = [(i, i ^ 4) for i in evens] if level == 1 else [(i, last - i) for i in evens]
        crit_other = send(crit, route)
        rest, prop = call(
            functools.partial(rest_kernel, level), f"rest{level}", [REST, pair], [SMEM] + [VMEM] * 4
        )(sides, inv, first, rest, rest_other)
        props.append(prop)
    rest_other = send(rest, [(i, last - i) for i in evens if i < last - i])
    (maps,) = call(map2_kernel, "map2", [(4,) + BLOCK], [SMEM] + [VMEM] * 3, micros=0)(
        sides, props[1], inner, props[2]
    )
    crit_other, maps = lax.optimization_barrier((crit_other, maps))
    (inv,) = call(
        functools.partial(inverse_kernel, 3), "inverse3", [BLOCK], [SMEM, VMEM, VMEM], [MAT], 7
    )(sides, crit, crit_other)
    mine, partner = call(root_kernel, "root", [pair, pair], [SMEM] + [VMEM] * 5, [MAT])(
        sides, inv, rest, rest_other, props[2], maps
    )
    got = send(partner, [(i, i + 1) for i in evens])
    (density,) = call(density_kernel, "density", [(lax.axis_size("energy"), per_dev, W)], [SMEM, SMEM] + [VMEM] * 4)(
        sides, weight, mine, got, local, left
    )
    density = lax.all_to_all(density, "energy", 0, 0)
    total, sums = call(
        moments_kernel, "moments", [(per_dev, W), (slab_count, 8, W)], [VMEM] * 3
    )(density, density_in, hist_residual)
    sums = lax.all_to_all(sums, "slab", 0, 0)
    (following,) = call(mix_kernel, "mix", [(per_dev, W)], [VMEM] * 5)(
        sums, total, density_in, hist_density, hist_residual
    )
    return (total, following)


def solution(mesh):
    in_specs = (
        P("slab", None, None),
        P("slab", None, None),
        P("slab", None),
        P("energy", None, None, None),
        P("energy", None, None, None),
        P("energy"),
        P("slab", None),
        P(None, "slab", None),
        P(None, "slab", None),
    )
    out_specs = (P("slab", None), P("slab", None))
    return jax.shard_map(
        on_device, mesh=mesh, in_specs=in_specs, out_specs=out_specs, check_vma=False
    )
```

```python
import functools

import jax
import jax.numpy as jnp
from jax import lax
from jax.experimental import pallas as pl
from jax.experimental.pallas import tpu as pltpu
from jax.sharding import PartitionSpec as P

INTERPRET = False
W = 128
PB = 16
ORDER = ((0, 0), (0, 1), (1, 0), (0, 2), (2, 0), (1, 1))
F32 = jnp.float32
BF16 = jnp.bfloat16


def dot(a, b):
    return jnp.dot(a, b, preferred_element_type=F32)


def dot_tn(a, b):
    return lax.dot_general(a, b, (((0,), (0,)), ((), ())), preferred_element_type=F32)


def split2(x):
    hi = x.astype(BF16)
    return hi, (x - hi.astype(F32)).astype(BF16)


def split3(x):
    hi = x.astype(BF16)
    rest = x - hi.astype(F32)
    mid = rest.astype(BF16)
    return hi, mid, (rest - mid.astype(F32)).astype(BF16)


def mul3(left, right):
    return split_product(split2(left), split2(right))


def split_product(left, right):
    lh, ll = left
    rh, rl = right
    rows = lh.shape[0]
    both = dot(jnp.concatenate([lh, ll], 0), rh)
    return both[:rows] + (both[rows:] + dot(lh, rl))


def as_right(x):
    return jnp.concatenate([x, jnp.concatenate([-x[:, W:], x[:, :W]], 1)], 0)


def cmul(left, right):
    rh, rl = split2(right)
    return split_product(split2(left), (as_right(rh), as_right(rl)))


def ctrans(x):
    return jnp.concatenate([x[:, :W].T, x[:, W:].T], 1)


def sweep_panels(mats):
    lane = lax.broadcasted_iota(jnp.int32, (8, W), 1)
    row = lax.broadcasted_iota(jnp.int32, (8, W), 0)
    keep = lax.broadcasted_iota(jnp.int32, (W - PB, W), 1) < W - PB

    groups = PB // 8

    def spread(parts, j):
        return {
            g: jnp.broadcast_to(jnp.sum(jnp.where(lane == j, p, 0.0), axis=1, keepdims=True), (8, W))
            for g, p in parts.items()
        }

    def eliminate(cols_r, cols_i, k, active, all_live):
        gk, rk = divmod(k, 8)
        here = row == rk
        mult_r, mult_i = cols_r[k], cols_i[k]
        piv_r = jnp.broadcast_to(mult_r[gk][rk : rk + 1], (8, W))
        piv_i = jnp.broadcast_to(mult_i[gk][rk : rk + 1], (8, W))
        den = 1.0 / (piv_r * piv_r + piv_i * piv_i)
        inv_r = piv_r * den
        inv_i = -piv_i * den
        fr, fi = {}, {}
        for g in all_live:
            a = mult_r[g] * inv_r - mult_i[g] * inv_i
            b = mult_r[g] * inv_i + mult_i[g] * inv_r
            if g == gk:
                a = jnp.where(here, -inv_r, a)
                b = jnp.where(here, -inv_i, b)
            fr[g], fi[g] = a, b
        at = lane == W - PB + k
        for j in active:
            xr, xi = cols_r[j], cols_i[j]
            row_r, row_i = (xr[gk], xi[gk]) if gk in xr else (mult_r[j // 8], mult_i[j // 8])
            rj = rk if gk in xr else j % 8
            row_r = jnp.broadcast_to(row_r[rj : rj + 1], (8, W))
            row_i = jnp.broadcast_to(row_i[rj : rj + 1], (8, W))
            new_r, new_i = dict(xr), dict(xi)
            for g in (g for g in all_live if g in xr):
                br, bi = xr[g], xi[g]
                if g == gk:
                    br = jnp.where(here, 0.0, br)
                    bi = jnp.where(here, 0.0, bi)
                nr = br - (fr[g] * row_r - fi[g] * row_i)
                ni = bi - (fr[g] * row_i + fi[g] * row_r)
                if j == "w":
                    nr, ni = jnp.where(at, fr[g], nr), jnp.where(at, fi[g], ni)
                new_r[g], new_i[g] = nr, ni
            cols_r[j], cols_i[j] = new_r, new_i

    def panel(_, carry):
        state = []
        for ref in mats:
            pr = {g: ref[8 * g : 8 * g + 8, :W] for g in range(groups)}
            pi = {g: ref[8 * g : 8 * g + 8, W:] for g in range(groups)}
            cols_r = {j: spread(pr, j) for j in range(8)}
            cols_i = {j: spread(pi, j) for j in range(8)}
            if len(mats) == 1:
                for j in range(8, PB):
                    below = range(j // 8, groups)
                    cols_r[j] = spread({g: pr[g] for g in below}, j)
                    cols_i[j] = spread({g: pi[g] for g in below}, j)
            cols_r["w"] = {g: pltpu.roll(p, W - PB, 1) for g, p in pr.items()}
            cols_i["w"] = {g: pltpu.roll(p, W - PB, 1) for g, p in pi.items()}
            state.append((cols_r, cols_i, [], []))
        for s in range(groups):
            edge = W - PB + 8 * s
            unit = jnp.where(lane == edge + row, -1.0, 0.0)
            for cols_r, cols_i, left_r, left_i in state:
                left_r.append(jnp.where(lane < edge, cols_r["w"][s], unit))
                left_i.append(jnp.where(lane < edge, cols_i["w"][s], 0.0))
                if s and len(mats) > 1:
                    for cols in (cols_r, cols_i):
                        below = {g: cols["w"][g] for g in range(s, groups)}
                        for j in range(8 * s, 8 * s + 8):
                            cols[j] = spread(below, W - PB + j)
            for k in range(8 * s, 8 * s + 8):
                own = range(k + 1, 8 * s + 8)
                later = range(8 * s + 8, PB) if len(mats) == 1 else ()
                for cols_r, cols_i, _, _ in state:
                    eliminate(cols_r, cols_i, k, [*own, *later, "w"], range(s, groups))
            for cols_r, cols_i, _, _ in state:
                for cols in (cols_r, cols_i):
                    cols["w"][s] = jnp.where(lane < edge + 8, cols["w"][s], 0.0)
        for ref, (cols_r, cols_i, left_r, left_i) in zip(mats, state):
            pieces_p = split3(jnp.concatenate(left_r + left_i, 0))
            wr = jnp.concatenate([cols_r["w"][g] for g in range(groups)], 0)
            wi = jnp.concatenate([cols_i["w"][g] for g in range(groups)], 0)
            pieces_w = [
                jnp.concatenate([jnp.concatenate([r, i], 1), jnp.concatenate([-i, r], 1)], 0)
                for r, i in zip(split3(wr), split3(wi))
            ]
            lhs = jnp.concatenate([pieces_p[a] for a, _ in ORDER], 0)
            rhs = jnp.concatenate([pieces_w[b] for _, b in ORDER], 0)
            update = dot_tn(lhs, rhs)
            old_r = jnp.where(keep, pltpu.roll(ref[PB:, :W], W - PB, 1), 0.0)
            old_i = jnp.where(keep, pltpu.roll(ref[PB:, W:], W - PB, 1), 0.0)
            ref[: W - PB, :W] = old_r - update[: W - PB, :W]
            ref[: W - PB, W:] = old_i - update[: W - PB, W:]
            ref[W - PB :, :] = -update[W - PB :, :]
        return carry

    lax.fori_loop(0, W // PB, panel, 0)


def invert(refs):
    sweep_panels(refs)
    return [-ref[...] for ref in refs]


def triangles():
    row = lax.broadcasted_iota(jnp.int32, (W, W), 0)
    col = lax.broadcasted_iota(jnp.int32, (W, W), 1)
    return row, col


def pack(x):
    row, col = triangles()
    real, imag = x[:, :W], x[:, W:]
    tip = jnp.sum(jnp.where(row == col, imag, 0.0), axis=0, keepdims=True)
    return jnp.concatenate([jnp.where(row <= col, real, imag), jnp.broadcast_to(tip, (8, W))], 0)


def unpack(packed):
    row, col = triangles()
    body = packed[:W]
    turned = body.T
    imag = jnp.where(row == col, packed[W : W + 1], turned)
    return jnp.concatenate(
        [jnp.where(row <= col, body, turned), jnp.where(row > col, body, imag)], 1
    )


def tall(x):
    return jnp.concatenate([x[:, :W], x[:, W:]], 0)


def wide(x):
    return jnp.concatenate([x[:W], x[W:]], 1)


def real_right(inv, real):
    out = mul3(jnp.concatenate([inv[:, :W], inv[:, W:]], 0), real)
    return jnp.concatenate([out[:W], out[W:]], 1)


def local_kernel(
    flag_ref, energy_ref, onsite_hbm, coupling_hbm, potential_hbm, left_hbm, right_hbm,
    part_ref, prop_ref,
    onsite_ref, coupling_ref, potential_ref, left_ref, right_ref, mat_a, mat_b, sems,
):
    is_first = flag_ref[0] == 1
    is_last = flag_ref[1] == 1
    energy = energy_ref[0]
    copies = []

    def fetch(src, dst):
        copy = pltpu.make_async_copy(src, dst, sems.at[len(copies)])
        copy.start()
        copies.append(copy)
        return copy

    potential_copy = fetch(potential_hbm, potential_ref)
    onsite_copy = {s: fetch(onsite_hbm.at[s], onsite_ref.at[s]) for s in (1, 3)}
    right_copy = fetch(right_hbm, right_ref)
    coupling_copy = [fetch(coupling_hbm.at[s], coupling_ref.at[s]) for s in range(4)]
    onsite_copy.update({s: fetch(onsite_hbm.at[s], onsite_ref.at[s]) for s in (2, 0)})
    left_copy = fetch(left_hbm, left_ref)
    eye = lax.broadcasted_iota(jnp.int32, (W, W), 0) == lax.broadcasted_iota(jnp.int32, (W, W), 1)
    broaden = jnp.where(eye, energy_ref[1], 0.0)

    def diagonal(s):
        onsite_copy[s].wait()
        real = jnp.where(eye, energy - potential_ref[s : s + 1, :], 0.0) - onsite_ref[s]
        return jnp.concatenate([real, broaden], 1)

    potential_copy.wait()
    mat_a[...] = diagonal(1)
    diag_3 = diagonal(3)
    right_copy.wait()
    last = jnp.concatenate([right_ref[0], right_ref[1]], 1)
    mat_b[...] = diag_3 - jnp.where(is_last, last, 0.0)
    inv_1, inv_3 = invert([mat_a, mat_b])
    for copy in coupling_copy:
        copy.wait()
    c0, c1, c2 = coupling_ref[0], coupling_ref[1], coupling_ref[2]
    c3 = jnp.where(is_last, 0.0, coupling_ref[3])
    prop_1r = real_right(inv_1, c1)
    prop_3l = real_right(inv_3, c2.T)
    prop_1l = real_right(inv_1, c0.T)
    prop_3r = real_right(inv_3, c3)
    mat_a[...] = diagonal(2) - mul3(c1.T, prop_1r) - mul3(c2, prop_3l)
    diag_0 = diagonal(0)
    left_copy.wait()
    first = jnp.concatenate([left_ref[0], left_ref[1]], 1)
    top = diag_0 - jnp.where(is_first, first, 0.0) - mul3(c0, prop_1l)
    nxt = mul3(c3.T, prop_3r)
    k02 = mul3(c0, prop_1r)
    k2n = mul3(c2, prop_3r)
    k02_t, k2n_t = ctrans(k02), ctrans(k2n)
    (inv_2,) = invert([mat_a])
    prop_2l = cmul(inv_2, k02_t)
    prop_2r = cmul(inv_2, k2n)
    part_ref[:PACKED] = pack(top - cmul(k02, prop_2l))
    part_ref[PACKED : 2 * PACKED] = pack(nxt + cmul(k2n_t, prop_2r))
    part_ref[2 * PACKED :] = tall(cmul(k02, prop_2r))
    for n, prop in enumerate((prop_1l, prop_1r, prop_2l, prop_2r, prop_3l, prop_3r)):
        prop_ref[n] = prop


def facing(link_l, link_r, to_right):
    plain = jnp.where(to_right, link_r, link_l)
    turned = ctrans(plain)
    return jnp.where(to_right, plain, turned), jnp.where(to_right, turned, plain)


def urgent(inv, link_l, link_r, base, goes_left):
    side, side_t = facing(link_l, link_r, goes_left)
    prop = cmul(inv, side)
    change = cmul(side_t, prop)
    return prop, pack(unpack(base) + jnp.where(goes_left, change, -change))


def others(inv, prop, link_l, link_r, base, goes_left, rest_ref, prop_ref):
    side, side_t = facing(link_l, link_r, jnp.logical_not(goes_left))
    second = cmul(inv, side)
    change = cmul(side_t, second)
    prop_r = jnp.where(goes_left, prop, second)
    rest_ref[:PACKED] = pack(unpack(base) + jnp.where(goes_left, -change, change))
    rest_ref[PACKED:] = tall(cmul(link_l, prop_r))
    prop_ref[0] = jnp.where(goes_left, second, prop)
    prop_ref[1] = prop_r


def chip_sides(side_ref, mine_ref, other_ref):
    goes_left = side_ref[1] == 1
    diag_l = mine_ref[:PACKED]
    next_r = other_ref[PACKED : 2 * PACKED]
    links = wide(mine_ref[2 * PACKED :]), wide(other_ref[2 * PACKED :])
    return links, (diag_l, next_r), goes_left


def chip_kernel(side_ref, mine_ref, other_ref, inv_ref, first_ref, crit_ref, mat):
    mat[...] = unpack(other_ref[:PACKED] - mine_ref[PACKED : 2 * PACKED])
    (inv,) = invert([mat])
    inv_ref[...] = inv
    links, (diag_l, next_r), goes_left = chip_sides(side_ref, mine_ref, other_ref)
    first_ref[...], crit_ref[...] = urgent(inv, *links, jnp.where(goes_left, next_r, diag_l), goes_left)


def chip_rest_kernel(side_ref, inv_ref, first_ref, mine_ref, other_ref, rest_ref, prop_ref):
    links, (diag_l, next_r), goes_left = chip_sides(side_ref, mine_ref, other_ref)
    others(
        inv_ref[...], first_ref[...], *links, jnp.where(goes_left, diag_l, next_r), goes_left,
        rest_ref, prop_ref,
    )


def inverse_kernel(level, side_ref, mine_ref, other_ref, inv_ref, mat):
    mine, other = mine_ref[...], other_ref[...]
    mat[...] = unpack(jnp.where(side_ref[level] == 1, other - mine, mine - other))
    (inv_ref[...],) = invert([mat])


def both_sides(level, side_ref, mine_ref, other_ref):
    on_left = side_ref[level] == 1
    mine, other = mine_ref[...], other_ref[...]
    left, right = jnp.where(on_left, mine, other), jnp.where(on_left, other, mine)
    links = wide(left[PACKED:]), wide(right[PACKED:])
    return links, (left[:PACKED], right[:PACKED]), side_ref[level + 1] == 1


def crit_kernel(level, side_ref, inv_ref, mine_ref, other_ref, first_ref, crit_ref):
    links, (diag_l, next_r), goes_left = both_sides(level, side_ref, mine_ref, other_ref)
    first_ref[...], crit_ref[...] = urgent(
        inv_ref[...], *links, jnp.where(goes_left, next_r, diag_l), goes_left
    )


def rest_kernel(level, side_ref, inv_ref, first_ref, mine_ref, other_ref, rest_ref, prop_ref):
    links, (diag_l, next_r), goes_left = both_sides(level, side_ref, mine_ref, other_ref)
    others(
        inv_ref[...], first_ref[...], *links, jnp.where(goes_left, diag_l, next_r), goes_left,
        rest_ref, prop_ref,
    )


def composed(goes_left, inner, outer):
    near, far = inner
    through = jnp.where(goes_left, far, near)
    return (
        cmul(through, outer[0]) + jnp.where(goes_left, near, 0.0),
        cmul(through, outer[1]) + jnp.where(goes_left, 0.0, far),
    )


def map1_kernel(side_ref, inner_ref, outer_ref, after_ref, out_ref):
    goes = side_ref[1] == 1
    out_ref[0], out_ref[1] = composed(goes, (inner_ref[0], inner_ref[1]), outer_ref)


def map2_kernel(side_ref, mid_ref, inner_ref, outer_ref, out_ref):
    goes = side_ref[2] == 1
    out_ref[0], out_ref[1] = composed(goes, (mid_ref[0], mid_ref[1]), outer_ref)
    out_ref[2], out_ref[3] = composed(goes, (inner_ref[0], inner_ref[1]), outer_ref)


def root_kernel(
    side_ref, inv_ref, mine_ref, other_ref, prop_ref, map_ref, mine_out, partner_out, mat
):
    on_left = side_ref[3] == 1
    lower = jnp.where(on_left, mine_ref[...], other_ref[...])
    diag_l = unpack(lower[:PACKED])
    link_l = wide(lower[PACKED:])
    prop = cmul(inv_ref[...], ctrans(link_l))
    mat[...] = diag_l - cmul(link_l, prop)
    (root,) = invert([mat])
    middle = cmul(prop, root)
    x_left = jnp.where(on_left, root, middle)
    x_right = jnp.where(on_left, middle, 0.0)
    inside_2 = cmul(prop_ref[0], x_left) + cmul(prop_ref[1], x_right)
    inside_1 = cmul(map_ref[0], x_left) + cmul(map_ref[1], x_right)
    inside = cmul(map_ref[2], x_left) + cmul(map_ref[3], x_right)
    for level, middle in ((2, inside_2), (1, inside_1)):
        goes = side_ref[level] == 1
        x_left, x_right = jnp.where(goes, x_left, middle), jnp.where(goes, middle, x_right)
    mine_out[0] = x_left
    mine_out[1] = inside
    partner_out[0] = inside
    partner_out[1] = x_right


def fold_kernel(prop_ref, out_ref):
    to_l, to_r = prop_ref[2], prop_ref[3]
    out_ref[0] = prop_ref[0] + cmul(prop_ref[1], to_l)
    out_ref[1] = cmul(prop_ref[1], to_r)
    out_ref[2] = to_l
    out_ref[3] = to_r
    out_ref[4] = cmul(prop_ref[4], to_l)
    out_ref[5] = prop_ref[5] + cmul(prop_ref[4], to_r)


def density_kernel(side_ref, weight_ref, mine_ref, got_ref, prop_ref, left_ref, density_ref):
    own = side_ref[0] == 1
    x_left = jnp.where(own, mine_ref[0], got_ref[0])
    x_right = jnp.where(own, mine_ref[1], got_ref[1])
    x_2 = cmul(prop_ref[2], x_left) + cmul(prop_ref[3], x_right)
    x_1 = cmul(prop_ref[0], x_left) + cmul(prop_ref[1], x_right)
    x_3 = cmul(prop_ref[4], x_left) + cmul(prop_ref[5], x_right)
    imag = left_ref[1]
    gamma = -(imag + imag.T)
    weight = weight_ref[0]
    stacked = jnp.concatenate([tall(x) for x in (x_left, x_1, x_2, x_3)], 0)
    terms = mul3(stacked, gamma) * stacked
    for s in range(density_ref.shape[1]):
        both = terms[2 * s * W : (2 * s + 1) * W] + terms[(2 * s + 1) * W : (2 * s + 2) * W]
        row = weight * jnp.sum(both.T, axis=0, keepdims=True)
        density_ref[:, s, :] = jnp.broadcast_to(row, (density_ref.shape[0], W))


def moments_kernel(parts_ref, current_ref, past_ref, total_ref, sums_ref):
    total = jnp.sum(parts_ref[...], axis=0)
    total_ref[...] = total
    residual = total - current_ref[...]
    count = past_ref.shape[0]
    diffs = [residual - past_ref[k] for k in range(count)]
    rows = []
    for k in range(count):
        for other in diffs[k:] + [residual]:
            rows.append(jnp.sum(diffs[k] * other, axis=0, keepdims=True))
    rows.append(jnp.zeros((W - len(rows), W), F32))
    sums = jnp.sum(jnp.concatenate(rows, 0).T, axis=0, keepdims=True)
    sums_ref[...] = jnp.broadcast_to(sums, sums_ref.shape)


def mix_kernel(sums_ref, total_ref, current_ref, density_ref, past_ref, next_ref):
    count = past_ref.shape[0]
    sums = jnp.sum(sums_ref[...], axis=0)[0:1]
    gram = {}
    place = 0
    for k in range(count):
        for other in range(k, count + 1):
            entry = jnp.broadcast_to(sums[:, place : place + 1], (1, W))
            gram[k, other] = entry
            if other < count:
                gram[other, k] = entry
            place += 1
    trace = gram[0, 0]
    for k in range(1, count):
        trace = trace + gram[k, k]
    ridge = RIDGE * trace / count
    for k in range(count):
        gram[k, k] = gram[k, k] + ridge
    for k in range(count):
        pivot = 1.0 / gram[k, k]
        for col in range(k + 1, count + 1):
            gram[k, col] = gram[k, col] * pivot
        for row in range(k + 1, count):
            for col in range(k + 1, count + 1):
                gram[row, col] = gram[row, col] - gram[row, k] * gram[k, col]
    mix = [None] * count
    for k in reversed(range(count)):
        value = gram[k, count]
        for col in range(k + 1, count):
            value = value - gram[k, col] * mix[col]
        mix[k] = value
    current = current_ref[...]
    residual = total_ref[...] - current
    out = current + MIX_BETA * residual
    for k in range(count):
        step = (current - density_ref[k]) + MIX_BETA * (residual - past_ref[k])
        out = out - mix[k] * step
    next_ref[...] = out


SMEM = pl.BlockSpec(memory_space=pltpu.SMEM)
VMEM = pl.BlockSpec(memory_space=pltpu.VMEM)
ANY = pl.BlockSpec(memory_space=pltpu.MemorySpace.HBM)
BLOCK = (W, 2 * W)
MAT = pltpu.VMEM(BLOCK, F32)
PACKED = W + 8
CRIT = (PACKED, W)
REST = (PACKED + 2 * W, W)
PART = (2 * PACKED + 2 * W, W)


def call(kernel, name, shapes, in_specs, scratch=(), micros=2):
    return pl.pallas_call(
        kernel,
        out_shape=[jax.ShapeDtypeStruct(s, F32) for s in shapes],
        in_specs=in_specs,
        out_specs=[VMEM] * len(shapes),
        scratch_shapes=list(scratch),
        compiler_params=pltpu.CompilerParams(vmem_limit_bytes=32 << 20),
        name=name,
        cost_estimate=pl.CostEstimate(
            flops=micros * 1000000000, transcendentals=0, bytes_accessed=micros * 3000000
        ),
        interpret=INTERPRET,
    )


GRID = 512
MIX_BETA = 0.3
RIDGE = 0.01


def in_hbm(array):
    return pltpu.with_memory_space_constraint(array, pltpu.MemorySpace.HBM)


def send(block, route):
    return lax.ppermute(block, "slab", route)


def on_device(onsite, coupling, potential, sigma_left, sigma_right, energy_index, density_in, hist_density, hist_residual):
    slab_count = lax.axis_size("slab")
    position = lax.axis_index("slab")
    per_dev = onsite.shape[0]
    energies_all = energy_index.shape[0] * lax.axis_size("energy")
    energy = -0.4 + 0.8 * (energy_index.astype(F32) + 0.5) / GRID
    weight = 4.0 / energies_all / (1.0 + jnp.exp(energy / 0.1))
    broaden = jnp.full((1,), 2.0 / (per_dev * slab_count), F32)
    ends = jnp.stack([position == 0, position == slab_count - 1]).astype(jnp.int32)
    sides = jnp.stack([(position // (1 << level)) % 2 == 0 for level in range(4)]).astype(jnp.int32)
    left, right = sigma_left[0], sigma_right[0]
    pair = (2,) + BLOCK
    part, local = call(
        local_kernel, "local", [PART, (6,) + BLOCK],
        [SMEM, SMEM, ANY, ANY, ANY, ANY, ANY],
        [
            pltpu.VMEM((per_dev, W, W), F32), pltpu.VMEM((per_dev, W, W), F32), pltpu.VMEM((per_dev, W), F32),
            pltpu.VMEM((2, W, W), F32), pltpu.VMEM((2, W, W), F32), MAT, MAT,
            pltpu.SemaphoreType.DMA((11,)),
        ],
    )(ends, jnp.concatenate([energy, broaden]), in_hbm(onsite), in_hbm(coupling), in_hbm(potential), in_hbm(left), in_hbm(right))
    evens = range(0, slab_count, 2)
    other = send(part, [(i + 1, i) for i in evens])
    (local,) = call(fold_kernel, "fold", [(6,) + BLOCK], [VMEM], micros=1)(local)
    other, local = lax.optimization_barrier((other, local))
    inv, first, crit = call(chip_kernel, "chip", [BLOCK, BLOCK, CRIT], [SMEM] + [VMEM] * 2, [MAT])(
        sides, part, other
    )
    route = [(i, i ^ 2) for i in evens]
    crit_other = send(crit, route)
    rest, prop = call(chip_rest_kernel, "chip_rest", [REST, pair], [SMEM] + [VMEM] * 4)(
        sides, inv, first, part, other
    )
    last = slab_count - 2
    props = [prop]
    for level in (1, 2):
        rest_other = send(rest, route)
        (inv,) = call(
            functools.partial(inverse_kernel, level), f"inverse{level}", [BLOCK], [SMEM, VMEM, VMEM], [MAT], 7
        )(sides, crit, crit_other)
        if level == 2:
            (inner,) = call(map1_kernel, "map1", [pair], [SMEM] + [VMEM] * 3, micros=1)(sides, *props, inv)
            rest_other, inner = lax.optimization_barrier((rest_other, inner))
        first, crit = call(
            functools.partial(crit_kernel, level), f"crit{level}", [BLOCK, CRIT], [SMEM] + [VMEM] * 3
        )(sides, inv, rest, rest_other)
        route = [(i, i ^ 4) for i in evens] if level == 1 else [(i, last - i) for i in evens]
        crit_other = send(crit, route)
        rest, prop = call(
            functools.partial(rest_kernel, level), f"rest{level}", [REST, pair], [SMEM] + [VMEM] * 4
        )(sides, inv, first, rest, rest_other)
        props.append(prop)
    rest_other = send(rest, [(i, last - i) for i in evens if i < last - i])
    (maps,) = call(map2_kernel, "map2", [(4,) + BLOCK], [SMEM] + [VMEM] * 3, micros=0)(
        sides, props[1], inner, props[2]
    )
    crit_other, maps = lax.optimization_barrier((crit_other, maps))
    (inv,) = call(
        functools.partial(inverse_kernel, 3), "inverse3", [BLOCK], [SMEM, VMEM, VMEM], [MAT], 7
    )(sides, crit, crit_other)
    mine, partner = call(root_kernel, "root", [pair, pair], [SMEM] + [VMEM] * 5, [MAT])(
        sides, inv, rest, rest_other, props[2], maps
    )
    got = send(partner, [(i, i + 1) for i in evens])
    (density,) = call(density_kernel, "density", [(lax.axis_size("energy"), per_dev, W)], [SMEM, SMEM] + [VMEM] * 4)(
        sides, weight, mine, got, local, left
    )
    density = lax.all_to_all(density, "energy", 0, 0)
    total, sums = call(
        moments_kernel, "moments", [(per_dev, W), (slab_count, 8, W)], [VMEM] * 3
    )(density, density_in, hist_residual)
    sums = lax.all_to_all(sums, "slab", 0, 0)
    (following,) = call(mix_kernel, "mix", [(per_dev, W)], [VMEM] * 5)(
        sums, total, density_in, hist_density, hist_residual
    )
    return (total, following)


def solution(mesh):
    in_specs = (
        P("slab", None, None),
        P("slab", None, None),
        P("slab", None),
        P("energy", None, None, None),
        P("energy", None, None, None),
        P("energy"),
        P("slab", None),
        P(None, "slab", None),
        P(None, "slab", None),
    )
    out_specs = (P("slab", None), P("slab", None))
    return jax.shard_map(
        on_device, mesh=mesh, in_specs=in_specs, out_specs=out_specs, check_vma=False
    )
```

```python
import functools

import jax
import jax.numpy as jnp
from jax import lax
from jax.experimental import pallas as pl
from jax.experimental.pallas import tpu as pltpu
from jax.sharding import PartitionSpec as P

INTERPRET = False
W = 128
PB = 16
ORDER = ((0, 0), (0, 1), (1, 0), (0, 2), (2, 0), (1, 1))
F32 = jnp.float32
BF16 = jnp.bfloat16


def dot(a, b):
    return jnp.dot(a, b, preferred_element_type=F32)


def dot_tn(a, b):
    return lax.dot_general(a, b, (((0,), (0,)), ((), ())), preferred_element_type=F32)


def split2(x):
    hi = x.astype(BF16)
    return hi, (x - hi.astype(F32)).astype(BF16)


def split3(x):
    hi = x.astype(BF16)
    rest = x - hi.astype(F32)
    mid = rest.astype(BF16)
    return hi, mid, (rest - mid.astype(F32)).astype(BF16)


def mul3(left, right):
    return split_product(split2(left), split2(right))


def split_product(left, right):
    lh, ll = left
    rh, rl = right
    rows = lh.shape[0]
    both = dot(jnp.concatenate([lh, ll], 0), rh)
    return both[:rows] + (both[rows:] + dot(lh, rl))


def as_right(x):
    return jnp.concatenate([x, jnp.concatenate([-x[:, W:], x[:, :W]], 1)], 0)


def cmul(left, right):
    rh, rl = split2(right)
    return split_product(split2(left), (as_right(rh), as_right(rl)))


def ctrans(x):
    return jnp.concatenate([x[:, :W].T, x[:, W:].T], 1)


def sweep_panels(mats):
    lane = lax.broadcasted_iota(jnp.int32, (8, W), 1)
    row = lax.broadcasted_iota(jnp.int32, (8, W), 0)
    keep = lax.broadcasted_iota(jnp.int32, (W - PB, W), 1) < W - PB

    groups = PB // 8

    def spread(parts, j):
        return {
            g: jnp.broadcast_to(jnp.sum(jnp.where(lane == j, p, 0.0), axis=1, keepdims=True), (8, W))
            for g, p in parts.items()
        }

    def eliminate(cols_r, cols_i, k, active, all_live):
        gk, rk = divmod(k, 8)
        here = row == rk
        mult_r, mult_i = cols_r[k], cols_i[k]
        piv_r = jnp.broadcast_to(mult_r[gk][rk : rk + 1], (8, W))
        piv_i = jnp.broadcast_to(mult_i[gk][rk : rk + 1], (8, W))
        den = 1.0 / (piv_r * piv_r + piv_i * piv_i)
        inv_r = piv_r * den
        inv_i = -piv_i * den
        fr, fi = {}, {}
        for g in all_live:
            a = mult_r[g] * inv_r - mult_i[g] * inv_i
            b = mult_r[g] * inv_i + mult_i[g] * inv_r
            if g == gk:
                a = jnp.where(here, -inv_r, a)
                b = jnp.where(here, -inv_i, b)
            fr[g], fi[g] = a, b
        at = lane == W - PB + k
        for j in active:
            xr, xi = cols_r[j], cols_i[j]
            row_r, row_i = (xr[gk], xi[gk]) if gk in xr else (mult_r[j // 8], mult_i[j // 8])
            rj = rk if gk in xr else j % 8
            row_r = jnp.broadcast_to(row_r[rj : rj + 1], (8, W))
            row_i = jnp.broadcast_to(row_i[rj : rj + 1], (8, W))
            new_r, new_i = dict(xr), dict(xi)
            for g in (g for g in all_live if g in xr):
                br, bi = xr[g], xi[g]
                if g == gk:
                    br = jnp.where(here, 0.0, br)
                    bi = jnp.where(here, 0.0, bi)
                nr = br - (fr[g] * row_r - fi[g] * row_i)
                ni = bi - (fr[g] * row_i + fi[g] * row_r)
                if j == "w":
                    nr, ni = jnp.where(at, fr[g], nr), jnp.where(at, fi[g], ni)
                new_r[g], new_i[g] = nr, ni
            cols_r[j], cols_i[j] = new_r, new_i

    def panel(_, carry):
        state = []
        for ref in mats:
            pr = {g: ref[8 * g : 8 * g + 8, :W] for g in range(groups)}
            pi = {g: ref[8 * g : 8 * g + 8, W:] for g in range(groups)}
            cols_r = {j: spread(pr, j) for j in range(8)}
            cols_i = {j: spread(pi, j) for j in range(8)}
            if len(mats) == 1:
                for j in range(8, PB):
                    below = range(j // 8, groups)
                    cols_r[j] = spread({g: pr[g] for g in below}, j)
                    cols_i[j] = spread({g: pi[g] for g in below}, j)
            cols_r["w"] = {g: pltpu.roll(p, W - PB, 1) for g, p in pr.items()}
            cols_i["w"] = {g: pltpu.roll(p, W - PB, 1) for g, p in pi.items()}
            state.append((cols_r, cols_i, [], []))
        for s in range(groups):
            edge = W - PB + 8 * s
            unit = jnp.where(lane == edge + row, -1.0, 0.0)
            for cols_r, cols_i, left_r, left_i in state:
                left_r.append(jnp.where(lane < edge, cols_r["w"][s], unit))
                left_i.append(jnp.where(lane < edge, cols_i["w"][s], 0.0))
                if s and len(mats) > 1:
                    for cols in (cols_r, cols_i):
                        below = {g: cols["w"][g] for g in range(s, groups)}
                        for j in range(8 * s, 8 * s + 8):
                            cols[j] = spread(below, W - PB + j)
            for k in range(8 * s, 8 * s + 8):
                own = range(k + 1, 8 * s + 8)
                later = range(8 * s + 8, PB) if len(mats) == 1 else ()
                for cols_r, cols_i, _, _ in state:
                    eliminate(cols_r, cols_i, k, [*own, *later, "w"], range(s, groups))
            for cols_r, cols_i, _, _ in state:
                for cols in (cols_r, cols_i):
                    cols["w"][s] = jnp.where(lane < edge + 8, cols["w"][s], 0.0)
        for ref, (cols_r, cols_i, left_r, left_i) in zip(mats, state):
            pieces_p = split3(jnp.concatenate(left_r + left_i, 0))
            wr = jnp.concatenate([cols_r["w"][g] for g in range(groups)], 0)
            wi = jnp.concatenate([cols_i["w"][g] for g in range(groups)], 0)
            pieces_w = [
                jnp.concatenate([jnp.concatenate([r, i], 1), jnp.concatenate([-i, r], 1)], 0)
                for r, i in zip(split3(wr), split3(wi))
            ]
            lhs = jnp.concatenate([pieces_p[a] for a, _ in ORDER], 0)
            rhs = jnp.concatenate([pieces_w[b] for _, b in ORDER], 0)
            update = dot_tn(lhs, rhs)
            old_r = jnp.where(keep, pltpu.roll(ref[PB:, :W], W - PB, 1), 0.0)
            old_i = jnp.where(keep, pltpu.roll(ref[PB:, W:], W - PB, 1), 0.0)
            ref[: W - PB, :W] = old_r - update[: W - PB, :W]
            ref[: W - PB, W:] = old_i - update[: W - PB, W:]
            ref[W - PB :, :] = -update[W - PB :, :]
        return carry

    lax.fori_loop(0, W // PB, panel, 0)


def invert(refs):
    sweep_panels(refs)
    return [-ref[...] for ref in refs]


def triangles():
    row = lax.broadcasted_iota(jnp.int32, (W, W), 0)
    col = lax.broadcasted_iota(jnp.int32, (W, W), 1)
    return row, col


def pack(x):
    row, col = triangles()
    real, imag = x[:, :W], x[:, W:]
    tip = jnp.sum(jnp.where(row == col, imag, 0.0), axis=0, keepdims=True)
    return jnp.concatenate([jnp.where(row <= col, real, imag), jnp.broadcast_to(tip, (8, W))], 0)


def unpack(packed):
    row, col = triangles()
    body = packed[:W]
    turned = body.T
    imag = jnp.where(row == col, packed[W : W + 1], turned)
    return jnp.concatenate(
        [jnp.where(row <= col, body, turned), jnp.where(row > col, body, imag)], 1
    )


def tall(x):
    return jnp.concatenate([x[:, :W], x[:, W:]], 0)


def wide(x):
    return jnp.concatenate([x[:W], x[W:]], 1)


def real_right(inv, real):
    out = mul3(jnp.concatenate([inv[:, :W], inv[:, W:]], 0), real)
    return jnp.concatenate([out[:W], out[W:]], 1)


def local_kernel(
    flag_ref, energy_ref, onsite_hbm, coupling_hbm, potential_hbm, left_hbm, right_hbm,
    part_ref, prop_ref,
    onsite_ref, coupling_ref, potential_ref, left_ref, right_ref, mat_a, mat_b, sems,
):
    is_first = flag_ref[0] == 1
    is_last = flag_ref[1] == 1
    energy = energy_ref[0]
    copies = []

    def fetch(src, dst):
        copy = pltpu.make_async_copy(src, dst, sems.at[len(copies)])
        copy.start()
        copies.append(copy)
        return copy

    potential_copy = fetch(potential_hbm, potential_ref)
    onsite_copy = {s: fetch(onsite_hbm.at[s], onsite_ref.at[s]) for s in (1, 3)}
    right_copy = fetch(right_hbm, right_ref)
    coupling_copy = [fetch(coupling_hbm.at[s], coupling_ref.at[s]) for s in range(4)]
    onsite_copy.update({s: fetch(onsite_hbm.at[s], onsite_ref.at[s]) for s in (2, 0)})
    left_copy = fetch(left_hbm, left_ref)
    eye = lax.broadcasted_iota(jnp.int32, (W, W), 0) == lax.broadcasted_iota(jnp.int32, (W, W), 1)
    broaden = jnp.where(eye, energy_ref[1], 0.0)

    def diagonal(s):
        onsite_copy[s].wait()
        real = jnp.where(eye, energy - potential_ref[s : s + 1, :], 0.0) - onsite_ref[s]
        return jnp.concatenate([real, broaden], 1)

    potential_copy.wait()
    mat_a[...] = diagonal(1)
    diag_3 = diagonal(3)
    right_copy.wait()
    last = jnp.concatenate([right_ref[0], right_ref[1]], 1)
    mat_b[...] = diag_3 - jnp.where(is_last, last, 0.0)
    inv_1, inv_3 = invert([mat_a, mat_b])
    for copy in coupling_copy:
        copy.wait()
    c0, c1, c2 = coupling_ref[0], coupling_ref[1], coupling_ref[2]
    c3 = jnp.where(is_last, 0.0, coupling_ref[3])
    prop_1r = real_right(inv_1, c1)
    prop_3l = real_right(inv_3, c2.T)
    prop_1l = real_right(inv_1, c0.T)
    prop_3r = real_right(inv_3, c3)
    mat_a[...] = diagonal(2) - mul3(c1.T, prop_1r) - mul3(c2, prop_3l)
    diag_0 = diagonal(0)
    left_copy.wait()
    first = jnp.concatenate([left_ref[0], left_ref[1]], 1)
    top = diag_0 - jnp.where(is_first, first, 0.0) - mul3(c0, prop_1l)
    nxt = mul3(c3.T, prop_3r)
    k02 = mul3(c0, prop_1r)
    k2n = mul3(c2, prop_3r)
    k02_t, k2n_t = ctrans(k02), ctrans(k2n)
    (inv_2,) = invert([mat_a])
    prop_2l = cmul(inv_2, k02_t)
    prop_2r = cmul(inv_2, k2n)
    part_ref[:PACKED] = pack(top - cmul(k02, prop_2l))
    part_ref[PACKED : 2 * PACKED] = pack(nxt + cmul(k2n_t, prop_2r))
    part_ref[2 * PACKED :] = tall(cmul(k02, prop_2r))
    for n, prop in enumerate((prop_1l, prop_1r, prop_2l, prop_2r, prop_3l, prop_3r)):
        prop_ref[n] = prop


def facing(link_l, link_r, to_right):
    plain = jnp.where(to_right, link_r, link_l)
    turned = ctrans(plain)
    return jnp.where(to_right, plain, turned), jnp.where(to_right, turned, plain)


def urgent(inv, link_l, link_r, base, goes_left):
    side, side_t = facing(link_l, link_r, goes_left)
    prop = cmul(inv, side)
    change = cmul(side_t, prop)
    return prop, pack(unpack(base) + jnp.where(goes_left, change, -change))


def others(inv, prop, link_l, link_r, base, goes_left, rest_ref, prop_ref):
    side, side_t = facing(link_l, link_r, jnp.logical_not(goes_left))
    second = cmul(inv, side)
    change = cmul(side_t, second)
    prop_r = jnp.where(goes_left, prop, second)
    rest_ref[:PACKED] = pack(unpack(base) + jnp.where(goes_left, -change, change))
    rest_ref[PACKED:] = tall(cmul(link_l, prop_r))
    prop_ref[0] = jnp.where(goes_left, second, prop)
    prop_ref[1] = prop_r


def chip_sides(side_ref, mine_ref, other_ref):
    goes_left = side_ref[1] == 1
    diag_l = mine_ref[:PACKED]
    next_r = other_ref[PACKED : 2 * PACKED]
    links = wide(mine_ref[2 * PACKED :]), wide(other_ref[2 * PACKED :])
    return links, (diag_l, next_r), goes_left


def chip_kernel(side_ref, mine_ref, other_ref, inv_ref, first_ref, crit_ref, mat):
    mat[...] = unpack(other_ref[:PACKED] - mine_ref[PACKED : 2 * PACKED])
    (inv,) = invert([mat])
    inv_ref[...] = inv
    links, (diag_l, next_r), goes_left = chip_sides(side_ref, mine_ref, other_ref)
    first_ref[...], crit_ref[...] = urgent(inv, *links, jnp.where(goes_left, next_r, diag_l), goes_left)


def chip_rest_kernel(side_ref, inv_ref, first_ref, mine_ref, other_ref, rest_ref, prop_ref):
    links, (diag_l, next_r), goes_left = chip_sides(side_ref, mine_ref, other_ref)
    others(
        inv_ref[...], first_ref[...], *links, jnp.where(goes_left, diag_l, next_r), goes_left,
        rest_ref, prop_ref,
    )


def inverse_kernel(level, side_ref, mine_ref, other_ref, inv_ref, mat):
    mine, other = mine_ref[...], other_ref[...]
    mat[...] = unpack(jnp.where(side_ref[level] == 1, other - mine, mine - other))
    (inv_ref[...],) = invert([mat])


def both_sides(level, side_ref, mine_ref, other_ref):
    on_left = side_ref[level] == 1
    mine, other = mine_ref[...], other_ref[...]
    left, right = jnp.where(on_left, mine, other), jnp.where(on_left, other, mine)
    links = wide(left[PACKED:]), wide(right[PACKED:])
    return links, (left[:PACKED], right[:PACKED]), side_ref[level + 1] == 1


def crit_kernel(level, side_ref, inv_ref, mine_ref, other_ref, first_ref, crit_ref):
    links, (diag_l, next_r), goes_left = both_sides(level, side_ref, mine_ref, other_ref)
    first_ref[...], crit_ref[...] = urgent(
        inv_ref[...], *links, jnp.where(goes_left, next_r, diag_l), goes_left
    )


def rest_kernel(level, side_ref, inv_ref, first_ref, mine_ref, other_ref, rest_ref, prop_ref):
    links, (diag_l, next_r), goes_left = both_sides(level, side_ref, mine_ref, other_ref)
    others(
        inv_ref[...], first_ref[...], *links, jnp.where(goes_left, diag_l, next_r), goes_left,
        rest_ref, prop_ref,
    )


def composed(goes_left, inner, outer):
    near, far = inner
    through = jnp.where(goes_left, far, near)
    return (
        cmul(through, outer[0]) + jnp.where(goes_left, near, 0.0),
        cmul(through, outer[1]) + jnp.where(goes_left, 0.0, far),
    )


def map1_kernel(side_ref, inner_ref, outer_ref, after_ref, out_ref):
    goes = side_ref[1] == 1
    out_ref[0], out_ref[1] = composed(goes, (inner_ref[0], inner_ref[1]), outer_ref)


def map2_kernel(side_ref, mid_ref, inner_ref, outer_ref, out_ref):
    goes = side_ref[2] == 1
    out_ref[0], out_ref[1] = composed(goes, (mid_ref[0], mid_ref[1]), outer_ref)
    out_ref[2], out_ref[3] = composed(goes, (inner_ref[0], inner_ref[1]), outer_ref)


def root_kernel(
    side_ref, inv_ref, mine_ref, other_ref, prop_ref, map_ref, mine_out, partner_out, mat
):
    on_left = side_ref[3] == 1
    lower = jnp.where(on_left, mine_ref[...], other_ref[...])
    diag_l = unpack(lower[:PACKED])
    link_l = wide(lower[PACKED:])
    prop = cmul(inv_ref[...], ctrans(link_l))
    mat[...] = diag_l - cmul(link_l, prop)
    (root,) = invert([mat])
    middle = cmul(prop, root)
    x_left = jnp.where(on_left, root, middle)
    x_right = jnp.where(on_left, middle, 0.0)
    inside_2 = cmul(prop_ref[0], x_left) + cmul(prop_ref[1], x_right)
    inside_1 = cmul(map_ref[0], x_left) + cmul(map_ref[1], x_right)
    inside = cmul(map_ref[2], x_left) + cmul(map_ref[3], x_right)
    for level, middle in ((2, inside_2), (1, inside_1)):
        goes = side_ref[level] == 1
        x_left, x_right = jnp.where(goes, x_left, middle), jnp.where(goes, middle, x_right)
    mine_out[0] = x_left
    mine_out[1] = inside
    partner_out[0] = inside
    partner_out[1] = x_right


def fold_kernel(prop_ref, out_ref):
    to_l, to_r = prop_ref[2], prop_ref[3]
    out_ref[0] = prop_ref[0] + cmul(prop_ref[1], to_l)
    out_ref[1] = cmul(prop_ref[1], to_r)
    out_ref[2] = to_l
    out_ref[3] = to_r
    out_ref[4] = cmul(prop_ref[4], to_l)
    out_ref[5] = prop_ref[5] + cmul(prop_ref[4], to_r)


def density_kernel(side_ref, weight_ref, mine_ref, got_ref, prop_ref, left_ref, density_ref):
    own = side_ref[0] == 1
    x_left = jnp.where(own, mine_ref[0], got_ref[0])
    x_right = jnp.where(own, mine_ref[1], got_ref[1])
    x_2 = cmul(prop_ref[2], x_left) + cmul(prop_ref[3], x_right)
    x_1 = cmul(prop_ref[0], x_left) + cmul(prop_ref[1], x_right)
    x_3 = cmul(prop_ref[4], x_left) + cmul(prop_ref[5], x_right)
    imag = left_ref[1]
    gamma = -(imag + imag.T)
    weight = weight_ref[0]
    stacked = jnp.concatenate([tall(x) for x in (x_left, x_1, x_2, x_3)], 0)
    terms = mul3(stacked, gamma) * stacked
    for s in range(density_ref.shape[1]):
        both = terms[2 * s * W : (2 * s + 1) * W] + terms[(2 * s + 1) * W : (2 * s + 2) * W]
        row = weight * jnp.sum(both.T, axis=0, keepdims=True)
        density_ref[:, s, :] = jnp.broadcast_to(row, (density_ref.shape[0], W))


def moments_kernel(parts_ref, current_ref, past_ref, total_ref, sums_ref):
    total = jnp.sum(parts_ref[...], axis=0)
    total_ref[...] = total
    residual = total - current_ref[...]
    count = past_ref.shape[0]
    diffs = [residual - past_ref[k] for k in range(count)]
    rows = []
    for k in range(count):
        for other in diffs[k:] + [residual]:
            rows.append(jnp.sum(diffs[k] * other, axis=0, keepdims=True))
    rows.append(jnp.zeros((W - len(rows), W), F32))
    sums = jnp.sum(jnp.concatenate(rows, 0).T, axis=0, keepdims=True)
    sums_ref[...] = jnp.broadcast_to(sums, sums_ref.shape)


def mix_kernel(sums_ref, total_ref, current_ref, density_ref, past_ref, next_ref):
    count = past_ref.shape[0]
    sums = jnp.sum(sums_ref[...], axis=0)[0:1]
    gram = {}
    place = 0
    for k in range(count):
        for other in range(k, count + 1):
            entry = jnp.broadcast_to(sums[:, place : place + 1], (1, W))
            gram[k, other] = entry
            if other < count:
                gram[other, k] = entry
            place += 1
    trace = gram[0, 0]
    for k in range(1, count):
        trace = trace + gram[k, k]
    ridge = RIDGE * trace / count
    for k in range(count):
        gram[k, k] = gram[k, k] + ridge
    for k in range(count):
        pivot = 1.0 / gram[k, k]
        for col in range(k + 1, count + 1):
            gram[k, col] = gram[k, col] * pivot
        for row in range(k + 1, count):
            for col in range(k + 1, count + 1):
                gram[row, col] = gram[row, col] - gram[row, k] * gram[k, col]
    mix = [None] * count
    for k in reversed(range(count)):
        value = gram[k, count]
        for col in range(k + 1, count):
            value = value - gram[k, col] * mix[col]
        mix[k] = value
    current = current_ref[...]
    residual = total_ref[...] - current
    out = current + MIX_BETA * residual
    for k in range(count):
        step = (current - density_ref[k]) + MIX_BETA * (residual - past_ref[k])
        out = out - mix[k] * step
    next_ref[...] = out


SMEM = pl.BlockSpec(memory_space=pltpu.SMEM)
VMEM = pl.BlockSpec(memory_space=pltpu.VMEM)
ANY = pl.BlockSpec(memory_space=pltpu.MemorySpace.HBM)
BLOCK = (W, 2 * W)
MAT = pltpu.VMEM(BLOCK, F32)
PACKED = W + 8
CRIT = (PACKED, W)
REST = (PACKED + 2 * W, W)
PART = (2 * PACKED + 2 * W, W)


def call(kernel, name, shapes, in_specs, scratch=(), micros=2):
    return pl.pallas_call(
        kernel,
        out_shape=[jax.ShapeDtypeStruct(s, F32) for s in shapes],
        in_specs=in_specs,
        out_specs=[VMEM] * len(shapes),
        scratch_shapes=list(scratch),
        compiler_params=pltpu.CompilerParams(vmem_limit_bytes=32 << 20),
        name=name,
        cost_estimate=pl.CostEstimate(
            flops=micros * 1000000000, transcendentals=0, bytes_accessed=micros * 3000000
        ),
        interpret=INTERPRET,
    )


GRID = 512
MIX_BETA = 0.3
RIDGE = 0.01


def in_hbm(array):
    return pltpu.with_memory_space_constraint(array, pltpu.MemorySpace.HBM)


def send(block, route):
    return lax.ppermute(block, "slab", route)


def on_device(onsite, coupling, potential, sigma_left, sigma_right, energy_index, density_in, hist_density, hist_residual):
    slab_count = lax.axis_size("slab")
    position = lax.axis_index("slab")
    per_dev = onsite.shape[0]
    energies_all = energy_index.shape[0] * lax.axis_size("energy")
    energy = -0.4 + 0.8 * (energy_index.astype(F32) + 0.5) / GRID
    weight = 4.0 / energies_all / (1.0 + jnp.exp(energy / 0.1))
    broaden = jnp.full((1,), 2.0 / (per_dev * slab_count), F32)
    ends = jnp.stack([position == 0, position == slab_count - 1]).astype(jnp.int32)
    sides = jnp.stack([(position // (1 << level)) % 2 == 0 for level in range(4)]).astype(jnp.int32)
    left, right = sigma_left[0], sigma_right[0]
    pair = (2,) + BLOCK
    part, local = call(
        local_kernel, "local", [PART, (6,) + BLOCK],
        [SMEM, SMEM, ANY, ANY, ANY, ANY, ANY],
        [
            pltpu.VMEM((per_dev, W, W), F32), pltpu.VMEM((per_dev, W, W), F32), pltpu.VMEM((per_dev, W), F32),
            pltpu.VMEM((2, W, W), F32), pltpu.VMEM((2, W, W), F32), MAT, MAT,
            pltpu.SemaphoreType.DMA((11,)),
        ],
    )(ends, jnp.concatenate([energy, broaden]), in_hbm(onsite), in_hbm(coupling), in_hbm(potential), in_hbm(left), in_hbm(right))
    evens = range(0, slab_count, 2)
    other = send(part, [(i + 1, i) for i in evens])
    (local,) = call(fold_kernel, "fold", [(6,) + BLOCK], [VMEM], micros=1)(local)
    other, local = lax.optimization_barrier((other, local))
    inv, first, crit = call(chip_kernel, "chip", [BLOCK, BLOCK, CRIT], [SMEM] + [VMEM] * 2, [MAT])(
        sides, part, other
    )
    route = [(i, i ^ 2) for i in evens]
    crit_other = send(crit, route)
    rest, prop = call(chip_rest_kernel, "chip_rest", [REST, pair], [SMEM] + [VMEM] * 4)(
        sides, inv, first, part, other
    )
    last = slab_count - 2
    props = [prop]
    for level in (1, 2):
        rest_other = send(rest, route)
        (inv,) = call(
            functools.partial(inverse_kernel, level), f"inverse{level}", [BLOCK], [SMEM, VMEM, VMEM], [MAT], 7
        )(sides, crit, crit_other)
        if level == 2:
            (inner,) = call(map1_kernel, "map1", [pair], [SMEM] + [VMEM] * 3, micros=1)(sides, *props, inv)
            rest_other, inner = lax.optimization_barrier((rest_other, inner))
        first, crit = call(
            functools.partial(crit_kernel, level), f"crit{level}", [BLOCK, CRIT], [SMEM] + [VMEM] * 3
        )(sides, inv, rest, rest_other)
        route = [(i, i ^ 6) for i in evens] if level == 1 else [(i, last - i) for i in evens]
        crit_other = send(crit, route)
        rest, prop = call(
            functools.partial(rest_kernel, level), f"rest{level}", [REST, pair], [SMEM] + [VMEM] * 4
        )(sides, inv, first, rest, rest_other)
        props.append(prop)
    rest_other = send(rest, [(i, last - i) for i in evens if i < last - i])
    (maps,) = call(map2_kernel, "map2", [(4,) + BLOCK], [SMEM] + [VMEM] * 3, micros=0)(
        sides, props[1], inner, props[2]
    )
    crit_other, maps = lax.optimization_barrier((crit_other, maps))
    (inv,) = call(
        functools.partial(inverse_kernel, 3), "inverse3", [BLOCK], [SMEM, VMEM, VMEM], [MAT], 7
    )(sides, crit, crit_other)
    mine, partner = call(root_kernel, "root", [pair, pair], [SMEM] + [VMEM] * 5, [MAT])(
        sides, inv, rest, rest_other, props[2], maps
    )
    got = send(partner, [(i, i + 1) for i in evens])
    (density,) = call(density_kernel, "density", [(lax.axis_size("energy"), per_dev, W)], [SMEM, SMEM] + [VMEM] * 4)(
        sides, weight, mine, got, local, left
    )
    density = lax.all_to_all(density, "energy", 0, 0)
    total, sums = call(
        moments_kernel, "moments", [(per_dev, W), (slab_count, 8, W)], [VMEM] * 3
    )(density, density_in, hist_residual)
    sums = lax.all_to_all(sums, "slab", 0, 0)
    (following,) = call(mix_kernel, "mix", [(per_dev, W)], [VMEM] * 5)(
        sums, total, density_in, hist_density, hist_residual
    )
    return (total, following)


def solution(mesh):
    in_specs = (
        P("slab", None, None),
        P("slab", None, None),
        P("slab", None),
        P("energy", None, None, None),
        P("energy", None, None, None),
        P("energy"),
        P("slab", None),
        P(None, "slab", None),
        P(None, "slab", None),
    )
    out_specs = (P("slab", None), P("slab", None))
    return jax.shard_map(
        on_device, mesh=mesh, in_specs=in_specs, out_specs=out_specs, check_vma=False
    )
```
